32 devices in a mesh: dp: 4 (over y, x), mp: 8 (over z, core).
Axes of the slice: x: 2, y: 2, z: 4, core: 2. Of those that a mesh axis runs over, the one named last changes fastest.
Arguments:
- block_arguments: bfloat16 [2, 512, 2048], P(None, 'dp'), may hold values from -6 to 6
- bundled_spans: int32 [2, 4, 8], P(None, 'dp'), may hold values from 0 to 128, as said below
- opening_normalize_scale: float32 [2048], replicated, may hold values from 0.5 to 1.5
- accept_lagmix: float32 [2048], replicated, may hold values from 0 to 1
- lookup_lagmix: float32 [2048], replicated, may hold values from 0 to 1
- payload_lagmix: float32 [2048], replicated, may hold values from 0 to 1
- valve_lagmix: float32 [2048], replicated, may hold values from 0 to 1
- accept_weights: bfloat16 [2048, 2048], P(('dp', 'mp')), may hold values from -0.125 to 0.125
- lookup_weights: bfloat16 [2048, 2048], P(('dp', 'mp')), may hold values from -0.125 to 0.125
- payload_weights: bfloat16 [2048, 2048], P(('dp', 'mp')), may hold values from -0.125 to 0.125
- valve_weights: bfloat16 [2048, 2048], P(('dp', 'mp')), may hold values from -0.125 to 0.125
- fading_speed_logs: float32 [2048], replicated, may hold values from -6 to -1
- present_reward: float32 [2048], replicated, may hold values from -1 to 1
- lane_normalize_scale: float32 [2048], replicated, may hold values from 0.5 to 1.5
- emission_weights: bfloat16 [2048, 2048], P(('dp', 'mp')), may hold values from -0.125 to 0.125
- closing_normalize_scale: float32 [2048], replicated, may hold values from 0.5 to 1.5
- feedforward_lookup_lagmix: float32 [2048], replicated, may hold values from 0 to 1
- feedforward_accept_lagmix: float32 [2048], replicated, may hold values from 0 to 1
- feedforward_lookup_weights: bfloat16 [2048, 7168], P('dp', 'mp'), may hold values from -0.125 to 0.125
- feedforward_payload_weights: bfloat16 [2048, 7168], P('dp', 'mp'), may hold values from -0.0625 to 0.0625
- feedforward_accept_weights: bfloat16 [2048, 2048], P(('dp', 'mp')), may hold values from -0.125 to 0.125
- upstream_sensitivity: bfloat16 [2, 512, 2048], P(None, 'dp'), may hold values from -6 to 6
Outputs:
- outputs: bfloat16 [2, 512, 2048], P(None, 'dp')
- grad_inputs: bfloat16 [2, 512, 2048], P(None, 'dp')
- opening_scale_derivative: float32 [2048], P('dp')
- accept_lagmix_derivative: float32 [2048], P('dp')
- lookup_lagmix_derivative: float32 [2048], P('dp')
- payload_lagmix_derivative: float32 [2048], P('dp')
- valve_lagmix_derivative: float32 [2048], P('dp')
- accept_weights_derivative: float32 [2048, 2048], P(('dp', 'mp'))
- lookup_weights_derivative: float32 [2048, 2048], P(('dp', 'mp'))
- payload_weights_derivative: float32 [2048, 2048], P(('dp', 'mp'))
- valve_weights_derivative: float32 [2048, 2048], P(('dp', 'mp'))
- fading_speed_derivative: float32 [2048], P('dp')
- present_reward_derivative: float32 [2048], P('dp')
- lane_scale_derivative: float32 [2048], P('dp')
- emission_weights_derivative: float32 [2048, 2048], P(('dp', 'mp'))
- closing_scale_derivative: float32 [2048], P('dp')
- feedforward_lookup_lagmix_sens: float32 [2048], P('dp')
- feedforward_accept_lagmix_sens: float32 [2048], P('dp')
- feedforward_lookup_derivative: float32 [2048, 7168], P('dp', 'mp')
- feedforward_payload_derivative: float32 [2048, 7168], P('dp', 'mp')
- feedforward_accept_derivative: float32 [2048, 2048], P(('dp', 'mp'))
The draws below stay inside these ranges and needn't reach their ends.
Inputs may be any that keep to these rules, and one draw needn't show every extreme that they name: `bundled_spans`: zero entries are empty slots. The lengths of one bucket sum to at most 128; its rows past that sum are padding. In every draw some bucket holds a single sequence of 128 tokens.
All inputs are finite; a program needn't handle non-finite values.
Results may differ from the reference program's by a relative error of at most 0.04.
Values may be sent and summed in bfloat16 or wider, within the bound.
A program may use at most 168 MiB of HBM per device.

```python
import jax
import jax.numpy as jnp
from jax import lax

EMBED_WIDTH = 2048
MIXER_LANES = 32
LANE_WIDTH = 64
FF = 7168
SPAN = 64
BUCKET = 128
SUBGROUP_COUNT = 2
SLOTS = 8
BUCKETS = 4
SUBGROUP_LINES = 512


def draw_bundled_spans(key, part):
    bucket_count = SUBGROUP_COUNT * BUCKETS
    streams = jax.random.split(key, 4)
    counts = jax.random.randint(streams[0], (bucket_count,), BUCKET // 2, BUCKET + 1)
    chosen = jax.random.randint(streams[1], (), 0, bucket_count)
    filled = jnp.arange(bucket_count) == chosen
    counts = jnp.where(filled, BUCKET, counts)
    cuts_used = jax.random.randint(streams[2], (bucket_count,), 0, SLOTS)
    cuts_used = jnp.where(filled, 0, cuts_used)
    drawn = jax.random.randint(streams[3], (bucket_count, SLOTS - 1), 0, BUCKET * 64)
    cut_points = 1 + drawn % (counts[:, None] - 1)
    columns = jnp.arange(SLOTS - 1)[None, :]
    cut_points = jnp.where(columns < cuts_used[:, None], cut_points, counts[:, None])
    cut_points = jnp.sort(cut_points, axis=1)
    bounds = jnp.concatenate([jnp.zeros((bucket_count, 1), jnp.int32), cut_points.astype(jnp.int32), counts[:, None].astype(jnp.int32)], axis=1)
    lengths = (bounds[:, 1:] - bounds[:, :-1]).astype(jnp.int32)
    return lengths.reshape(SUBGROUP_COUNT, BUCKETS, SLOTS)


def level_of(key, dims, shards, low, largest):
    level, own = 1.0, jax.random.fold_in(key, 6)
    for dim, parts in shards:
        draws = jnp.exp(jax.random.uniform(jax.random.fold_in(own, dim), (parts,), jnp.float32, low / len(shards), largest / len(shards)))
        level = level * jnp.repeat(draws, dims[dim] // parts).reshape([-1 if axis == dim else 1 for axis in range(len(dims))])
    return level


def noise(key, dims, scale, most, cuts=(), held_as=jnp.bfloat16):
    level = level_of(key, dims, cuts, -0.22, 0.18) if cuts else 1.0
    values = jax.random.normal(key, dims, jnp.float32) * scale * level
    return jnp.minimum(jnp.maximum(values, -most), most).astype(held_as)


def setup_inputs(seed: int = 0) -> dict:
    streams_of = jax.random.split(jax.random.key(seed), 23)
    block_arguments = noise(streams_of[0], (SUBGROUP_COUNT, SUBGROUP_LINES, EMBED_WIDTH), 1.0, 6.0, ((1, 4),))
    bundled_spans = draw_bundled_spans(jax.random.fold_in(streams_of[22], 71), 0)
    opening_normalize_scale = jnp.clip(1.0 + 0.1 * jax.random.normal(streams_of[2], (EMBED_WIDTH,), jnp.float32), 0.5, 1.5)
    accept_lagmix = jnp.clip(jax.random.uniform(streams_of[3], (EMBED_WIDTH,), jnp.float32, 0.0, 1.0), 0.0, 1.0)
    lookup_lagmix = jnp.clip(jax.random.uniform(streams_of[4], (EMBED_WIDTH,), jnp.float32, 0.0, 1.0), 0.0, 1.0)
    payload_lagmix = jnp.clip(jax.random.uniform(streams_of[5], (EMBED_WIDTH,), jnp.float32, 0.0, 1.0), 0.0, 1.0)
    valve_lagmix = jnp.clip(jax.random.uniform(streams_of[6], (EMBED_WIDTH,), jnp.float32, 0.0, 1.0), 0.0, 1.0)
    accept_weights = noise(streams_of[7], (EMBED_WIDTH, EMBED_WIDTH), EMBED_WIDTH ** -0.5, 0.125, ((0, 32),))
    lookup_weights = noise(streams_of[8], (EMBED_WIDTH, EMBED_WIDTH), EMBED_WIDTH ** -0.5, 0.125, ((0, 32),))
    payload_weights = noise(streams_of[9], (EMBED_WIDTH, EMBED_WIDTH), EMBED_WIDTH ** -0.5, 0.125, ((0, 32),))
    valve_weights = noise(streams_of[10], (EMBED_WIDTH, EMBED_WIDTH), EMBED_WIDTH ** -0.5, 0.125, ((0, 32),))
    fading_speed_logs = jnp.clip(jax.random.uniform(streams_of[11], (EMBED_WIDTH,), jnp.float32, -6.0, -1.0), -6.0, -1.0)
    present_reward = jnp.clip(jax.random.uniform(streams_of[12], (EMBED_WIDTH,), jnp.float32, -1.0, 1.0), -1.0, 1.0)
    lane_normalize_scale = jnp.clip(1.0 + 0.1 * jax.random.normal(streams_of[13], (EMBED_WIDTH,), jnp.float32), 0.5, 1.5)
    emission_weights = noise(streams_of[14], (EMBED_WIDTH, EMBED_WIDTH), EMBED_WIDTH ** -0.5, 0.125, ((0, 32),))
    closing_normalize_scale = jnp.clip(1.0 + 0.1 * jax.random.normal(streams_of[15], (EMBED_WIDTH,), jnp.float32), 0.5, 1.5)
    feedforward_lookup_lagmix = jnp.clip(jax.random.uniform(streams_of[16], (EMBED_WIDTH,), jnp.float32, 0.0, 1.0), 0.0, 1.0)
    feedforward_accept_lagmix = jnp.clip(jax.random.uniform(streams_of[17], (EMBED_WIDTH,), jnp.float32, 0.0, 1.0), 0.0, 1.0)
    feedforward_lookup_weights = noise(streams_of[18], (EMBED_WIDTH, FF), EMBED_WIDTH ** -0.5, 0.125, ((0, 4), (1, 8)))
    feedforward_payload_weights = noise(streams_of[19], (EMBED_WIDTH, FF), FF ** -0.5, 0.0625, ((0, 4), (1, 8)))
    feedforward_accept_weights = noise(streams_of[20], (EMBED_WIDTH, EMBED_WIDTH), EMBED_WIDTH ** -0.5, 0.125, ((0, 32),))
    upstream_sensitivity = noise(streams_of[21], (SUBGROUP_COUNT, SUBGROUP_LINES, EMBED_WIDTH), 1.0, 6.0, ((1, 4),))
    return {"block_arguments": block_arguments, "bundled_spans": bundled_spans, "opening_normalize_scale": opening_normalize_scale, "accept_lagmix": accept_lagmix, "lookup_lagmix": lookup_lagmix, "payload_lagmix": payload_lagmix, "valve_lagmix": valve_lagmix, "accept_weights": accept_weights, "lookup_weights": lookup_weights, "payload_weights": payload_weights, "valve_weights": valve_weights, "fading_speed_logs": fading_speed_logs, "present_reward": present_reward, "lane_normalize_scale": lane_normalize_scale, "emission_weights": emission_weights, "closing_normalize_scale": closing_normalize_scale, "feedforward_lookup_lagmix": feedforward_lookup_lagmix, "feedforward_accept_lagmix": feedforward_accept_lagmix, "feedforward_lookup_weights": feedforward_lookup_weights, "feedforward_payload_weights": feedforward_payload_weights, "feedforward_accept_weights": feedforward_accept_weights, "upstream_sensitivity": upstream_sensitivity}


@jax.custom_vjp
def low(v):
    return lax.optimization_barrier(v.astype(jnp.bfloat16)).astype(jnp.float32)

@jax.custom_vjp
def low_back(v):
    return v

def low_keep(v):
    return (low(v), None)

def low_pass(kept, grad):
    return (grad,)

def back_keep(v):
    return (v, None)

def back_low(kept, grad):
    return (low(grad),)
low.defvjp(low_keep, low_pass)
low_back.defvjp(back_keep, back_low)
EPSILON = 1e-05
GROUP_EPSILON = 0.25
EXACT_MATH_MODE = lax.Precision.HIGHEST

def matmul(first_operand, second_operand):
    return jnp.dot(first_operand, second_operand, precision=EXACT_MATH_MODE, preferred_element_type=jnp.float32)

def layer_norm(values, gain_entries):
    average = lax.optimization_barrier(jnp.mean(values, axis=-1, keepdims=True))
    centered = values - average
    spread = lax.optimization_barrier(jnp.mean(centered * centered, axis=-1, keepdims=True))
    return centered * lax.rsqrt(spread + EPSILON) * gain_entries

def group_norm(values):
    grouped = values.reshape(values.shape[0], MIXER_LANES, LANE_WIDTH)
    average = lax.optimization_barrier(jnp.mean(grouped, axis=-1, keepdims=True))
    centered = grouped - average
    spread = lax.optimization_barrier(jnp.mean(centered * centered, axis=-1, keepdims=True))
    return (centered * lax.rsqrt(spread + GROUP_EPSILON)).reshape(values.shape)

def segment_info(lengths, row_count):
    segment_ends = jnp.cumsum(lengths).astype(jnp.int32)
    places = jnp.arange(row_count, dtype=jnp.int32)
    sequence_label = lax.optimization_barrier(jnp.sum((places[:, None] >= segment_ends[None, :]).astype(jnp.int32), axis=1)).astype(jnp.int32)
    earlier = jnp.concatenate([jnp.full((1,), -1, jnp.int32), sequence_label[:-1]])
    common_series_filter = (sequence_label == earlier).astype(jnp.float32)
    valid_rows = (places < segment_ends[-1]).astype(jnp.float32)
    return (sequence_label, common_series_filter, valid_rows)

def shift_rows(values, common_series_filter):
    before = jnp.concatenate([jnp.zeros_like(values[:1]), values[:-1]], axis=0)
    return before * common_series_filter[:, None]

def iterative_renewal(accept_lines, lookup_weight_lines, payload_weight_lines, fading_multiplier, reward_scaler, common_series_filter):
    block_count = accept_lines.shape[0] // SPAN

    def row_step(carry_state, row_pieces):
        accept_array, lookup_array, payload_array, keep_flag = row_pieces
        earlier_memory = carry_state * keep_flag
        reward_term = lax.optimization_barrier(jnp.sum(accept_array * reward_scaler * lookup_array, axis=-1))
        merged_lanes = jnp.einsum('kd,kdv->kv', accept_array, earlier_memory, precision=EXACT_MATH_MODE) + reward_term[:, None] * payload_array
        next_state = fading_multiplier[:, :, None] * earlier_memory + lookup_array[:, :, None] * payload_array[:, None, :]
        return (next_state, merged_lanes)

    def block_step(carry_state, block_pieces):
        return lax.scan(row_step, carry_state, block_pieces)
    block_pieces = (accept_lines.reshape(block_count, SPAN, MIXER_LANES, LANE_WIDTH), lookup_weight_lines.reshape(block_count, SPAN, MIXER_LANES, LANE_WIDTH), payload_weight_lines.reshape(block_count, SPAN, MIXER_LANES, LANE_WIDTH), common_series_filter.reshape(block_count, SPAN))
    initial = jnp.zeros((MIXER_LANES, LANE_WIDTH, LANE_WIDTH), jnp.float32)
    unused, gathered_answers = lax.scan(jax.checkpoint(block_step), initial, block_pieces)
    return gathered_answers.reshape(accept_lines.shape)

def bucket_forward(weight_collection, bucket_rows, lengths):
    opening_normalize_scale, accept_lagmix, lookup_lagmix, payload_lagmix, valve_lagmix, accept_weights, lookup_weights, payload_weights, valve_weights, fading_speed_logs, present_reward, lane_normalize_scale, emission_weights, closing_normalize_scale, feedforward_lookup_lagmix, feedforward_accept_lagmix, feedforward_lookup_weights, feedforward_payload_weights, feedforward_accept_weights = weight_collection
    sequence_label, common_series_filter, valid_rows = segment_info(lengths, BUCKET)
    normed = layer_norm(bucket_rows, opening_normalize_scale)
    before = shift_rows(normed, common_series_filter)
    recept_in = low(normed * accept_lagmix + before * (1.0 - accept_lagmix))
    key_in = low(normed * lookup_lagmix + before * (1.0 - lookup_lagmix))
    value_in = low(normed * payload_lagmix + before * (1.0 - payload_lagmix))
    gate_in = low(normed * valve_lagmix + before * (1.0 - valve_lagmix))
    accept_lines = low(low_back(matmul(recept_in, accept_weights)))
    lookup_weight_lines = low(low_back(matmul(key_in, lookup_weights)))
    payload_weight_lines = low(low_back(matmul(value_in, payload_weights)))
    gate_raw = low_back(matmul(gate_in, valve_weights))
    fading_multiplier = jnp.exp(-jnp.exp(fading_speed_logs)).reshape(MIXER_LANES, LANE_WIDTH)
    reward_scaler = present_reward.reshape(MIXER_LANES, LANE_WIDTH)
    reformed_array = (BUCKET, MIXER_LANES, LANE_WIDTH)
    lane_answers = iterative_renewal(accept_lines.reshape(reformed_array), lookup_weight_lines.reshape(reformed_array), payload_weight_lines.reshape(reformed_array), fading_multiplier, reward_scaler, common_series_filter)
    merged_lanes = low(group_norm(lane_answers.reshape(BUCKET, EMBED_WIDTH)) * lane_normalize_scale * jax.nn.silu(gate_raw))
    middle = bucket_rows + low_back(matmul(merged_lanes, emission_weights))
    second_normed = layer_norm(middle, closing_normalize_scale)
    second_before = shift_rows(second_normed, common_series_filter)
    channel_key_in = low(second_normed * feedforward_lookup_lagmix + second_before * (1.0 - feedforward_lookup_lagmix))
    channel_recept_in = low(second_normed * feedforward_accept_lagmix + second_before * (1.0 - feedforward_accept_lagmix))
    hidden_input = low_back(matmul(channel_key_in, feedforward_lookup_weights))
    hidden = low(jnp.square(jnp.maximum(hidden_input, 0.0)))
    carried = low_back(matmul(hidden, feedforward_payload_weights.T))
    channel_gate = jax.nn.sigmoid(low_back(matmul(channel_recept_in, feedforward_accept_weights)))
    return (middle + channel_gate * carried) * valid_rows[:, None]

def reference(block_arguments, bundled_spans, opening_normalize_scale, accept_lagmix, lookup_lagmix, payload_lagmix, valve_lagmix, accept_weights, lookup_weights, payload_weights, valve_weights, fading_speed_logs, present_reward, lane_normalize_scale, emission_weights, closing_normalize_scale, feedforward_lookup_lagmix, feedforward_accept_lagmix, feedforward_lookup_weights, feedforward_payload_weights, feedforward_accept_weights, upstream_sensitivity):
    weight_collection = tuple((slice_amount.astype(jnp.float32) for slice_amount in (opening_normalize_scale, accept_lagmix, lookup_lagmix, payload_lagmix, valve_lagmix, accept_weights, lookup_weights, payload_weights, valve_weights, fading_speed_logs, present_reward, lane_normalize_scale, emission_weights, closing_normalize_scale, feedforward_lookup_lagmix, feedforward_accept_lagmix, feedforward_lookup_weights, feedforward_payload_weights, feedforward_accept_weights)))
    bucket_total = SUBGROUP_COUNT * BUCKETS
    rows_all = block_arguments.astype(jnp.float32).reshape(bucket_total, BUCKET, EMBED_WIDTH)
    lengths_all = bundled_spans.reshape(bucket_total, SLOTS).astype(jnp.int32)
    checked = jax.checkpoint(bucket_forward)

    def forward(rows_value, weight_values):

        def step(carry_value, pieces):
            return (carry_value, checked(weight_values, pieces[0], pieces[1]))
        unused, gathered_answers = lax.scan(step, jnp.zeros((), jnp.float32), (rows_value, lengths_all))
        return gathered_answers
    gathered_answers, pullback = jax.vjp(forward, rows_all, weight_collection)
    line_derivatives, weight_derivatives = pullback(upstream_sensitivity.astype(jnp.float32).reshape(bucket_total, BUCKET, EMBED_WIDTH))
    opening_scale_derivative, accept_lagmix_derivative, lookup_lagmix_derivative, payload_lagmix_derivative, valve_lagmix_derivative, accept_weights_derivative, lookup_weights_derivative, payload_weights_derivative, valve_weights_derivative, fading_speed_derivative, present_reward_derivative, lane_scale_derivative, emission_weights_derivative, closing_scale_derivative, feedforward_lookup_lagmix_sens, feedforward_accept_lagmix_sens, feedforward_lookup_derivative, feedforward_payload_derivative, feedforward_accept_derivative = weight_derivatives
    return (gathered_answers.reshape(SUBGROUP_COUNT, SUBGROUP_LINES, EMBED_WIDTH).astype(jnp.bfloat16), line_derivatives.reshape(SUBGROUP_COUNT, SUBGROUP_LINES, EMBED_WIDTH).astype(jnp.bfloat16), opening_scale_derivative, accept_lagmix_derivative, lookup_lagmix_derivative, payload_lagmix_derivative, valve_lagmix_derivative, accept_weights_derivative, lookup_weights_derivative, payload_weights_derivative, valve_weights_derivative, fading_speed_derivative, present_reward_derivative, lane_scale_derivative, emission_weights_derivative, closing_scale_derivative, feedforward_lookup_lagmix_sens, feedforward_accept_lagmix_sens, feedforward_lookup_derivative, feedforward_payload_derivative, feedforward_accept_derivative)
```

```python
import functools
from functools import reduce

import jax
import jax.numpy as jnp
from jax import lax
from jax.experimental import pallas as pl
from jax.experimental.pallas import tpu as pltpu
from jax.sharding import PartitionSpec as P

LANE_WIDTH = 64
SPAN = 64


EPSILON = 1e-05
GROUP_EPSILON = 0.25
MIXED_MODE = lax.Precision.HIGH


def shortened(x):
    return jax.tree.map(lambda a: a.astype(jnp.bfloat16) if a.dtype == jnp.float32 else a, x)


def product(first_operand, second_operand):
    return jnp.dot(first_operand, second_operand, preferred_element_type=jnp.float32)


def product_rows(first_operand, second_operand):
    return lax.dot_general(
        first_operand, second_operand, (((0,), (0,)), ((), ())), preferred_element_type=jnp.float32
    )


def product_back(first_operand, second_operand):
    return lax.dot_general(
        first_operand, second_operand, (((1,), (1,)), ((), ())), preferred_element_type=jnp.float32
    )


def layer_norm(values, gain_entries):
    average = jnp.mean(values, axis=-1, keepdims=True)
    centered = values - average
    spread = jnp.mean(centered * centered, axis=-1, keepdims=True)
    return centered * lax.rsqrt(spread + EPSILON) * gain_entries


def group_norm(values, head_count):
    grouped = values.reshape(values.shape[0], head_count, -1)
    average = jnp.mean(grouped, axis=-1, keepdims=True)
    centered = grouped - average
    spread = jnp.mean(centered * centered, axis=-1, keepdims=True)
    return (centered * lax.rsqrt(spread + GROUP_EPSILON)).reshape(values.shape)


def segment_info(lengths, row_count):
    segment_ends = jnp.cumsum(lengths)
    places = jnp.arange(row_count, dtype=jnp.int32)
    sequence_label = jnp.sum((places[:, None] >= segment_ends[None, :]).astype(jnp.int32), axis=1)
    earlier = jnp.concatenate([jnp.full((1,), -1, jnp.int32), sequence_label[:-1]])
    common_series_filter = (sequence_label == earlier).astype(jnp.float32)
    valid_rows = (places < segment_ends[-1]).astype(jnp.float32)
    return (sequence_label, common_series_filter, valid_rows)


def shift_rows(values, common_series_filter):
    before = jnp.concatenate([jnp.zeros_like(values[:1]), values[:-1]], axis=0)
    return before * common_series_filter[:, None]


def iterative_renewal(
    accept_lines,
    lookup_weight_lines,
    payload_weight_lines,
    decay_logarithm,
    reward_scaler,
    sequence_label,
    layer_rows,
):
    row_count, head_count, head_width = accept_lines.shape
    block_count = row_count // layer_rows
    blocked = (block_count, layer_rows, head_count, head_width)
    accept_blocks = accept_lines.reshape(blocked)
    lookup_blocks = lookup_weight_lines.reshape(blocked)
    payload_blocks = payload_weight_lines.reshape(blocked)
    segment_blocks = sequence_label.reshape(block_count, layer_rows)
    positions = jnp.arange(layer_rows, dtype=jnp.float32)
    middle_step = float(layer_rows // 2)
    query_scale = jnp.exp(decay_logarithm[None] * (positions - middle_step)[:, None, None])
    key_scale = jnp.exp(decay_logarithm[None] * (middle_step - 1.0 - positions)[:, None, None])
    scores = jnp.einsum(
        "cthi,cshi->chts",
        accept_blocks * query_scale,
        lookup_blocks * key_scale,
        precision=MIXED_MODE,
    )
    causal = positions[:, None] > positions[None, :]
    within = segment_blocks[:, :, None] == segment_blocks[:, None, :]
    allowed = jnp.logical_and(causal[None], within).astype(jnp.float32)
    scores = scores * allowed[:, None]
    nested_routine = jnp.einsum("chts,cshj->cthj", scores, payload_blocks, precision=MIXED_MODE)
    reward_term = jnp.sum(accept_blocks * reward_scaler * lookup_blocks, axis=-1)
    nested_routine = nested_routine + reward_term[..., None] * payload_blocks
    last_segment = segment_blocks[:, -1]
    prior_segment = jnp.concatenate([jnp.full((1,), -1, jnp.int32), last_segment[:-1]])
    tail_scale = jnp.exp(decay_logarithm[None] * (layer_rows - 1.0 - positions)[:, None, None])
    tail_keep = (segment_blocks == last_segment[:, None]).astype(jnp.float32)
    added_state = jnp.einsum(
        "cshi,cshj->chij",
        lookup_blocks * tail_scale * tail_keep[:, :, None, None],
        payload_blocks,
        precision=MIXED_MODE,
    )
    carry_keep = (last_segment == prior_segment).astype(jnp.float32)
    whole_decay = jnp.exp(decay_logarithm * layer_rows)

    def advance(carry_state, piece_pair):
        addition, keep_flag = piece_pair
        return (whole_decay[:, :, None] * carry_state * keep_flag + addition, carry_state)

    initial = jnp.zeros((head_count, head_width, head_width), jnp.float32)
    unused, starts = lax.scan(advance, initial, (added_state, carry_keep))
    entry_keep = (segment_blocks == prior_segment[:, None]).astype(jnp.float32)
    entry_scale = jnp.exp(decay_logarithm[None] * positions[:, None, None])
    outside = jnp.einsum(
        "cthi,chij->cthj",
        accept_blocks * entry_scale * entry_keep[:, :, None, None],
        starts,
        precision=MIXED_MODE,
    )
    return (nested_routine + outside).reshape(row_count, head_count, head_width)


def add_terms(first_terms, second_terms):
    return jax.tree.map(jnp.add, first_terms, second_terms)


def general_body(
    block_arguments,
    bundled_spans,
    opening_normalize_scale,
    accept_lagmix,
    lookup_lagmix,
    payload_lagmix,
    valve_lagmix,
    accept_weights,
    lookup_weights,
    payload_weights,
    valve_weights,
    fading_speed_logs,
    present_reward,
    lane_normalize_scale,
    emission_weights,
    closing_normalize_scale,
    feedforward_lookup_lagmix,
    feedforward_accept_lagmix,
    feedforward_lookup_weights,
    feedforward_payload_weights,
    feedforward_accept_weights,
    upstream_sensitivity,
):
    micro_count, row_count, model_width = block_arguments.shape
    layer_rows = SPAN
    data_parts = lax.axis_size("dp")
    model_parts = lax.axis_size("mp")
    shard_rows = accept_weights.shape[0]
    model_place = lax.axis_index("mp")
    partition_lanes = model_width // LANE_WIDTH

    def own_columns(values):
        split_values = values.reshape(row_count, data_parts, model_parts, shard_rows)
        picked = lax.dynamic_index_in_dim(split_values, model_place, axis=2, keepdims=False)
        return picked.reshape(row_count, data_parts * shard_rows)

    outputs_list = []
    input_grads = []
    gradient_terms = []
    for micro_index in range(micro_count):
        projections = (
            lax.all_gather(accept_weights, ("dp", "mp"), axis=0, tiled=True),
            lax.all_gather(lookup_weights, ("dp", "mp"), axis=0, tiled=True),
            lax.all_gather(payload_weights, ("dp", "mp"), axis=0, tiled=True),
            lax.all_gather(valve_weights, ("dp", "mp"), axis=0, tiled=True),
            lax.all_gather(emission_weights, ("dp", "mp"), axis=0, tiled=True),
            lax.all_gather(feedforward_accept_weights, ("dp", "mp"), axis=0, tiled=True),
        )
        hidden_pair = (
            lax.all_gather(feedforward_lookup_weights, "dp", axis=0, tiled=True),
            lax.all_gather(feedforward_payload_weights, "dp", axis=0, tiled=True),
        )
        full_recept, full_key, full_value, full_gate, full_output, full_channel = projections
        hidden_key, hidden_value = hidden_pair
        sequence_label, common_series_filter, valid_rows = segment_info(
            bundled_spans[micro_index, 0], row_count
        )
        rows_float = block_arguments[micro_index].astype(jnp.float32)

        def front_part(rows_value, gain_entries, recept_mix, key_mix, value_mix, gate_mix):
            normed = layer_norm(rows_value, gain_entries)
            before = shift_rows(normed, common_series_filter)
            return tuple(
                (
                    normed * weight_mix + before * (1.0 - weight_mix)
                    for weight_mix in (recept_mix, key_mix, value_mix, gate_mix)
                )
            )

        front_values, front_pull = jax.vjp(
            front_part,
            rows_float,
            opening_normalize_scale,
            accept_lagmix,
            lookup_lagmix,
            payload_lagmix,
            valve_lagmix,
        )
        recept_in, key_in, value_in, gate_in = [
            front_piece.astype(jnp.bfloat16) for front_piece in front_values
        ]
        accept_lines = product(recept_in, full_recept).astype(jnp.bfloat16)
        lookup_weight_lines = product(key_in, full_key).astype(jnp.bfloat16)
        payload_weight_lines = product(value_in, full_value).astype(jnp.bfloat16)
        gate_raw = product(gate_in, full_gate)

        def middle_part(
            receptance_activation,
            key_value_product,
            value_activation,
            gate_activation,
            decay_parameter,
            reward_weight,
            gain_entries,
        ):
            decay_logarithm = -jnp.exp(decay_parameter).reshape(partition_lanes, -1)
            reward_scaler = reward_weight.reshape(partition_lanes, -1)
            reformed_array = (row_count, partition_lanes, model_width // partition_lanes)
            lane_answers = iterative_renewal(
                receptance_activation.reshape(reformed_array),
                key_value_product.reshape(reformed_array),
                value_activation.reshape(reformed_array),
                decay_logarithm,
                reward_scaler,
                sequence_label,
                layer_rows,
            )
            grouped = (
                group_norm(lane_answers.reshape(row_count, model_width), partition_lanes)
                * gain_entries
            )
            return grouped * jax.nn.silu(gate_activation)

        mixed_float, middle_pull = jax.vjp(
            middle_part,
            accept_lines.astype(jnp.float32),
            lookup_weight_lines.astype(jnp.float32),
            payload_weight_lines.astype(jnp.float32),
            gate_raw,
            fading_speed_logs,
            present_reward,
            lane_normalize_scale,
        )
        merged_lanes = mixed_float.astype(jnp.bfloat16)
        middle = rows_float + product(merged_lanes, full_output)

        def back_part(middle_value, gain_entries, key_mix, recept_mix):
            normed = layer_norm(middle_value, gain_entries)
            before = shift_rows(normed, common_series_filter)
            return (
                normed * key_mix + before * (1.0 - key_mix),
                normed * recept_mix + before * (1.0 - recept_mix),
            )

        channel_values, back_pull = jax.vjp(
            back_part,
            middle,
            closing_normalize_scale,
            feedforward_lookup_lagmix,
            feedforward_accept_lagmix,
        )
        channel_key_in = channel_values[0].astype(jnp.bfloat16)
        channel_recept_in = channel_values[1].astype(jnp.bfloat16)
        hidden_input = product(channel_key_in, hidden_key)
        hidden = jnp.square(jnp.maximum(hidden_input, 0.0)).astype(jnp.bfloat16)
        carried = lax.psum(product_back(hidden, hidden_value).astype(jnp.bfloat16), "mp").astype(
            jnp.float32
        )
        channel_gate = jax.nn.sigmoid(product(channel_recept_in, full_channel))
        outputs_list.append(
            ((middle + channel_gate * carried) * valid_rows[:, None]).astype(jnp.bfloat16)
        )
        top_grad = upstream_sensitivity[micro_index].astype(jnp.float32) * valid_rows[:, None]
        carried_grad = (top_grad * channel_gate).astype(jnp.bfloat16)
        gate_input_grad = (top_grad * carried * channel_gate * (1.0 - channel_gate)).astype(
            jnp.bfloat16
        )
        pre_grad = (
            product(carried_grad, hidden_value) * 2.0 * jnp.maximum(hidden_input, 0.0)
        ).astype(jnp.bfloat16)
        channel_key_grad = lax.psum(
            product_back(pre_grad, hidden_key).astype(jnp.bfloat16), "mp"
        ).astype(jnp.float32)
        channel_recept_grad = product_back(gate_input_grad, full_channel)
        middle_back, grad_second, feedforward_lookup_lagmix_sens, feedforward_accept_lagmix_sens = (
            back_pull((channel_key_grad, channel_recept_grad))
        )
        middle_grad = top_grad + middle_back
        branch_grad = middle_grad.astype(jnp.bfloat16)
        mixed_grad = product_back(branch_grad, full_output)
        output_term = product_rows(own_columns(merged_lanes), branch_grad)
        (
            receptance_single_precision,
            key_single_precision,
            value_single_precision,
            gate_single_precision,
            decay_gradient,
            reward_derivative,
            lane_normalize_derivative,
        ) = middle_pull(mixed_grad)
        recept_grad = receptance_single_precision.astype(jnp.bfloat16)
        key_grad = key_single_precision.astype(jnp.bfloat16)
        value_grad = value_single_precision.astype(jnp.bfloat16)
        gate_grad = gate_single_precision.astype(jnp.bfloat16)
        (
            line_derivatives,
            grad_first,
            grad_recept_mix,
            grad_key_mix,
            grad_value_mix,
            grad_gate_mix,
        ) = front_pull(
            (
                product_back(recept_grad, full_recept),
                product_back(key_grad, full_key),
                product_back(value_grad, full_value),
                product_back(gate_grad, full_gate),
            )
        )
        projection_terms = (
            product_rows(own_columns(recept_in), recept_grad),
            product_rows(own_columns(key_in), key_grad),
            product_rows(own_columns(value_in), value_grad),
            product_rows(own_columns(gate_in), gate_grad),
            output_term,
        )
        input_grads.append((middle_grad + line_derivatives).astype(jnp.bfloat16))
        local_terms = (
            grad_first,
            grad_recept_mix,
            grad_key_mix,
            grad_value_mix,
            grad_gate_mix,
            decay_gradient,
            reward_derivative,
            lane_normalize_derivative,
            grad_second,
            feedforward_lookup_lagmix_sens,
            feedforward_accept_lagmix_sens,
            product_rows(channel_key_in, pre_grad),
            product_rows(carried_grad, hidden),
            product_rows(own_columns(channel_recept_in), gate_input_grad),
        ) + projection_terms
        gradient_terms.append(local_terms)
    summed = reduce(add_terms, gradient_terms)
    summed = jax.tree.map(
        lambda part: part.astype(jnp.float32),
        lax.psum_scatter(shortened(summed), "dp", scatter_dimension=0, tiled=True),
    )
    (
        grad_first,
        grad_recept_mix,
        grad_key_mix,
        grad_value_mix,
        grad_gate_mix,
        decay_gradient,
        reward_derivative,
        lane_normalize_derivative,
        grad_second,
        feedforward_lookup_lagmix_sens,
        feedforward_accept_lagmix_sens,
        feedforward_lookup_derivative,
        feedforward_payload_derivative,
        feedforward_accept_derivative,
        grad_recept,
        grad_key,
        grad_value,
        grad_gate,
        grad_output,
    ) = summed
    return (
        jnp.stack(outputs_list),
        jnp.stack(input_grads),
        grad_first,
        grad_recept_mix,
        grad_key_mix,
        grad_value_mix,
        grad_gate_mix,
        grad_recept,
        grad_key,
        grad_value,
        grad_gate,
        decay_gradient,
        reward_derivative,
        lane_normalize_derivative,
        grad_output,
        grad_second,
        feedforward_lookup_lagmix_sens,
        feedforward_accept_lagmix_sens,
        feedforward_lookup_derivative,
        feedforward_payload_derivative,
        feedforward_accept_derivative,
    )


MESH = pl.DeviceIdType.MESH
BF = jnp.bfloat16
F32 = jnp.float32
VMEM_LIMIT = 56 << 20


def vmem_specs(count):
    return [pl.BlockSpec(memory_space=pltpu.VMEM)] * count


def flip(place, other):
    low = lax.rem(lax.rem(place, 2) + lax.rem(other, 2), 2)
    high = lax.rem(lax.div(place, 2) + lax.div(other, 2), 2)
    return 2 * high + low


def column_of(owner, data_place, shifted):
    if not shifted:
        return owner
    return 2 * flip(lax.div(owner, 2), data_place) + lax.rem(owner, 2)


def over_x(a):
    return lax.ppermute(a, "dp", [(i, i ^ 1) for i in range(4)])


def over_y(a):
    return lax.ppermute(a, "dp", [(i, i ^ 2) for i in range(4)])


def greet(barrier, peers):
    for peer in peers:
        pl.semaphore_signal(barrier, inc=1, device_id=peer, device_id_type=MESH)
    pl.semaphore_wait(barrier, len(peers))


def gather_kernel(chips, shifted, a_ref, o_ref, send, recv, local):
    d, m = lax.axis_index("dp"), lax.axis_index("mp")
    z, c = lax.div(m, 2), lax.rem(m, 2)
    mate = (d, 2 * z + 1 - c)
    width = a_ref.shape[1]

    def place(owner):
        return o_ref.at[:, pl.ds(pl.multiple_of(column_of(owner, d, shifted) * width, width), width)]

    chips_away = [lax.rem(z + i, chips) for i in range(1, chips)]
    greet(pltpu.get_barrier_semaphore(), [mate] + [(d, 2 * other + c) for other in chips_away])
    keep = pltpu.make_async_copy(a_ref, place(m), local)
    keep.start()
    copies = []
    for i, other in enumerate(chips_away):
        copies.append(
            pltpu.make_async_remote_copy(
                a_ref, place(m), send.at[i], recv.at[i], device_id=(d, 2 * other + c), device_id_type=MESH
            )
        )
    across = pltpu.make_async_remote_copy(
        a_ref, place(m), send.at[chips - 1], recv.at[chips - 1], device_id=mate, device_id_type=MESH
    )
    for copy in copies:
        copy.start()
    across.start()
    onward = []
    for i in range(chips - 1):
        source = 2 * lax.rem(z - (i + 1) + chips, chips) + c
        copies[i].wait_recv()
        copy = pltpu.make_async_remote_copy(
            place(source),
            place(source),
            send.at[chips + i],
            recv.at[chips + i],
            device_id=mate,
            device_id_type=MESH,
        )
        copy.start()
        onward.append(copy)
    for copy in copies:
        copy.wait_send()
    across.wait()
    for copy in onward:
        copy.wait()
    keep.wait()


def gather_mp(block, shifted, collective_id):
    chips = lax.axis_size("mp") // 2
    rows, width = block.shape
    count = 2 * chips - 1
    return pl.pallas_call(
        functools.partial(gather_kernel, chips, shifted),
        out_shape=jax.ShapeDtypeStruct((rows, width * 2 * chips), block.dtype),
        in_specs=vmem_specs(1),
        out_specs=pl.BlockSpec(memory_space=pltpu.VMEM),
        scratch_shapes=[
            pltpu.SemaphoreType.DMA((count,)),
            pltpu.SemaphoreType.DMA((count,)),
            pltpu.SemaphoreType.DMA,
        ],
        compiler_params=pltpu.CompilerParams(
            collective_id=collective_id, has_side_effects=True, vmem_limit_bytes=VMEM_LIMIT
        ),
        name="gather_mp",
    )(block)


def scatter_kernel(chips, shifted, with_rows, *refs):
    if with_rows:
        p_ref, s_ref, o_ref, so_ref, half, pair, far, small, send, recv = refs
    else:
        p_ref, o_ref, half, pair, far, send, recv = refs
    d, m = lax.axis_index("dp"), lax.axis_index("mp")
    z, c = lax.div(m, 2), lax.rem(m, 2)
    mate = (d, 2 * z + 1 - c)
    width = o_ref.shape[1]
    chips_away = [lax.rem(z + i, chips) for i in range(1, chips)]
    greet(pltpu.get_barrier_semaphore(), [mate] + [(d, 2 * other + c) for other in chips_away])

    def part(owner):
        return p_ref.at[:, pl.ds(pl.multiple_of(column_of(owner, d, shifted) * width, width), width)]

    first = []
    for i, other in enumerate(chips_away + [z]):
        copy = pltpu.make_async_remote_copy(
            part(2 * other + 1 - c), half.at[i], send.at[i], recv.at[i], device_id=mate, device_id_type=MESH
        )
        copy.start()
        first.append(copy)
    far_copies = []
    base = chips
    if with_rows:
        mates_rows = pltpu.make_async_remote_copy(
            s_ref, small.at[0], send.at[base], recv.at[base], device_id=mate, device_id_type=MESH
        )
        mates_rows.start()
        base += 1
    for i, other in enumerate(chips_away):
        first[i].wait_recv()
        pair[i] = (part(2 * other + c)[...].astype(F32) + half[i].astype(F32)).astype(pair.dtype)
        copy = pltpu.make_async_remote_copy(
            pair.at[i],
            far.at[i],
            send.at[base + i],
            recv.at[base + i],
            device_id=(d, 2 * other + c),
            device_id_type=MESH,
        )
        copy.start()
        far_copies.append(copy)
    base += chips - 1
    row_copies = []
    if with_rows:
        mates_rows.wait_recv()
        small[1] = s_ref[...] + small[0]
        for i, other in enumerate(chips_away):
            copy = pltpu.make_async_remote_copy(
                small.at[1],
                small.at[2 + i],
                send.at[base + i],
                recv.at[base + i],
                device_id=(d, 2 * other + c),
                device_id_type=MESH,
            )
            copy.start()
            row_copies.append(copy)
    first[chips - 1].wait_recv()
    o_ref[...] = part(m)[...].astype(F32) + half[chips - 1].astype(F32)
    for i in range(chips - 1):
        far_copies[i].wait_recv()
        o_ref[...] += far[i].astype(F32)
    if with_rows:
        total = small[1]
        for i in range(chips - 1):
            row_copies[i].wait_recv()
            total = total + small[2 + i]
        so_ref[...] = total
        mates_rows.wait_send()
    for copy in first + far_copies + row_copies:
        copy.wait_send()


def scatter_mp(partial_sums, shifted, collective_id, row_sums=None):
    parts = lax.axis_size("mp")
    chips = parts // 2
    rows, columns = partial_sums.shape
    width = columns // parts
    with_rows = row_sums is not None
    out_shape = [jax.ShapeDtypeStruct((rows, width), F32)]
    scratch = [
        pltpu.VMEM((chips, rows, width), partial_sums.dtype),
        pltpu.VMEM((chips - 1, rows, width), partial_sums.dtype),
        pltpu.VMEM((chips - 1, rows, width), partial_sums.dtype),
    ]
    count = 2 * chips - 1
    args = [partial_sums]
    if with_rows:
        args.append(row_sums)
        out_shape.append(jax.ShapeDtypeStruct(row_sums.shape, F32))
        scratch.append(pltpu.VMEM((chips + 1,) + row_sums.shape, F32))
        count += chips
    result = pl.pallas_call(
        functools.partial(scatter_kernel, chips, shifted, with_rows),
        out_shape=out_shape,
        in_specs=vmem_specs(len(args)),
        out_specs=vmem_specs(len(out_shape)),
        scratch_shapes=scratch + [pltpu.SemaphoreType.DMA((count,)), pltpu.SemaphoreType.DMA((count,))],
        compiler_params=pltpu.CompilerParams(
            collective_id=collective_id, has_side_effects=True, vmem_limit_bytes=VMEM_LIMIT
        ),
        name="scatter_mp",
    )(*args)
    return result if with_rows else result[0]


def exchange_kernel(parts, a_ref, o_ref, send, recv, local):
    d, m = lax.axis_index("dp"), lax.axis_index("mp")
    others = [lax.rem(m + i, parts) for i in range(1, parts)]
    greet(pltpu.get_barrier_semaphore(), [(d, other) for other in others])
    keep = pltpu.make_async_copy(a_ref.at[m], o_ref.at[m], local)
    keep.start()
    copies = []
    for i, other in enumerate(others):
        copy = pltpu.make_async_remote_copy(
            a_ref.at[other], o_ref.at[m], send.at[i], recv.at[i], device_id=(d, other), device_id_type=MESH
        )
        copy.start()
        copies.append(copy)
    for copy in copies:
        copy.wait()
    keep.wait()


def exchange_mp(blocks, collective_id):
    parts = blocks.shape[0]
    return pl.pallas_call(
        functools.partial(exchange_kernel, parts),
        out_shape=jax.ShapeDtypeStruct(blocks.shape, blocks.dtype),
        in_specs=vmem_specs(1),
        out_specs=pl.BlockSpec(memory_space=pltpu.VMEM),
        scratch_shapes=[
            pltpu.SemaphoreType.DMA((parts - 1,)),
            pltpu.SemaphoreType.DMA((parts - 1,)),
            pltpu.SemaphoreType.DMA,
        ],
        compiler_params=pltpu.CompilerParams(
            collective_id=collective_id, has_side_effects=True, vmem_limit_bytes=VMEM_LIMIT
        ),
        name="exchange_mp",
    )(blocks)


def local_call(kernel, name, out_shape, args, scratch=(), scalars=0):
    specs = [pl.BlockSpec(memory_space=pltpu.SMEM)] * scalars + vmem_specs(len(args) - scalars)
    return pl.pallas_call(
        kernel,
        out_shape=out_shape,
        in_specs=specs,
        out_specs=vmem_specs(len(out_shape)),
        scratch_shapes=list(scratch),
        compiler_params=pltpu.CompilerParams(vmem_limit_bytes=VMEM_LIMIT),
        name=name,
    )(*args)


def struct(shape, dtype):
    return jax.ShapeDtypeStruct(shape, dtype)


def roll_rows(values, shift):
    return pltpu.roll(values, shift % values.shape[0], 0)


def mix_kernel(mixes, shifted, *refs):
    if shifted:
        order, refs = refs[0], refs[1:]
    x_ref, same_ref, gain_ref, mix_ref = refs[:4]
    outs = refs[4 : 4 + mixes]
    mean_ref, rstd_ref = refs[4 + mixes : 6 + mixes]
    rows, width = x_ref.shape
    block = width // 4
    moved = refs[6 + mixes] if shifted else x_ref
    half = rows // 2

    for r in range(2):
        rs = pl.ds(r * half, half)
        total = jnp.zeros((half, 1), F32)
        for j in range(4):
            if shifted:
                lanes = pl.ds(pl.multiple_of(order[j] * block, block), block)
                moved[rs, j * block : (j + 1) * block] = x_ref[rs, lanes]
            total = total + jnp.sum(
                moved[rs, j * block : (j + 1) * block].astype(F32), axis=1, keepdims=True
            )
        average = total / width
        spread = jnp.zeros((half, 1), F32)
        for j in range(4):
            centered = moved[rs, j * block : (j + 1) * block].astype(F32) - average
            spread = spread + jnp.sum(centered * centered, axis=1, keepdims=True)
        scale = lax.rsqrt(spread / width + EPSILON)
        mean_ref[rs, :] = average
        rstd_ref[rs, :] = scale
        same = same_ref[rs, :]
        for j in range(4):
            cols = slice(j * block, (j + 1) * block)
            normed = (moved[rs, cols].astype(F32) - average) * scale * gain_ref[0:1, cols]
            before = roll_rows(normed, 1) * same
            for i in range(mixes):
                weight = mix_ref[i : i + 1, cols]
                outs[i][rs, cols] = (normed * weight + before * (1.0 - weight)).astype(BF)


def mix_rows(x, same, gain, mixes, order=None):
    rows, width = x.shape
    count = mixes.shape[0]
    out = [struct((rows, width), BF)] * count + [struct((rows, 1), F32)] * 2
    args = [x, same, gain, mixes]
    if order is not None:
        out.append(struct((rows, width), BF))
        args = [order] + args
    return local_call(
        functools.partial(mix_kernel, count, order is not None),
        "mix_rows",
        out,
        args,
        scalars=0 if order is None else 1,
    )


def nt(a, b):
    return lax.dot_general(a, b, (((1,), (1,)), ((), ())), preferred_element_type=F32)


def tn(a, b):
    return lax.dot_general(a, b, (((0,), (0,)), ((), ())), preferred_element_type=F32)


def nn(a, b):
    return lax.dot_general(a, b, (((1,), (0,)), ((), ())), preferred_element_type=F32)


def decay_scales(logs, rows):
    places = lax.broadcasted_iota(jnp.int32, (rows, 1), 0).astype(F32)
    middle = float(rows // 2)
    log_decay = -jnp.exp(logs)
    return jnp.exp(log_decay * (places - middle)), jnp.exp(log_decay * (middle - 1.0 - places)), places - middle


def lane_choice(rows, lanes):
    return lax.broadcasted_iota(jnp.int32, (rows, lanes), 1) < LANE_WIDTH


def head_sums(values, low):
    first = jnp.sum(jnp.where(low, values, 0.0), axis=1, keepdims=True)
    second = jnp.sum(jnp.where(low, 0.0, values), axis=1, keepdims=True)
    return jnp.where(low, first, second)


def time_forward_kernel(
    buckets,
    in0, in1, in2, in3, own, by_x, by_y, far0, far1, label_c, label_r, logs, bonus, gain,
    r_ref, k_ref, v_ref, g_ref, n_ref, rstd_ref, mixed_ref,
):
    block = own.shape[1]
    for w, (in_ref, out_ref) in enumerate(zip((in0, in1, in2, in3), (r_ref, k_ref, v_ref, g_ref))):
        total = nn(in_ref[:, 0:block], own[w])
        total += nn(in_ref[:, block : 2 * block], by_x[w])
        total += nn(in_ref[:, 2 * block : 3 * block], by_y[w])
        total += nn(in_ref[:, 3 * block : 4 * block], far0[w] if w < far0.shape[0] else far1[w - far0.shape[0]])
        out_ref[...] = total.astype(out_ref.dtype)
    rows = r_ref.shape[0] // buckets
    pair = 2 * LANE_WIDTH
    low = lane_choice(rows, pair)
    t = lax.broadcasted_iota(jnp.int32, (rows, rows), 0)
    s = lax.broadcasted_iota(jnp.int32, (rows, rows), 1)
    for p in range(r_ref.shape[1] // pair):
        cols = slice(p * pair, (p + 1) * pair)
        out_scale, in_scale, unused = decay_scales(logs[0:1, cols], rows)
        for b in range(buckets):
            rs = slice(b * rows, (b + 1) * rows)
            allowed = jnp.logical_and(s < t, label_c[rs, :] == label_r[b : b + 1, :])
            r, k = r_ref[rs, cols].astype(F32), k_ref[rs, cols].astype(F32)
            v = v_ref[rs, cols]
            rt, kt = r * out_scale, (k * in_scale).astype(BF)
            now = r * bonus[0:1, cols] * k
            parts = []
            for h in range(2):
                mine = low if h == 0 else jnp.logical_not(low)
                scores = nt(jnp.where(mine, rt, 0.0).astype(BF), kt)
                here = jnp.sum(jnp.where(mine, now, 0.0), axis=1, keepdims=True)
                scores = jnp.where(allowed, scores, jnp.where(s == t, here, 0.0))
                parts.append(nn(scores.astype(BF), v))
            wkv = jnp.where(low, parts[0], parts[1])
            centered = wkv - head_sums(wkv, low) / LANE_WIDTH
            scale = lax.rsqrt(head_sums(centered * centered, low) / LANE_WIDTH + GROUP_EPSILON)
            n = centered * scale
            n_ref[rs, cols] = n
            rstd_ref[rs, cols] = scale
            gate = g_ref[rs, cols]
            mixed_ref[rs, cols] = (n * gain[0:1, cols] * gate * jax.nn.sigmoid(gate)).astype(BF)


def time_backward_kernel(
    buckets,
    mg, r_ref, k_ref, v_ref, g_ref, n_ref, rstd_ref, label_c, label_r, logs, bonus, gain,
    dr_ref, dk_ref, dv_ref, dg_ref, small_ref,
):
    rows = r_ref.shape[0] // buckets
    pair = 2 * LANE_WIDTH
    low = lane_choice(rows, pair)
    t = lax.broadcasted_iota(jnp.int32, (rows, rows), 0)
    s = lax.broadcasted_iota(jnp.int32, (rows, rows), 1)
    small_ref[...] = jnp.zeros_like(small_ref)
    for p in range(r_ref.shape[1] // pair):
        cols = slice(p * pair, (p + 1) * pair)
        out_scale, in_scale, place = decay_scales(logs[0:1, cols], rows)
        u, gn = bonus[0:1, cols], gain[0:1, cols]
        for b in range(buckets):
            rs = slice(b * rows, (b + 1) * rows)
            allowed = jnp.logical_and(s < t, label_c[rs, :] == label_r[b : b + 1, :])
            m, gate, n = mg[rs, cols], g_ref[rs, cols], n_ref[rs, cols]
            sg = jax.nn.sigmoid(gate)
            silu = gate * sg
            dg_ref[rs, cols] = (m * n * gn * sg * (1.0 + gate * (1.0 - sg))).astype(BF)
            lane_d = jnp.sum(m * n * silu, axis=0, keepdims=True)
            q = m * gn * silu
            dout = q - head_sums(q, low) / LANE_WIDTH - n * (head_sums(q * n, low) / LANE_WIDTH)
            dout = dout * rstd_ref[rs, cols]
            r, k = r_ref[rs, cols].astype(F32), k_ref[rs, cols].astype(F32)
            v = v_ref[rs, cols]
            rt, kt = (r * out_scale).astype(BF), (k * in_scale).astype(BF)
            now = r * u * k
            diag = head_sums(dout * v.astype(F32), low)
            drs, dks, dvs = [], [], []
            for h in range(2):
                mine = low if h == 0 else jnp.logical_not(low)
                dmine = jnp.where(mine, dout, 0.0).astype(BF)
                scores = nt(jnp.where(mine, rt, jnp.zeros_like(rt)), kt)
                here = jnp.sum(jnp.where(mine, now, 0.0), axis=1, keepdims=True)
                scores = jnp.where(allowed, scores, jnp.where(s == t, here, 0.0))
                dvs.append(tn(scores.astype(BF), dmine))
                a = jnp.where(allowed, nt(dmine, v), 0.0).astype(BF)
                drs.append(nn(a, kt))
                dks.append(tn(a, rt))
            drt = jnp.where(low, drs[0], drs[1])
            dkt = jnp.where(low, dks[0], dks[1])
            dr_ref[rs, cols] = (drt * out_scale + u * k * diag).astype(BF)
            dk_ref[rs, cols] = (dkt * in_scale + u * r * diag).astype(BF)
            dv_ref[rs, cols] = jnp.where(low, dvs[0], dvs[1]).astype(BF)
            lags = place * rt.astype(F32) * drt - (place + 1.0) * kt.astype(F32) * dkt
            small_ref[0:1, cols] += jnp.sum(lags, axis=0, keepdims=True) * -jnp.exp(logs[0:1, cols])
            small_ref[1:2, cols] += jnp.sum(r * k * diag, axis=0, keepdims=True)
            small_ref[2:3, cols] += lane_d


def channel_forward_kernel(
    key_in, recept_in, wk0, wk1, wk2, wk3, wk4, wa0, wa1, wa2, wa3, top, hid_ref, pos_ref, gate_ref, cg_ref
):
    start = 0
    total = None
    for w in (wk0, wk1, wk2, wk3, wk4):
        size = w.shape[0]
        term = nn(key_in[:, start : start + size], w[...])
        total = term if total is None else total + term
        start += size
    positive = jnp.maximum(total, 0.0)
    hid_ref[...] = (positive * positive).astype(BF)
    pos_ref[...] = positive.astype(BF)
    start = 0
    total = None
    for w in (wa0, wa1, wa2, wa3):
        size = w.shape[0]
        term = nn(recept_in[:, start : start + size], w[...])
        total = term if total is None else total + term
        start += size
    gate = jax.nn.sigmoid(total)
    gate_ref[...] = gate
    cg_ref[...] = (top[...] * gate).astype(BF)


def carried_kernel(hid, w0, w1, w2, w3, w4, out_ref):
    start = 0
    for w in (w0, w1, w2, w3, w4):
        size = w.shape[0]
        out_ref[:, start : start + size] = nt(hid[...], w[...]).astype(BF)
        start += size


def pre_grad_kernel(cg, pos, w0, w1, w2, w3, w4, out_ref):
    start = 0
    total = None
    for w in (w0, w1, w2, w3, w4):
        size = w.shape[0]
        term = nn(cg[:, start : start + size], w[...])
        total = term if total is None else total + term
        start += size
    out_ref[...] = (total * 2.0 * pos[...].astype(F32)).astype(BF)


def back_mix_kernel(count, layout, *refs):
    x_ref, mean_ref, rstd_ref, same_ref, next_ref, gain_ref, mix_ref = refs[:7]
    grads = refs[7 : 7 + count]
    weights = refs[7 + count : -3]
    out_ref, sens_ref, stat_ref = refs[-3:]
    rows = x_ref.shape[0]
    same, following = same_ref[...], next_ref[...]
    mean, rstd = mean_ref[...], rstd_ref[...]
    stat_ref[...] = jnp.zeros_like(stat_ref)
    sens_ref[...] = jnp.zeros_like(sens_ref)
    ones = jnp.ones((8, 256), BF)
    for start in range(0, x_ref.shape[1], 256):
        cols = slice(start, start + 256)
        hat = (x_ref[:, cols].astype(F32) - mean) * rstd
        gain = gain_ref[0:1, cols]
        normed = hat * gain
        change = normed - roll_rows(normed, 1) * same
        now = jnp.zeros((rows, 256), F32)
        later = jnp.zeros((rows, 256), F32)
        for i in range(count):
            which, lead, row = layout(i, start)
            w = weights[which]
            w = w[row : row + 256, :] if lead is None else w[lead, row : row + 256, :]
            g = nt(grads[i][...], w)
            sens_ref[i : i + 1, cols] = jnp.sum(g * change, axis=0, keepdims=True)
            weight = mix_ref[i : i + 1, cols]
            now = now + g * weight
            later = later + g * (1.0 - weight)
        back = now + following * roll_rows(later, -1)
        out_ref[:, cols] = back.astype(BF)
        scaled = back * gain
        stat_ref[0:8, :] += nt(ones, scaled.astype(BF))
        stat_ref[8:16, :] += nt(ones, (scaled * hat).astype(BF))


def weight_grad_kernel(lhs, rhs, send_x, send_y, keep):
    places = ((keep, 0), (keep, 2), (send_x, 0), (keep, 3), (keep, 1), (send_y, 0), (send_x, 1), (send_y, 1))
    piece = lhs.shape[1] // 8
    for i, (ref, slot) in enumerate(places):
        ref[slot] = tn(lhs[:, i * piece : (i + 1) * piece], rhs[...]).astype(BF)


def weight_grad(lhs, rhs):
    piece, columns = lhs.shape[1] // 8, rhs.shape[1]
    return local_call(
        weight_grad_kernel,
        "weight_grad",
        [struct((2, piece, columns), BF), struct((2, piece, columns), BF), struct((4, piece, columns), BF)],
        [lhs, rhs],
    )


def reduce_relay(send_x, send_y, keep):
    got_x, got_y = over_x(send_x), over_y(send_y)
    f = lambda a: a.astype(F32)
    next_y = over_y((f(keep[1]) + f(got_x[1])).astype(BF))
    next_x = over_x((f(keep[3]) + f(got_y[1])).astype(BF))
    upper = f(keep[0]) + f(got_x[0]) + f(next_y)
    lower = f(keep[2]) + f(got_y[0]) + f(next_x)
    return upper, lower


def fast_body(
    block_arguments,
    bundled_spans,
    opening_normalize_scale,
    accept_lagmix,
    lookup_lagmix,
    payload_lagmix,
    valve_lagmix,
    accept_weights,
    lookup_weights,
    payload_weights,
    valve_weights,
    fading_speed_logs,
    present_reward,
    lane_normalize_scale,
    emission_weights,
    closing_normalize_scale,
    feedforward_lookup_lagmix,
    feedforward_accept_lagmix,
    feedforward_lookup_weights,
    feedforward_payload_weights,
    feedforward_accept_weights,
    upstream_sensitivity,
):
    buckets, bucket_rows, width = block_arguments.shape
    rows = buckets * bucket_rows
    parts = lax.axis_size("mp")
    d, m = lax.axis_index("dp"), lax.axis_index("mp")
    own_width = width // parts
    own_heads = own_width // LANE_WIDTH
    block = width // 4
    shard = accept_weights.shape[0]
    order = jnp.stack([flip(jnp.int32(j), d) for j in range(4)]).astype(jnp.int32)

    def features_in_order(vectors):
        split = vectors.reshape(vectors.shape[0], 4, block)
        return jnp.concatenate(
            [lax.dynamic_index_in_dim(split, order[j], axis=1, keepdims=False) for j in range(4)], axis=1
        )

    def own_columns(values):
        return lax.dynamic_slice_in_dim(values, m * own_width, own_width, axis=values.ndim - 1)

    def of_own_heads(vectors):
        split = vectors.reshape(vectors.shape[0], own_heads, parts, LANE_WIDTH)
        return lax.dynamic_index_in_dim(split, m, axis=2, keepdims=False).reshape(vectors.shape[0], own_width)

    wk1, wk2 = over_x(feedforward_lookup_weights), over_y(feedforward_lookup_weights)
    half = block // 2
    wk3, wk4 = over_y(wk1[:half]), over_x(wk2[half:])
    wk = (feedforward_lookup_weights, wk1, wk2, wk3, wk4)

    stacked = jnp.stack([accept_weights, lookup_weights, payload_weights, valve_weights])
    by_head = stacked.reshape(4, shard, own_heads, parts, LANE_WIDTH).transpose(3, 0, 1, 2, 4)
    by_head = by_head.reshape(parts, 4, shard, own_width)
    by_column = feedforward_accept_weights.reshape(shard, parts, own_width).transpose(1, 0, 2)
    blocks = jnp.concatenate([by_head, by_column[:, None]], axis=1)
    got = exchange_mp(blocks, 0)
    own = got.transpose(1, 0, 2, 3).reshape(5, parts * shard, own_width)
    by_x, by_y = over_x(own), over_y(own)
    far0, far1 = over_y(by_x[:2]), over_x(by_y[2:])
    full_output = lax.all_gather(emission_weights, "dp", axis=0, tiled=True)

    wv_own, by_x_held = lax.optimization_barrier((feedforward_payload_weights, by_x))
    by_x = by_x_held
    wv1, wv2 = over_x(wv_own), over_y(wv_own)
    wv3, wv4 = over_y(wv1[:half]), over_x(wv2[half:])
    wv = (wv_own, wv1, wv2, wv3, wv4)

    lengths = bundled_spans.reshape(buckets, -1)
    slots = lengths.shape[1]
    before_slot = (jnp.arange(slots)[:, None] <= jnp.arange(slots)[None, :]).astype(jnp.int32)
    ends = jnp.sum(lengths[:, :, None] * before_slot[None], axis=1)
    places = jnp.arange(bucket_rows, dtype=jnp.int32)
    label = jnp.sum((places[None, :, None] >= ends[:, None, :]).astype(jnp.int32), axis=2)
    past = jnp.sum((places[None, :, None] >= ends[:, None, :] + 1).astype(jnp.int32), axis=2)
    ahead = jnp.sum((places[None, :, None] + 1 >= ends[:, None, :]).astype(jnp.int32), axis=2)
    same = jnp.logical_and(label == past, places[None] > 0).astype(F32).reshape(rows, 1)
    following = jnp.logical_and(label == ahead, places[None] < bucket_rows - 1).astype(F32).reshape(rows, 1)
    valid = (places[None] < ends[:, -1:]).astype(F32).reshape(rows, 1)
    label_column = label.reshape(rows, 1)

    x_rows = block_arguments.reshape(rows, width)
    gains = features_in_order(jnp.stack([opening_normalize_scale, closing_normalize_scale]))
    mixes = features_in_order(
        jnp.stack(
            [
                accept_lagmix,
                lookup_lagmix,
                payload_lagmix,
                valve_lagmix,
                feedforward_lookup_lagmix,
                feedforward_accept_lagmix,
            ]
        )
    )
    head_vectors = of_own_heads(jnp.stack([fading_speed_logs, present_reward, lane_normalize_scale]))
    logs, bonus, lane_gain = head_vectors[0:1], head_vectors[1:2], head_vectors[2:3]
    x_own = own_columns(x_rows).astype(F32)
    top_own = own_columns(upstream_sensitivity.reshape(rows, width)).astype(F32) * valid

    recept_in, key_in, value_in, gate_in, mean1, rstd1, x_moved = mix_rows(
        x_rows, same, gains[0:1], mixes[0:4], order
    )
    wide = struct((rows, own_width), F32)
    narrow = struct((rows, own_width), BF)
    recept, key, value, gate_raw, n, n_scale, mixed = local_call(
        functools.partial(time_forward_kernel, buckets),
        "time_forward",
        [narrow, narrow, narrow, wide, wide, wide, narrow],
        [recept_in, key_in, value_in, gate_in, own, by_x, by_y, far0, far1, label_column, label, logs, bonus, lane_gain],
    )
    mixed_out = product(mixed, full_output).astype(BF)
    middle_own = x_own + scatter_mp(mixed_out, False, 1)
    middle = gather_mp(middle_own.astype(BF), True, 2)
    channel_key_in, channel_recept_in, mean2, rstd2 = mix_rows(middle, same, gains[1:2], mixes[4:6])
    wa = (own[4], by_x[4], by_y[4], far1[2])
    hidden_width = wv_own.shape[1]
    hidden, positive, channel_gate, carried_grad_own = local_call(
        channel_forward_kernel,
        "channel_forward",
        [struct((rows, hidden_width), BF)] * 2 + [wide, narrow],
        [channel_key_in, channel_recept_in, *wk, *wa, top_own],
    )
    carried_grad = gather_mp(carried_grad_own, True, 3)
    ff_value = reduce_relay(*weight_grad(carried_grad, hidden))
    (carried_part,) = local_call(
        carried_kernel, "carried", [struct((rows, width), BF)], [hidden, *wv]
    )
    (pre_grad,) = local_call(
        pre_grad_kernel, "pre_grad", [struct((rows, hidden_width), BF)], [carried_grad, positive, *wv]
    )
    carried = scatter_mp(carried_part, True, 4)
    ff_key = reduce_relay(*weight_grad(channel_key_in, pre_grad))
    outputs_own = ((middle_own + channel_gate * carried) * valid).astype(BF)
    gate_input_grad = (top_own * carried * channel_gate * (1.0 - channel_gate)).astype(BF)

    def channel_layout(i, start):
        if i == 0:
            for which, (first, size) in enumerate(
                ((0, block), (block, block), (2 * block, block), (3 * block, half), (3 * block + half, half))
            ):
                if first <= start < first + size:
                    return which, None, start - first
        return 5 + start // block, None, start % block

    back_part, channel_sens, stats = local_call(
        functools.partial(back_mix_kernel, 2, channel_layout),
        "channel_back",
        [struct((rows, width), BF), struct((8, width), F32), struct((16, rows), F32)],
        [middle, mean2, rstd2, same, following, gains[1:2], mixes[4:6], pre_grad, gate_input_grad, *wk, *wa],
    )
    back_own, stats = scatter_mp(back_part, True, 5, stats)

    def norm_back(back, hat, gain, rstd, sums):
        mean_g = sums[0][:, None] / width
        mean_gh = sums[8][:, None] / width
        return (back * gain - mean_g - hat * mean_gh) * rstd

    hat2 = (middle_own.astype(BF).astype(F32) - mean2) * rstd2
    closing_own = jnp.sum(back_own * hat2, axis=0)
    middle_grad = top_own + norm_back(
        back_own, hat2, own_columns(closing_normalize_scale)[None], rstd2, stats
    )
    branch_own = middle_grad.astype(BF)
    branch = gather_mp(branch_own, False, 6)
    mixed_grad = product_back(branch, full_output)
    grad_output = lax.psum_scatter(
        product_rows(mixed, branch).astype(BF), "dp", scatter_dimension=0, tiled=True
    ).astype(F32)
    recept_grad, key_grad, value_grad, gate_grad, small = local_call(
        functools.partial(time_backward_kernel, buckets),
        "time_backward",
        [narrow, narrow, narrow, narrow, struct((8, own_width), F32)],
        [mixed_grad, recept, key, value, gate_raw, n, n_scale, label_column, label, logs, bonus, lane_gain],
    )

    def time_layout(i, start):
        which = start // block
        if which < 3:
            return which, i, start % block
        return (3, i, start % block) if i < 2 else (4, i - 2, start % block)

    back_part1, time_sens, stats1 = local_call(
        functools.partial(back_mix_kernel, 4, time_layout),
        "time_back",
        [struct((rows, width), BF), struct((8, width), F32), struct((16, rows), F32)],
        [
            x_moved, mean1, rstd1, same, following, gains[0:1], mixes[0:4],
            recept_grad, key_grad, value_grad, gate_grad,
            own, by_x, by_y, far0, far1,
        ],
    )
    pieces = [
        weight_grad(a, b)
        for a, b in (
            (recept_in, recept_grad),
            (key_in, key_grad),
            (value_in, value_grad),
            (gate_in, gate_grad),
            (channel_recept_in, gate_input_grad),
        )
    ]
    send_x, send_y, keep = (jnp.stack([p[i] for p in pieces], axis=1) for i in range(3))
    upper, lower = reduce_relay(send_x, send_y, keep)
    back_own1, stats1 = scatter_mp(back_part1, True, 7, stats1)
    hat1 = (x_own - mean1) * rstd1
    opening_own = jnp.sum(back_own1 * hat1, axis=0)
    rows_grad = norm_back(back_own1, hat1, own_columns(opening_normalize_scale)[None], rstd1, stats1)
    input_own = (middle_grad + rows_grad).astype(BF)
    outputs = gather_mp(outputs_own, False, 8)
    input_grads = gather_mp(input_own, False, 9)

    both = jnp.concatenate([upper, lower], axis=1).astype(BF)
    both = both.reshape(5, parts, shard, own_width).transpose(1, 0, 2, 3)
    back = exchange_mp(both, 10)
    heads_back = back[:, :4].reshape(parts, 4, shard, own_heads, LANE_WIDTH).transpose(1, 2, 3, 0, 4)
    heads_back = heads_back.reshape(4, shard, width).astype(F32)
    columns_back = back[:, 4].transpose(1, 0, 2).reshape(shard, width).astype(F32)

    def from_order(vectors):
        return features_in_order(vectors)

    sens = from_order(jnp.concatenate([time_sens[:4], channel_sens[:2]], axis=0))
    zeros = jnp.zeros((2, width), F32)
    columns = lax.dynamic_update_slice_in_dim(zeros, jnp.stack([opening_own, closing_own]), m * own_width, axis=1)
    head_zeros = jnp.zeros((3, own_heads, parts, LANE_WIDTH), F32)
    head_part = small[:3].reshape(3, own_heads, 1, LANE_WIDTH)
    heads = lax.dynamic_update_slice_in_dim(head_zeros, head_part, m, axis=2).reshape(3, width)
    vectors = lax.psum(jnp.concatenate([sens, columns, heads], axis=0), ("dp", "mp"))
    vectors = lax.dynamic_slice_in_dim(vectors, d * block, block, axis=1)
    shape = (buckets, bucket_rows, width)
    return (
        outputs.reshape(shape),
        input_grads.reshape(shape),
        vectors[6],
        vectors[0],
        vectors[1],
        vectors[2],
        vectors[3],
        heads_back[0],
        heads_back[1],
        heads_back[2],
        heads_back[3],
        vectors[8],
        vectors[9],
        vectors[10],
        grad_output,
        vectors[7],
        vectors[4],
        vectors[5],
        jnp.concatenate(ff_key, axis=0),
        jnp.concatenate(ff_value, axis=0),
        columns_back,
    )


def body(*args):
    data_parts, parts = lax.axis_size("dp"), lax.axis_size("mp")
    width, shard, hidden = args[0].shape[2], args[7].shape[0], args[18].shape[1]
    aligned = (
        data_parts == 4
        and parts % 2 == 0
        and shard == LANE_WIDTH
        and (width // parts) % 256 == 0
        and hidden % 128 == 0
    )
    return fast_body(*args) if aligned else general_body(*args)


def solution(mesh):
    return jax.shard_map(
        body,
        mesh=mesh,
        in_specs=(
            P(None, "dp", None),
            P(None, "dp", None),
            P(),
            P(),
            P(),
            P(),
            P(),
            P(("dp", "mp"), None),
            P(("dp", "mp"), None),
            P(("dp", "mp"), None),
            P(("dp", "mp"), None),
            P(),
            P(),
            P(),
            P(("dp", "mp"), None),
            P(),
            P(),
            P(),
            P("dp", "mp"),
            P("dp", "mp"),
            P(("dp", "mp"), None),
            P(None, "dp", None),
        ),
        out_specs=(
            P(None, "dp", None),
            P(None, "dp", None),
            P("dp"),
            P("dp"),
            P("dp"),
            P("dp"),
            P("dp"),
            P(("dp", "mp"), None),
            P(("dp", "mp"), None),
            P(("dp", "mp"), None),
            P(("dp", "mp"), None),
            P("dp"),
            P("dp"),
            P("dp"),
            P(("dp", "mp"), None),
            P("dp"),
            P("dp"),
            P("dp"),
            P("dp", "mp"),
            P("dp", "mp"),
            P(("dp", "mp"), None),
        ),
        check_vma=False,
    )
```

```python
import functools
from functools import reduce

import jax
import jax.numpy as jnp
from jax import lax
from jax.experimental import pallas as pl
from jax.experimental.pallas import tpu as pltpu
from jax.sharding import PartitionSpec as P

LANE_WIDTH = 64
SPAN = 64


EPSILON = 1e-05
GROUP_EPSILON = 0.25
MIXED_MODE = lax.Precision.HIGH


def shortened(x):
    return jax.tree.map(lambda a: a.astype(jnp.bfloat16) if a.dtype == jnp.float32 else a, x)


def product(first_operand, second_operand):
    return jnp.dot(first_operand, second_operand, preferred_element_type=jnp.float32)


def product_rows(first_operand, second_operand):
    return lax.dot_general(
        first_operand, second_operand, (((0,), (0,)), ((), ())), preferred_element_type=jnp.float32
    )


def product_back(first_operand, second_operand):
    return lax.dot_general(
        first_operand, second_operand, (((1,), (1,)), ((), ())), preferred_element_type=jnp.float32
    )


def layer_norm(values, gain_entries):
    average = jnp.mean(values, axis=-1, keepdims=True)
    centered = values - average
    spread = jnp.mean(centered * centered, axis=-1, keepdims=True)
    return centered * lax.rsqrt(spread + EPSILON) * gain_entries


def group_norm(values, head_count):
    grouped = values.reshape(values.shape[0], head_count, -1)
    average = jnp.mean(grouped, axis=-1, keepdims=True)
    centered = grouped - average
    spread = jnp.mean(centered * centered, axis=-1, keepdims=True)
    return (centered * lax.rsqrt(spread + GROUP_EPSILON)).reshape(values.shape)


def segment_info(lengths, row_count):
    segment_ends = jnp.cumsum(lengths)
    places = jnp.arange(row_count, dtype=jnp.int32)
    sequence_label = jnp.sum((places[:, None] >= segment_ends[None, :]).astype(jnp.int32), axis=1)
    earlier = jnp.concatenate([jnp.full((1,), -1, jnp.int32), sequence_label[:-1]])
    common_series_filter = (sequence_label == earlier).astype(jnp.float32)
    valid_rows = (places < segment_ends[-1]).astype(jnp.float32)
    return (sequence_label, common_series_filter, valid_rows)


def shift_rows(values, common_series_filter):
    before = jnp.concatenate([jnp.zeros_like(values[:1]), values[:-1]], axis=0)
    return before * common_series_filter[:, None]


def iterative_renewal(
    accept_lines,
    lookup_weight_lines,
    payload_weight_lines,
    decay_logarithm,
    reward_scaler,
    sequence_label,
    layer_rows,
):
    row_count, head_count, head_width = accept_lines.shape
    block_count = row_count // layer_rows
    blocked = (block_count, layer_rows, head_count, head_width)
    accept_blocks = accept_lines.reshape(blocked)
    lookup_blocks = lookup_weight_lines.reshape(blocked)
    payload_blocks = payload_weight_lines.reshape(blocked)
    segment_blocks = sequence_label.reshape(block_count, layer_rows)
    positions = jnp.arange(layer_rows, dtype=jnp.float32)
    middle_step = float(layer_rows // 2)
    query_scale = jnp.exp(decay_logarithm[None] * (positions - middle_step)[:, None, None])
    key_scale = jnp.exp(decay_logarithm[None] * (middle_step - 1.0 - positions)[:, None, None])
    scores = jnp.einsum(
        "cthi,cshi->chts",
        accept_blocks * query_scale,
        lookup_blocks * key_scale,
        precision=MIXED_MODE,
    )
    causal = positions[:, None] > positions[None, :]
    within = segment_blocks[:, :, None] == segment_blocks[:, None, :]
    allowed = jnp.logical_and(causal[None], within).astype(jnp.float32)
    scores = scores * allowed[:, None]
    nested_routine = jnp.einsum("chts,cshj->cthj", scores, payload_blocks, precision=MIXED_MODE)
    reward_term = jnp.sum(accept_blocks * reward_scaler * lookup_blocks, axis=-1)
    nested_routine = nested_routine + reward_term[..., None] * payload_blocks
    last_segment = segment_blocks[:, -1]
    prior_segment = jnp.concatenate([jnp.full((1,), -1, jnp.int32), last_segment[:-1]])
    tail_scale = jnp.exp(decay_logarithm[None] * (layer_rows - 1.0 - positions)[:, None, None])
    tail_keep = (segment_blocks == last_segment[:, None]).astype(jnp.float32)
    added_state = jnp.einsum(
        "cshi,cshj->chij",
        lookup_blocks * tail_scale * tail_keep[:, :, None, None],
        payload_blocks,
        precision=MIXED_MODE,
    )
    carry_keep = (last_segment == prior_segment).astype(jnp.float32)
    whole_decay = jnp.exp(decay_logarithm * layer_rows)

    def advance(carry_state, piece_pair):
        addition, keep_flag = piece_pair
        return (whole_decay[:, :, None] * carry_state * keep_flag + addition, carry_state)

    initial = jnp.zeros((head_count, head_width, head_width), jnp.float32)
    unused, starts = lax.scan(advance, initial, (added_state, carry_keep))
    entry_keep = (segment_blocks == prior_segment[:, None]).astype(jnp.float32)
    entry_scale = jnp.exp(decay_logarithm[None] * positions[:, None, None])
    outside = jnp.einsum(
        "cthi,chij->cthj",
        accept_blocks * entry_scale * entry_keep[:, :, None, None],
        starts,
        precision=MIXED_MODE,
    )
    return (nested_routine + outside).reshape(row_count, head_count, head_width)


def add_terms(first_terms, second_terms):
    return jax.tree.map(jnp.add, first_terms, second_terms)


def general_body(
    block_arguments,
    bundled_spans,
    opening_normalize_scale,
    accept_lagmix,
    lookup_lagmix,
    payload_lagmix,
    valve_lagmix,
    accept_weights,
    lookup_weights,
    payload_weights,
    valve_weights,
    fading_speed_logs,
    present_reward,
    lane_normalize_scale,
    emission_weights,
    closing_normalize_scale,
    feedforward_lookup_lagmix,
    feedforward_accept_lagmix,
    feedforward_lookup_weights,
    feedforward_payload_weights,
    feedforward_accept_weights,
    upstream_sensitivity,
):
    micro_count, row_count, model_width = block_arguments.shape
    layer_rows = SPAN
    data_parts = lax.axis_size("dp")
    model_parts = lax.axis_size("mp")
    shard_rows = accept_weights.shape[0]
    model_place = lax.axis_index("mp")
    partition_lanes = model_width // LANE_WIDTH

    def own_columns(values):
        split_values = values.reshape(row_count, data_parts, model_parts, shard_rows)
        picked = lax.dynamic_index_in_dim(split_values, model_place, axis=2, keepdims=False)
        return picked.reshape(row_count, data_parts * shard_rows)

    outputs_list = []
    input_grads = []
    gradient_terms = []
    for micro_index in range(micro_count):
        projections = (
            lax.all_gather(accept_weights, ("dp", "mp"), axis=0, tiled=True),
            lax.all_gather(lookup_weights, ("dp", "mp"), axis=0, tiled=True),
            lax.all_gather(payload_weights, ("dp", "mp"), axis=0, tiled=True),
            lax.all_gather(valve_weights, ("dp", "mp"), axis=0, tiled=True),
            lax.all_gather(emission_weights, ("dp", "mp"), axis=0, tiled=True),
            lax.all_gather(feedforward_accept_weights, ("dp", "mp"), axis=0, tiled=True),
        )
        hidden_pair = (
            lax.all_gather(feedforward_lookup_weights, "dp", axis=0, tiled=True),
            lax.all_gather(feedforward_payload_weights, "dp", axis=0, tiled=True),
        )
        full_recept, full_key, full_value, full_gate, full_output, full_channel = projections
        hidden_key, hidden_value = hidden_pair
        sequence_label, common_series_filter, valid_rows = segment_info(
            bundled_spans[micro_index, 0], row_count
        )
        rows_float = block_arguments[micro_index].astype(jnp.float32)

        def front_part(rows_value, gain_entries, recept_mix, key_mix, value_mix, gate_mix):
            normed = layer_norm(rows_value, gain_entries)
            before = shift_rows(normed, common_series_filter)
            return tuple(
                (
                    normed * weight_mix + before * (1.0 - weight_mix)
                    for weight_mix in (recept_mix, key_mix, value_mix, gate_mix)
                )
            )

        front_values, front_pull = jax.vjp(
            front_part,
            rows_float,
            opening_normalize_scale,
            accept_lagmix,
            lookup_lagmix,
            payload_lagmix,
            valve_lagmix,
        )
        recept_in, key_in, value_in, gate_in = [
            front_piece.astype(jnp.bfloat16) for front_piece in front_values
        ]
        accept_lines = product(recept_in, full_recept).astype(jnp.bfloat16)
        lookup_weight_lines = product(key_in, full_key).astype(jnp.bfloat16)
        payload_weight_lines = product(value_in, full_value).astype(jnp.bfloat16)
        gate_raw = product(gate_in, full_gate)

        def middle_part(
            receptance_activation,
            key_value_product,
            value_activation,
            gate_activation,
            decay_parameter,
            reward_weight,
            gain_entries,
        ):
            decay_logarithm = -jnp.exp(decay_parameter).reshape(partition_lanes, -1)
            reward_scaler = reward_weight.reshape(partition_lanes, -1)
            reformed_array = (row_count, partition_lanes, model_width // partition_lanes)
            lane_answers = iterative_renewal(
                receptance_activation.reshape(reformed_array),
                key_value_product.reshape(reformed_array),
                value_activation.reshape(reformed_array),
                decay_logarithm,
                reward_scaler,
                sequence_label,
                layer_rows,
            )
            grouped = (
                group_norm(lane_answers.reshape(row_count, model_width), partition_lanes)
                * gain_entries
            )
            return grouped * jax.nn.silu(gate_activation)

        mixed_float, middle_pull = jax.vjp(
            middle_part,
            accept_lines.astype(jnp.float32),
            lookup_weight_lines.astype(jnp.float32),
            payload_weight_lines.astype(jnp.float32),
            gate_raw,
            fading_speed_logs,
            present_reward,
            lane_normalize_scale,
        )
        merged_lanes = mixed_float.astype(jnp.bfloat16)
        middle = rows_float + product(merged_lanes, full_output)

        def back_part(middle_value, gain_entries, key_mix, recept_mix):
            normed = layer_norm(middle_value, gain_entries)
            before = shift_rows(normed, common_series_filter)
            return (
                normed * key_mix + before * (1.0 - key_mix),
                normed * recept_mix + before * (1.0 - recept_mix),
            )

        channel_values, back_pull = jax.vjp(
            back_part,
            middle,
            closing_normalize_scale,
            feedforward_lookup_lagmix,
            feedforward_accept_lagmix,
        )
        channel_key_in = channel_values[0].astype(jnp.bfloat16)
        channel_recept_in = channel_values[1].astype(jnp.bfloat16)
        hidden_input = product(channel_key_in, hidden_key)
        hidden = jnp.square(jnp.maximum(hidden_input, 0.0)).astype(jnp.bfloat16)
        carried = lax.psum(product_back(hidden, hidden_value).astype(jnp.bfloat16), "mp").astype(
            jnp.float32
        )
        channel_gate = jax.nn.sigmoid(product(channel_recept_in, full_channel))
        outputs_list.append(
            ((middle + channel_gate * carried) * valid_rows[:, None]).astype(jnp.bfloat16)
        )
        top_grad = upstream_sensitivity[micro_index].astype(jnp.float32) * valid_rows[:, None]
        carried_grad = (top_grad * channel_gate).astype(jnp.bfloat16)
        gate_input_grad = (top_grad * carried * channel_gate * (1.0 - channel_gate)).astype(
            jnp.bfloat16
        )
        pre_grad = (
            product(carried_grad, hidden_value) * 2.0 * jnp.maximum(hidden_input, 0.0)
        ).astype(jnp.bfloat16)
        channel_key_grad = lax.psum(
            product_back(pre_grad, hidden_key).astype(jnp.bfloat16), "mp"
        ).astype(jnp.float32)
        channel_recept_grad = product_back(gate_input_grad, full_channel)
        middle_back, grad_second, feedforward_lookup_lagmix_sens, feedforward_accept_lagmix_sens = (
            back_pull((channel_key_grad, channel_recept_grad))
        )
        middle_grad = top_grad + middle_back
        branch_grad = middle_grad.astype(jnp.bfloat16)
        mixed_grad = product_back(branch_grad, full_output)
        output_term = product_rows(own_columns(merged_lanes), branch_grad)
        (
            receptance_single_precision,
            key_single_precision,
            value_single_precision,
            gate_single_precision,
            decay_gradient,
            reward_derivative,
            lane_normalize_derivative,
        ) = middle_pull(mixed_grad)
        recept_grad = receptance_single_precision.astype(jnp.bfloat16)
        key_grad = key_single_precision.astype(jnp.bfloat16)
        value_grad = value_single_precision.astype(jnp.bfloat16)
        gate_grad = gate_single_precision.astype(jnp.bfloat16)
        (
            line_derivatives,
            grad_first,
            grad_recept_mix,
            grad_key_mix,
            grad_value_mix,
            grad_gate_mix,
        ) = front_pull(
            (
                product_back(recept_grad, full_recept),
                product_back(key_grad, full_key),
                product_back(value_grad, full_value),
                product_back(gate_grad, full_gate),
            )
        )
        projection_terms = (
            product_rows(own_columns(recept_in), recept_grad),
            product_rows(own_columns(key_in), key_grad),
            product_rows(own_columns(value_in), value_grad),
            product_rows(own_columns(gate_in), gate_grad),
            output_term,
        )
        input_grads.append((middle_grad + line_derivatives).astype(jnp.bfloat16))
        local_terms = (
            grad_first,
            grad_recept_mix,
            grad_key_mix,
            grad_value_mix,
            grad_gate_mix,
            decay_gradient,
            reward_derivative,
            lane_normalize_derivative,
            grad_second,
            feedforward_lookup_lagmix_sens,
            feedforward_accept_lagmix_sens,
            product_rows(channel_key_in, pre_grad),
            product_rows(carried_grad, hidden),
            product_rows(own_columns(channel_recept_in), gate_input_grad),
        ) + projection_terms
        gradient_terms.append(local_terms)
    summed = reduce(add_terms, gradient_terms)
    summed = jax.tree.map(
        lambda part: part.astype(jnp.float32),
        lax.psum_scatter(shortened(summed), "dp", scatter_dimension=0, tiled=True),
    )
    (
        grad_first,
        grad_recept_mix,
        grad_key_mix,
        grad_value_mix,
        grad_gate_mix,
        decay_gradient,
        reward_derivative,
        lane_normalize_derivative,
        grad_second,
        feedforward_lookup_lagmix_sens,
        feedforward_accept_lagmix_sens,
        feedforward_lookup_derivative,
        feedforward_payload_derivative,
        feedforward_accept_derivative,
        grad_recept,
        grad_key,
        grad_value,
        grad_gate,
        grad_output,
    ) = summed
    return (
        jnp.stack(outputs_list),
        jnp.stack(input_grads),
        grad_first,
        grad_recept_mix,
        grad_key_mix,
        grad_value_mix,
        grad_gate_mix,
        grad_recept,
        grad_key,
        grad_value,
        grad_gate,
        decay_gradient,
        reward_derivative,
        lane_normalize_derivative,
        grad_output,
        grad_second,
        feedforward_lookup_lagmix_sens,
        feedforward_accept_lagmix_sens,
        feedforward_lookup_derivative,
        feedforward_payload_derivative,
        feedforward_accept_derivative,
    )


MESH = pl.DeviceIdType.MESH
BF = jnp.bfloat16
F32 = jnp.float32
VMEM_LIMIT = 63 << 20
OPENING, CLOSING, FADING, REWARD, LANE = 0, 5, 8, 9, 10


def struct(shape, dtype):
    return jax.ShapeDtypeStruct(shape, dtype)


def flip(place, other):
    low = lax.rem(lax.rem(place, 2) + lax.rem(other, 2), 2)
    high = lax.rem(lax.div(place, 2) + lax.div(other, 2), 2)
    return 2 * high + low


def nt(a, b):
    return lax.dot_general(a, b, (((1,), (1,)), ((), ())), preferred_element_type=F32)


def tn(a, b):
    return lax.dot_general(a, b, (((0,), (0,)), ((), ())), preferred_element_type=F32)


def nn(a, b):
    return lax.dot_general(a, b, (((1,), (0,)), ((), ())), preferred_element_type=F32)


def roll_rows(values, shift):
    return pltpu.roll(values, shift % values.shape[0], 0)


def swap_halves(tile):
    return pltpu.roll(tile, LANE_WIDTH, 1)


def head_sums(values, low):
    first = jnp.sum(jnp.where(low, values, 0.0), axis=1, keepdims=True)
    second = jnp.sum(jnp.where(low, 0.0, values), axis=1, keepdims=True)
    return jnp.where(low, first, second)


class Links:
    def __init__(self, send, recv):
        self.send, self.recv = send, recv
        self.used = 0
        self.open = []

    def push(self, source, target, peer):
        i = self.used
        self.used += 1
        copy = pltpu.make_async_remote_copy(
            source, target, self.send.at[i], self.recv.at[i], device_id=peer, device_id_type=MESH
        )
        copy.start()
        self.open.append(copy)
        return copy

    def group(self, sources, targets, peers, whole):
        i = self.used
        self.used += 1
        for source, target, peer in zip(sources, targets, peers):
            pltpu.make_async_remote_copy(
                source, target, self.send.at[i], self.recv.at[i], device_id=peer, device_id_type=MESH
            ).start()
        copy = pltpu.make_async_remote_copy(
            whole, whole, self.send.at[i], self.recv.at[i], device_id=peers[0], device_id_type=MESH
        )
        self.open.append(copy)
        return copy

    def sent(self, copy):
        if any(other is copy for other in self.open):
            copy.wait_send()
            self.open = [other for other in self.open if other is not copy]

    def finish(self):
        for copy in self.open:
            copy.wait_send()


COPIES = 300


def block_kernel(
    spans, x_ref, up_ref, vec, w_recept, w_key, w_value, w_gate, w_out, w_channel, fk, fv,
    out_full, gin_full, ffk_out, ffv_out, back_out, wo_out, vec_out,
    blocks, g, fkb, fvb, wob, acts, mean1, rstd1, mean2, rstd2, order_vec, head_vec, seen,
    rkv, gate_raw, n_ref, n_scale, mixed, part, half, pair, far, small,
    mid_own, mid_own_b, mid, kin, cri, hid, pos, pre, channel_gate, cg_own, cg,
    out_own, gig, middle_grad, branch_own, branch, mixed_grad, time_grads, sens, head_small,
    ff_send, ff_got, ff_got2, tm_send, tm_got, tm_got2, channel_sum,
    wo_part, wo_got, gin_own, u_got, u2_own, u2_got, u3_own, u3_got,
    send, recv, local,
):
    d, m = lax.axis_index("dp"), lax.axis_index("mp")
    z, c = lax.div(m, 2), lax.rem(m, 2)
    chips, parts = 4, 8
    buckets, rows = 2, x_ref.shape[0] // 2
    width = x_ref.shape[1]
    own = width // parts
    block = width // 4
    shard = w_out.shape[0]
    pairs = own // 128
    links = Links(send, recv)
    mate = (d, 2 * z + 1 - c)
    chips_away = [lax.rem(z + i, chips) for i in range(1, chips)]
    others = [lax.rem(m + i, parts) for i in range(1, parts)]
    x_peer = (d + 1 - 2 * lax.rem(d, 2), m)
    y_peer = (d + 2 - 4 * lax.div(d, 2), m)
    diagonal = (3 - d, m)
    order = [d, x_peer[0], y_peer[0], diagonal[0]]

    def own_lanes(owner):
        return pl.ds(pl.multiple_of(owner * own, own), own)

    def moved_lanes(owner):
        place = 2 * flip(lax.div(owner, 2), d) + lax.rem(owner, 2)
        return pl.ds(pl.multiple_of(place * own, own), own)

    def bucket_rows(b):
        return slice(b * rows, (b + 1) * rows)

    barrier = pltpu.get_barrier_semaphore()
    greeted = [(d, other) for other in others] + [x_peer, y_peer, diagonal]
    for peer in greeted:
        pl.semaphore_signal(barrier, inc=1, device_id=peer, device_id_type=MESH)
    top_copy = pltpu.make_async_copy(up_ref.at[:, own_lanes(m)], seen, local)
    top_copy.start()
    low16 = lax.broadcasted_iota(jnp.int32, (shard, 128), 1) < LANE_WIDTH

    def head_blocks(w, weight):
        for to in range(parts):
            for q in range(pairs):
                tiles = []
                for j in (2 * q, 2 * q + 1):
                    start = j * block + (to // 2) * 128
                    tiles.append(weight[:, start : start + 128].astype(F32))
                if to % 2 == 0:
                    tile = jnp.where(low16, tiles[0], swap_halves(tiles[1]))
                else:
                    tile = jnp.where(low16, swap_halves(tiles[0]), tiles[1])
                blocks[w, to, :, q * 128 : (q + 1) * 128] = tile.astype(BF)

    head_blocks(0, w_recept)
    pl.semaphore_wait(barrier, len(greeted))

    my_rows = pl.ds(pl.multiple_of(m * shard, shard), shard)

    def exchange(w):
        if w < 4:
            sources = [blocks.at[w, other] for other in others]
        else:
            sources = [w_channel.at[:, own_lanes(other)] for other in others]
        return links.group(
            sources,
            [g.at[0, w, my_rows]] * (parts - 1),
            [(d, other) for other in others],
            g.at[0, w, pl.ds(0, (parts - 1) * shard)],
        )

    arrivals = [exchange(0)]
    for w, weight in ((1, w_key), (2, w_value), (3, w_gate)):
        head_blocks(w, weight)
        arrivals.append(exchange(w))
    arrivals.append(exchange(4))
    for w in range(4):
        g[0, w, my_rows] = blocks[w, m]
    g[0, 4, my_rows] = w_channel[:, own_lanes(m)]
    out_rows = pl.ds(pl.multiple_of(d * shard, shard), shard)
    wo_arrivals = [links.push(w_out, wob.at[out_rows], peer) for peer in (x_peer, y_peer, diagonal)]
    wob[out_rows] = w_out[...]

    for j in range(4):
        order_vec[:, j * block : (j + 1) * block] = vec[
            :, pl.ds(pl.multiple_of(order[j] * block, block), block)
        ]
    low_row = lax.broadcasted_iota(jnp.int32, (16, 128), 1) < LANE_WIDTH
    upper = lax.rem(m, 2) == 1

    def head_tile(j):
        start = pl.multiple_of(j * block + lax.div(m, 2) * 128, 128)
        return vec[:, pl.ds(start, 128)]

    for q in range(pairs):
        first, second = head_tile(2 * q), head_tile(2 * q + 1)
        first = jnp.where(upper, swap_halves(first), first)
        second = jnp.where(upper, second, swap_halves(second))
        head_vec[:, q * 128 : (q + 1) * 128] = jnp.where(low_row, first, second)

    def row_masks(b):
        t = lax.broadcasted_iota(jnp.int32, (rows, 1), 0)
        lane = lax.broadcasted_iota(jnp.int32, (1, rows), 1)
        label, past, ahead = (jnp.zeros((rows, 1), jnp.int32) for unused in range(3))
        label_row = jnp.zeros((1, rows), jnp.int32)
        end = jnp.int32(0)
        for j in range(spans.shape[1]):
            end = end + spans[b, j]
            label = label + jnp.where(t >= end, 1, 0)
            past = past + jnp.where(t - 1 >= end, 1, 0)
            ahead = ahead + jnp.where(t + 1 >= end, 1, 0)
            label_row = label_row + jnp.where(lane >= end, 1, 0)
        same = jnp.where(jnp.logical_and(label == past, t > 0), 1.0, 0.0)
        following = jnp.where(jnp.logical_and(label == ahead, t < rows - 1), 1.0, 0.0)
        valid = jnp.where(t < end, 1.0, 0.0)
        return label, label_row, same, following, valid

    masks = [row_masks(b) for b in range(buckets)]

    def mix(b, take, mean, rstd, gain_row, mix_row, outs):
        rs = bucket_rows(b)
        same = masks[b][2]
        total = jnp.zeros((rows, 1), F32)
        for j in range(4):
            total = total + jnp.sum(take(rs, j).astype(F32), axis=1, keepdims=True)
        average = total / width
        spread = jnp.zeros((rows, 1), F32)
        for j in range(4):
            centered = take(rs, j).astype(F32) - average
            spread = spread + jnp.sum(centered * centered, axis=1, keepdims=True)
        scale = lax.rsqrt(spread / width + EPSILON)
        mean[rs, :] = average
        rstd[rs, :] = scale
        for j in range(4):
            cols = slice(j * block, (j + 1) * block)
            normed = (take(rs, j).astype(F32) - average) * scale * order_vec[gain_row : gain_row + 1, cols]
            before = roll_rows(normed, 1) * same
            for i, out in enumerate(outs):
                weight = order_vec[mix_row + i : mix_row + i + 1, cols]
                out[rs, cols] = (normed * weight + before * (1.0 - weight)).astype(BF)

    def take_x(rs, j):
        return x_ref[rs, pl.ds(pl.multiple_of(order[j] * block, block), block)]

    def take_mid(rs, j):
        return mid[rs, j * block : (j + 1) * block]

    def relay_out(source, slot1, slot2):
        return links.push(source, slot1, x_peer), links.push(source, slot2, y_peer)

    for b in range(buckets):
        mix(b, take_x, mean1, rstd1, OPENING, OPENING + 1, [acts.at[w] for w in range(4)])

    half_block = block // 2
    g_first = []
    for w in range(5):
        arrivals[w].wait_recv()
        g_first.append(relay_out(g.at[0, w], g.at[1, w], g.at[2, w]))

    def forward(copies, slot1, slot2, slot3):
        upper_half, lower_half = pl.ds(0, half_block), pl.ds(half_block, half_block)
        copies[0].wait_recv()
        one = links.push(slot1.at[upper_half], slot3.at[upper_half], y_peer)
        copies[1].wait_recv()
        return one, links.push(slot2.at[lower_half], slot3.at[lower_half], x_peer)

    fk_first = relay_out(fk, fkb.at[0], fkb.at[1])
    g_second = [forward(g_first[w], g.at[1, w], g.at[2, w], g.at[3, w]) for w in range(4)]

    for w in range(4):
        for copy in g_second[w]:
            copy.wait_recv()
        for b in range(buckets):
            rs = bucket_rows(b)
            total = nn(acts[w, rs, 0:block], g[0, w])
            for j in range(1, 4):
                total = total + nn(acts[w, rs, j * block : (j + 1) * block], g[j, w])
            if w < 3:
                rkv[w, rs] = total.astype(BF)
            else:
                gate_raw[rs] = total
    g_second.append(forward(g_first[4], g.at[1, 4], g.at[2, 4], g.at[3, 4]))

    low = lax.broadcasted_iota(jnp.int32, (rows, 128), 1) < LANE_WIDTH
    t_square = lax.broadcasted_iota(jnp.int32, (rows, rows), 0)
    s_square = lax.broadcasted_iota(jnp.int32, (rows, rows), 1)
    places = lax.broadcasted_iota(jnp.int32, (rows, 1), 0).astype(F32) - float(rows // 2)

    def decay_scales(cols):
        log_decay = -jnp.exp(head_vec[FADING : FADING + 1, cols])
        return jnp.exp(log_decay * places), jnp.exp(log_decay * (-1.0 - places))

    def allowed_pairs(b):
        return jnp.logical_and(s_square < t_square, masks[b][0] == masks[b][1])

    def scores_of(rt, kt, now, mine, allowed):
        scores = nt(jnp.where(mine, rt, 0.0).astype(BF), kt)
        here = jnp.sum(jnp.where(mine, now, 0.0), axis=1, keepdims=True)
        return jnp.where(allowed, scores, jnp.where(s_square == t_square, here, 0.0)).astype(BF)

    def time_forward(b):
        rs = bucket_rows(b)
        allowed = allowed_pairs(b)
        for p in range(pairs):
            cols = slice(p * 128, (p + 1) * 128)
            out_scale, in_scale = decay_scales(cols)
            r, k = rkv[0, rs, cols].astype(F32), rkv[1, rs, cols].astype(F32)
            v = rkv[2, rs, cols]
            rt, kt = r * out_scale, (k * in_scale).astype(BF)
            now = r * head_vec[REWARD : REWARD + 1, cols] * k
            first = nn(scores_of(rt, kt, now, low, allowed), v)
            second = nn(scores_of(rt, kt, now, jnp.logical_not(low), allowed), v)
            wkv = jnp.where(low, first, second)
            centered = wkv - head_sums(wkv, low) / LANE_WIDTH
            scale = lax.rsqrt(head_sums(centered * centered, low) / LANE_WIDTH + GROUP_EPSILON)
            n = centered * scale
            n_ref[rs, cols] = n
            n_scale[rs, cols] = scale
            gate = gate_raw[rs, cols]
            gained = n * head_vec[LANE : LANE + 1, cols] * gate * jax.nn.sigmoid(gate)
            mixed[rs, cols] = gained.astype(BF)

    pair_copies = {}

    def scatter_start(k, b, source, lanes):
        rs = pl.ds(b * rows, rows)
        return [
            links.push(source.at[rs, lanes(2 * other + 1 - c)], half.at[k, b, i], mate)
            for i, other in enumerate(chips_away + [z])
        ]

    def scatter_middle(k, b, source, lanes, first):
        rs = pl.ds(b * rows, rows)
        copies = []
        for i, other in enumerate(chips_away):
            if (b, i) in pair_copies:
                links.sent(pair_copies[b, i])
            first[i].wait_recv()
            value = source[rs, lanes(2 * other + c)].astype(F32) + half[k, b, i].astype(F32)
            pair[b, i] = value.astype(BF)
            copy = links.push(pair.at[b, i], far.at[k, b, i], (d, 2 * other + c))
            pair_copies[b, i] = copy
            copies.append(copy)
        return copies

    def scatter_end(k, b, source, lanes, first, second):
        rs = pl.ds(b * rows, rows)
        first[chips - 1].wait_recv()
        total = source[rs, lanes(m)].astype(F32) + half[k, b, chips - 1].astype(F32)
        for i, copy in enumerate(second):
            copy.wait_recv()
            total = total + far[k, b, i].astype(F32)
        return total

    def stats_start(k, b):
        return links.push(small.at[k, b, 0], small.at[k, b, 1], mate)

    def stats_middle(k, b, first):
        first.wait_recv()
        small[k, b, 2] = small[k, b, 0] + small[k, b, 1]
        return [
            links.push(small.at[k, b, 2], small.at[k, b, 3 + i], (d, 2 * other + c))
            for i, other in enumerate(chips_away)
        ]

    eye8 = jnp.where(lax.broadcasted_iota(jnp.int32, (16, 128), 0) == 0, 1.0, 0.0)
    eye16 = jnp.where(lax.broadcasted_iota(jnp.int32, (16, 128), 0) == 8, 1.0, 0.0)

    def stats_end(k, b, second):
        total = small[k, b, 2]
        for i, copy in enumerate(second):
            copy.wait_recv()
            total = total + small[k, b, 3 + i]
        total = total / width
        turn = lambda e: lax.dot_general(
            total, e, (((0,), (0,)), ((), ())), precision=lax.Precision.HIGHEST, preferred_element_type=F32
        )[:, 0:1]
        return turn(eye8), turn(eye16)

    def gather_start(source, target, lanes, rs):
        mine = target.at[rs, lanes(m)]
        copies = [links.push(source.at[rs], mine, (d, 2 * other + c)) for other in chips_away]
        copies.append(links.push(source.at[rs], mine, mate))
        target[rs, lanes(m)] = source[rs]
        return copies

    def gather_middle(target, lanes, rs, first):
        copies = []
        for i in range(chips - 1):
            source = 2 * lax.rem(z - (i + 1) + chips, chips) + c
            first[i].wait_recv()
            copies.append(links.push(target.at[rs, lanes(source)], target.at[rs, lanes(source)], mate))
        return copies

    def gather_end(first, second):
        first[-1].wait_recv()
        for copy in second:
            copy.wait_recv()

    both = (0, 1)
    slices = [pl.ds(b * rows, rows) for b in both]
    all_rows = pl.ds(0, buckets * rows)

    for copy in wo_arrivals:
        copy.wait_recv()
    first1 = []
    for b in both:
        time_forward(b)
        rs = bucket_rows(b)
        for j in range(4):
            cols = slice(j * block, (j + 1) * block)
            part[0, rs, cols] = nn(mixed[rs], wob[:, cols]).astype(BF)
        first1.append(scatter_start(0, b, part.at[0], own_lanes))
    fk_second = forward(fk_first, fkb.at[0], fkb.at[1], fkb.at[2])
    fv_first = relay_out(fv, fvb.at[0], fvb.at[1])
    second1 = [scatter_middle(0, b, part.at[0], own_lanes, first1[b]) for b in both]
    gathers = []
    for b in both:
        rs = bucket_rows(b)
        total = scatter_end(0, b, part.at[0], own_lanes, first1[b], second1[b])
        middle = x_ref[rs, own_lanes(m)].astype(F32) + total
        mid_own[rs] = middle
        mid_own_b[rs] = middle.astype(BF)
        gathers.append(gather_start(mid_own_b, mid, moved_lanes, slices[b]))
    onward = [gather_middle(mid, moved_lanes, slices[b], gathers[b]) for b in both]
    for b in both:
        gather_end(gathers[b], onward[b])
        mix(b, take_mid, mean2, rstd2, CLOSING, CLOSING + 1, [kin, cri])
    for copy in g_second[4]:
        copy.wait_recv()
    top_copy.wait()

    def top(b):
        return seen[bucket_rows(b)].astype(F32) * masks[b][4]

    for b in both:
        rs = bucket_rows(b)
        total = nn(cri[rs, 0:block], g[0, 4])
        for j in range(1, 4):
            total = total + nn(cri[rs, j * block : (j + 1) * block], g[j, 4])
        gate = jax.nn.sigmoid(total)
        channel_gate[rs] = gate
        cg_own[rs] = (top(b) * gate).astype(BF)
    gathers = gather_start(cg_own, cg, moved_lanes, all_rows)
    for copy in fk_second:
        copy.wait_recv()

    def fk_piece(j):
        return fk if j == 0 else fkb.at[j - 1]

    def fv_piece(j):
        return fv if j == 0 else fvb.at[j - 1]

    for b in both:
        rs = bucket_rows(b)
        total = nn(kin[rs, 0:block], fk[...])
        for j in range(1, 4):
            total = total + nn(kin[rs, j * block : (j + 1) * block], fkb[j - 1])
        positive = jnp.maximum(total, 0.0)
        hid[rs] = (positive * positive).astype(BF)
        pos[rs] = positive.astype(BF)
    onward = gather_middle(cg, moved_lanes, all_rows, gathers)
    fv_second = forward(fv_first, fvb.at[0], fvb.at[1], fvb.at[2])
    gather_end(gathers, onward)

    piece = own

    def product_piece(lhs, rhs, i):
        return tn(lhs[:, i * piece : (i + 1) * piece], rhs[...])

    def ff_grad_start(k, lhs, rhs):
        for i, (way, slot) in ((2, (0, 0)), (6, (0, 1)), (5, (1, 0)), (7, (1, 1))):
            ff_send[k, way, slot] = product_piece(lhs, rhs, i).astype(BF)
        return (
            links.push(ff_send.at[k, 0], ff_got.at[k, 0], x_peer),
            links.push(ff_send.at[k, 1], ff_got.at[k, 1], y_peer),
        )

    def ff_grad_middle(k, lhs, rhs, first):
        first[0].wait_recv()
        links.sent(first[0])
        ff_send[k, 0, 0] = (product_piece(lhs, rhs, 4) + ff_got[k, 0, 1].astype(F32)).astype(BF)
        one = links.push(ff_send.at[k, 0, 0], ff_got2.at[k, 0], y_peer)
        first[1].wait_recv()
        links.sent(first[1])
        ff_send[k, 1, 0] = (product_piece(lhs, rhs, 3) + ff_got[k, 1, 1].astype(F32)).astype(BF)
        return one, links.push(ff_send.at[k, 1, 0], ff_got2.at[k, 1], x_peer)

    def ff_grad_end(k, lhs, rhs, second, out):
        for way in range(2):
            second[way].wait_recv()
            total = product_piece(lhs, rhs, way) + ff_got[k, way, 0].astype(F32) + ff_got2[k, way].astype(F32)
            out[way * piece : (way + 1) * piece] = total.astype(BF)

    fv_grad1 = ff_grad_start(0, cg, hid)

    for copy in fv_second:
        copy.wait_recv()
    first3 = []
    for b in both:
        rs = bucket_rows(b)
        for j in range(4):
            cols = slice(j * block, (j + 1) * block)
            part[1, rs, cols] = nt(hid[rs], fv_piece(j)[...]).astype(BF)
        first3.append(scatter_start(1, b, part.at[1], moved_lanes))
    second3 = []
    for b in both:
        rs = bucket_rows(b)
        total = nn(cg[rs, 0:block], fv[...])
        for j in range(1, 4):
            total = total + nn(cg[rs, j * block : (j + 1) * block], fvb[j - 1])
        pre[rs] = (total * 2.0 * pos[rs].astype(F32)).astype(BF)
        second3.append(scatter_middle(1, b, part.at[1], moved_lanes, first3[b]))
    fk_grad1 = ff_grad_start(1, kin, pre)
    sens[...] = jnp.zeros_like(sens)
    head_small[...] = jnp.zeros_like(head_small)
    gate_first = []
    out_first = []
    for b in both:
        rs = bucket_rows(b)
        gate = channel_gate[rs]
        total = scatter_end(1, b, part.at[1], moved_lanes, first3[b], second3[b])
        out_own[rs] = ((mid_own[rs] + gate * total) * masks[b][4]).astype(BF)
        gig[rs] = (top(b) * total * gate * (1.0 - gate)).astype(BF)

    ones = jnp.ones((8, own), BF)

    def back_mix(k, b, target, take, mean, rstd, gain_row, mix_row, sens_row, grads):
        rs = bucket_rows(b)
        same, following = masks[b][2], masks[b][3]
        average, scale = mean[rs, :], rstd[rs, :]
        one, two = jnp.zeros((8, rows), F32), jnp.zeros((8, rows), F32)
        for e in range(parts):
            cols = slice(e * own, (e + 1) * own)
            hat = (take(rs, e).astype(F32) - average) * scale
            gain = order_vec[gain_row : gain_row + 1, cols]
            normed = hat * gain
            change = normed - roll_rows(normed, 1) * same
            now = jnp.zeros((rows, own), F32)
            later = jnp.zeros((rows, own), F32)
            for i, (grad, weight_of) in enumerate(grads):
                value = nt(grad(rs), weight_of(e))
                at = slice(sens_row + i, sens_row + i + 1)
                sens[at, cols] += jnp.sum(value * change, axis=0, keepdims=True)
                weight = order_vec[mix_row + i : mix_row + i + 1, cols]
                now = now + value * weight
                later = later + value * (1.0 - weight)
            back = now + following * roll_rows(later, -1)
            target[rs, cols] = back.astype(BF)
            scaled = back * gain
            one = one + nt(ones, scaled.astype(BF))
            two = two + nt(ones, (scaled * hat).astype(BF))
        small[k, b, 0, 0:8] = one
        small[k, b, 0, 8:16] = two

    def piece_rows(e):
        return slice((e % 2) * own, (e % 2 + 1) * own)

    def take_mid_own(rs, e):
        return mid[rs, e * own : (e + 1) * own]

    def take_x_own(rs, e):
        start = pl.multiple_of(order[e // 2] * block + (e % 2) * own, own)
        return x_ref[rs, pl.ds(start, own)]

    def fk_rows(e):
        return fk_piece(e // 2)[piece_rows(e)]

    def g_rows(w):
        return lambda e: g[e // 2, w, piece_rows(e)]

    for copies in first1 + second1:
        for copy in copies:
            links.sent(copy)
    first4, stats4 = [], []
    for b in both:
        back_mix(
            0, b, part.at[0], take_mid_own, mean2, rstd2, CLOSING, CLOSING + 1, 4,
            [(lambda rs: pre[rs], fk_rows), (lambda rs: gig[rs], g_rows(4))],
        )
        first4.append(scatter_start(2, b, part.at[0], moved_lanes))
        stats4.append(stats_start(0, b))
    second4, stats4b = [], []
    for b in both:
        second4.append(scatter_middle(2, b, part.at[0], moved_lanes, first4[b]))
        stats4b.append(stats_middle(0, b, stats4[b]))
    fv_grad2 = ff_grad_middle(0, cg, hid, fv_grad1)

    def norm_back(b, back, hat, gain_row, rstd, means):
        gain = vec[gain_row : gain_row + 1, own_lanes(m)]
        return (back * gain - means[0] - hat * means[1]) * rstd[bucket_rows(b), :]

    closing = jnp.zeros((1, own), F32)
    gathers = []
    for b in both:
        rs = bucket_rows(b)
        back = scatter_end(2, b, part.at[0], moved_lanes, first4[b], second4[b])
        means = stats_end(0, b, stats4b[b])
        hat = (mid_own_b[rs].astype(F32) - mean2[rs, :]) * rstd2[rs, :]
        closing = closing + jnp.sum(back * hat, axis=0, keepdims=True)
        value = top(b) + norm_back(b, back, hat, CLOSING, rstd2, means)
        middle_grad[rs] = value
        branch_own[rs] = value.astype(BF)
        gathers.append(gather_start(branch_own, branch, own_lanes, slices[b]))
    onward = [gather_middle(branch, own_lanes, slices[b], gathers[b]) for b in both]
    fk_grad2 = ff_grad_middle(1, kin, pre, fk_grad1)

    def time_backward(b):
        rs = bucket_rows(b)
        allowed = allowed_pairs(b)
        for p in range(pairs):
            cols = slice(p * 128, (p + 1) * 128)
            out_scale, in_scale = decay_scales(cols)
            u, gn = head_vec[REWARD : REWARD + 1, cols], head_vec[LANE : LANE + 1, cols]
            g_in, gate, n = mixed_grad[rs, cols], gate_raw[rs, cols], n_ref[rs, cols]
            sg = jax.nn.sigmoid(gate)
            silu = gate * sg
            time_grads[3, rs, cols] = (g_in * n * gn * sg * (1.0 + gate * (1.0 - sg))).astype(BF)
            q = g_in * gn * silu
            dout = q - head_sums(q, low) / LANE_WIDTH - n * (head_sums(q * n, low) / LANE_WIDTH)
            dout = dout * n_scale[rs, cols]
            r, k = rkv[0, rs, cols].astype(F32), rkv[1, rs, cols].astype(F32)
            v = rkv[2, rs, cols]
            rt, kt = r * out_scale, (k * in_scale).astype(BF)
            rtb = rt.astype(BF)
            now = r * u * k
            diag = head_sums(dout * v.astype(F32), low)
            found = []
            for mine in (low, jnp.logical_not(low)):
                dmine = jnp.where(mine, dout, 0.0).astype(BF)
                scores = scores_of(rt, kt, now, mine, allowed)
                a = jnp.where(allowed, nt(dmine, v), 0.0).astype(BF)
                found.append((tn(scores, dmine), nn(a, kt), tn(a, rtb)))
            dv, drt, dkt = (jnp.where(low, one, two) for one, two in zip(*found))
            time_grads[0, rs, cols] = (drt * out_scale + u * k * diag).astype(BF)
            time_grads[1, rs, cols] = (dkt * in_scale + u * r * diag).astype(BF)
            time_grads[2, rs, cols] = dv.astype(BF)
            lags = places * rtb.astype(F32) * drt - (places + 1.0) * kt.astype(F32) * dkt
            log_decay = -jnp.exp(head_vec[FADING : FADING + 1, cols])
            head_small[0:1, cols] += jnp.sum(lags, axis=0, keepdims=True) * log_decay
            head_small[1:2, cols] += jnp.sum(r * k * diag, axis=0, keepdims=True)
            head_small[2:3, cols] += jnp.sum(g_in * n * silu, axis=0, keepdims=True)

    for copies in first3 + second3:
        for copy in copies:
            links.sent(copy)
    first6, stats6 = [], []
    for b in both:
        gather_end(gathers[b], onward[b])
        rs = bucket_rows(b)
        mixed_grad[rs] = nt(branch[rs], wob[...])
        time_backward(b)
        back_mix(
            1, b, part.at[1], take_x_own, mean1, rstd1, OPENING, OPENING + 1, 0,
            [((lambda rs, w=w: time_grads[w, rs]), g_rows(w)) for w in range(4)],
        )
        first6.append(scatter_start(3, b, part.at[1], moved_lanes))
        stats6.append(stats_start(1, b))

    def tm_lhs(w):
        return acts.at[w] if w < 4 else cri

    def tm_rhs(w):
        return time_grads.at[w] if w < 4 else gig

    tm_first = {}
    for w in (4, 0, 1, 2, 3):
        for i, (way, slot) in ((2, (0, 0)), (6, (0, 1)), (5, (1, 0)), (7, (1, 1))):
            tm_send[w, way, slot] = product_piece(tm_lhs(w), tm_rhs(w), i).astype(BF)
        tm_first[w] = (
            links.push(tm_send.at[w, 0], tm_got.at[w, 0], x_peer),
            links.push(tm_send.at[w, 1], tm_got.at[w, 1], y_peer),
        )
    second6, stats6b = [], []
    for b in both:
        second6.append(scatter_middle(3, b, part.at[1], moved_lanes, first6[b]))
        stats6b.append(stats_middle(1, b, stats6[b]))
    for j in range(4):
        wo_part[j] = tn(mixed[:, j * LANE_WIDTH : (j + 1) * LANE_WIDTH], branch[...]).astype(BF)
    wo_copies = [
        links.push(wo_part.at[peer[0]], wo_got.at[i], peer) for i, peer in enumerate((x_peer, y_peer, diagonal))
    ]
    ff_grad_end(0, cg, hid, fv_grad2, ffv_out)
    tm_second = {}
    for w in (4, 0, 1, 2, 3):
        tm_first[w][0].wait_recv()
        links.sent(tm_first[w][0])
        value = product_piece(tm_lhs(w), tm_rhs(w), 4) + tm_got[w, 0, 1].astype(F32)
        tm_send[w, 0, 0] = value.astype(BF)
        one = links.push(tm_send.at[w, 0, 0], tm_got2.at[w, 0], y_peer)
        tm_first[w][1].wait_recv()
        links.sent(tm_first[w][1])
        value = product_piece(tm_lhs(w), tm_rhs(w), 3) + tm_got[w, 1, 1].astype(F32)
        tm_send[w, 1, 0] = value.astype(BF)
        tm_second[w] = (one, links.push(tm_send.at[w, 1, 0], tm_got2.at[w, 1], x_peer))

    opening = jnp.zeros((1, own), F32)
    for b in both:
        rs = bucket_rows(b)
        back = scatter_end(3, b, part.at[1], moved_lanes, first6[b], second6[b])
        means = stats_end(1, b, stats6b[b])
        hat = (x_ref[rs, own_lanes(m)].astype(F32) - mean1[rs, :]) * rstd1[rs, :]
        opening = opening + jnp.sum(back * hat, axis=0, keepdims=True)
        value = middle_grad[rs] + norm_back(b, back, hat, OPENING, rstd1, means)
        gin_own[rs] = value.astype(BF)
    gin_first = gather_start(gin_own, gin_full, own_lanes, all_rows)
    out_first = gather_start(out_own, out_full, own_lanes, all_rows)

    vec_copies = links.group(
        [sens.at[:, moved_lanes(other)] for other in others],
        [u_got.at[i] for i in range(parts - 1)],
        [(d, other) for other in others],
        u_got,
    )
    gin_second = gather_middle(gin_full, own_lanes, all_rows, gin_first)
    out_second = gather_middle(out_full, own_lanes, all_rows, out_first)
    vec_copies.wait_recv()
    total = sens[:, moved_lanes(m)]
    for i in range(parts - 1):
        total = total + u_got[i]
    u2_own[0:8] = total
    u2_own[6:7] = opening
    u2_own[7:8] = closing
    u2_own[8:16] = head_small[...]
    dp_copies = links.group(
        [u2_own] * 3, [u2_got.at[i] for i in range(3)], [x_peer, y_peer, diagonal], u2_got
    )
    dp_copies.wait_recv()
    u3_own[...] = (u2_own[...] + u2_got[0]) + (u2_got[1] + u2_got[2])
    all_copies = links.group(
        [u3_own] * (parts - 1),
        [u3_got.at[m]] * (parts - 1),
        [(d, other) for other in others],
        u3_got.at[pl.ds(0, parts - 1)],
    )
    u3_got[m] = u3_own[...]

    back_copies = []
    for w in (4, 0, 1, 2, 3):
        links.sent(arrivals[w])
        sums = blocks.at[w] if w < 4 else channel_sum
        for way in range(2):
            tm_second[w][way].wait_recv()
            value = product_piece(tm_lhs(w), tm_rhs(w), way)
            value = value + tm_got[w, way, 0].astype(F32) + tm_got2[w, way].astype(F32)
            sums[4 * way : 4 * way + 4] = value.astype(BF).reshape(4, shard, own)
        back_copies.append(
            links.group(
                [sums.at[other] for other in others],
                [back_out.at[w, m]] * (parts - 1),
                [(d, other) for other in others],
                back_out.at[w, pl.ds(0, parts - 1)],
            )
        )
        back_out[w, m] = sums[m]
    ff_grad_end(1, kin, pre, fk_grad2, ffk_out)
    total = wo_part[d].astype(F32)
    for i, copy in enumerate(wo_copies):
        copy.wait_recv()
        total = total + wo_got[i].astype(F32)
    wo_out[...] = total.astype(BF)
    all_copies.wait_recv()
    upper_d = lax.rem(d, 2) == 1
    low_vec = lax.broadcasted_iota(jnp.int32, (8, 128), 1) < LANE_WIDTH
    for e in range(2):
        vec_out[0:8, e * own : (e + 1) * own] = u3_got[2 * d + e, 0:8]
    for u in range(4):
        lanes = pl.ds(pl.multiple_of(lax.div(d, 2) * 128, 128), 128)
        first, second = u3_got[2 * u, 8:16, lanes], u3_got[2 * u + 1, 8:16, lanes]
        first = jnp.where(upper_d, swap_halves(first), first)
        second = jnp.where(upper_d, second, swap_halves(second))
        vec_out[8:16, u * 128 : (u + 1) * 128] = jnp.where(low_vec, first, second)
    gather_end(gin_first, gin_second)
    gather_end(out_first, out_second)
    for copy in back_copies:
        copy.wait_recv()
    links.finish()


def finish_kernel(out, gin, ffk, ffv, back, wo, out_o, gin_o, ffk_o, ffv_o, r_o, k_o, v_o, g_o, c_o, wo_o):
    out_o[...] = out[...].reshape(out_o.shape)
    gin_o[...] = gin[...].reshape(gin_o.shape)
    ffk_o[...] = ffk[...].astype(F32)
    ffv_o[...] = ffv[...].astype(F32)
    wo_o[...] = wo[...].astype(F32)
    parts, shard, own = back.shape[1:]
    low = lax.broadcasted_iota(jnp.int32, (shard, 128), 1) < LANE_WIDTH
    for w, target in enumerate((r_o, k_o, v_o, g_o)):
        for j in range(4):
            for u in range(4):
                lanes = slice((j // 2) * 128, (j // 2 + 1) * 128)
                first = back[w, 2 * u, :, lanes].astype(F32)
                second = back[w, 2 * u + 1, :, lanes].astype(F32)
                if j % 2 == 0:
                    tile = jnp.where(low, first, swap_halves(second))
                else:
                    tile = jnp.where(low, swap_halves(first), second)
                start = j * 4 * 128 + u * 128
                target[:, start : start + 128] = tile
    for to in range(parts):
        c_o[:, to * own : (to + 1) * own] = back[4, to].astype(F32)


def fast_body(*args):
    (
        block_arguments, bundled_spans, opening_gain, mix_r, mix_k, mix_v, mix_g, w_recept, w_key, w_value, w_gate,
        fading, reward, lane_gain, w_out, closing_gain, mix_fk, mix_fr, fk, fv, w_channel, upstream,
    ) = args
    buckets, bucket_rows, width = block_arguments.shape
    rows = buckets * bucket_rows
    parts, chips = 8, 4
    own, block = width // parts, width // 4
    hidden = fk.shape[1]
    shard = w_out.shape[0]
    vectors = [
        opening_gain, mix_r, mix_k, mix_v, mix_g, closing_gain, mix_fk, mix_fr, fading, reward, lane_gain,
    ]
    vec = jnp.stack(vectors + [opening_gain] * (16 - len(vectors)))
    v, sm = pltpu.VMEM, pltpu.SMEM
    vm = pl.BlockSpec(memory_space=pltpu.VMEM)
    half_block = block // 2
    scratch = [
        v((4, parts, shard, own), BF), v((4, 5, block, own), BF), v((3, block, hidden), BF), v((3, block, hidden), BF),
        v((4 * shard, width), BF), v((4, rows, width), BF), v((rows, 1), F32), v((rows, 1), F32), v((rows, 1), F32),
        v((rows, 1), F32), v((16, width), F32), v((16, own), F32), v((rows, own), BF),
        v((3, rows, own), BF), v((rows, own), F32), v((rows, own), F32), v((rows, own), F32), v((rows, own), BF),
        v((2, rows, width), BF), v((4, buckets, chips, bucket_rows, own), BF),
        v((buckets, chips - 1, bucket_rows, own), BF), v((4, buckets, chips - 1, bucket_rows, own), BF),
        v((2, buckets, chips + 2, 16, bucket_rows), F32),
        v((rows, own), F32), v((rows, own), BF), v((rows, width), BF), v((rows, width), BF), v((rows, width), BF),
        v((rows, hidden), BF), v((rows, hidden), BF), v((rows, hidden), BF), v((rows, own), F32), v((rows, own), BF),
        v((rows, width), BF),
        v((rows, own), BF), v((rows, own), BF), v((rows, own), F32), v((rows, own), BF),
        v((rows, width), BF), v((rows, own), F32), v((4, rows, own), BF), v((8, width), F32), v((8, own), F32),
        v((2, 2, 2, own, hidden), BF), v((2, 2, 2, own, hidden), BF), v((2, 2, own, hidden), BF),
        v((5, 2, 2, own, own), BF), v((5, 2, 2, own, own), BF), v((5, 2, own, own), BF),
        v((parts, shard, own), BF),
        v((4, shard, width), BF), v((3, shard, width), BF), v((rows, own), BF),
        v((parts - 1, 8, own), F32), v((16, own), F32), v((3, 16, own), F32), v((16, own), F32),
        v((parts, 16, own), F32),
        pltpu.SemaphoreType.DMA((COPIES,)), pltpu.SemaphoreType.DMA((COPIES,)), pltpu.SemaphoreType.DMA,
    ]
    out = pl.pallas_call(
        block_kernel,
        out_shape=[
            struct((rows, width), BF), struct((rows, width), BF), struct((block, hidden), BF),
            struct((block, hidden), BF), struct((5, parts, shard, own), BF), struct((shard, width), BF),
            struct((16, block), F32),
        ],
        in_specs=[pl.BlockSpec(memory_space=sm), vm, pl.BlockSpec(memory_space=pl.ANY)] + [vm] * 9,
        out_specs=[vm] * 7,
        scratch_shapes=scratch,
        compiler_params=pltpu.CompilerParams(
            collective_id=0, has_side_effects=True, vmem_limit_bytes=VMEM_LIMIT
        ),
        name="whole_block",
    )(
        bundled_spans.reshape(buckets, -1), block_arguments.reshape(rows, width), upstream.reshape(rows, width), vec,
        w_recept, w_key, w_value, w_gate, w_out, w_channel, fk, fv,
    )
    small = out[6]
    square = struct((shard, width), F32)
    done = pl.pallas_call(
        finish_kernel,
        out_shape=[
            struct(block_arguments.shape, BF), struct(block_arguments.shape, BF), struct(fk.shape, F32),
            struct(fv.shape, F32), square, square, square, square, square, square,
        ],
        in_specs=[vm] * 6,
        out_specs=[vm] * 10,
        compiler_params=pltpu.CompilerParams(vmem_limit_bytes=48 << 20),
        name="finish",
    )(*out[:6])
    outputs, grad_inputs, d_fk, d_fv, d_r, d_k, d_v, d_g, d_c, d_o = done
    return (
        outputs, grad_inputs, small[6], small[0], small[1], small[2], small[3], d_r, d_k, d_v, d_g,
        small[8], small[9], small[10], d_o, small[7], small[4], small[5], d_fk, d_fv, d_c,
    )


def body(*args):
    data_parts, parts = lax.axis_size("dp"), lax.axis_size("mp")
    width, shard, hidden = args[0].shape[2], args[7].shape[0], args[18].shape[1]
    fitted = (
        data_parts == 4
        and parts == 8
        and shard == LANE_WIDTH
        and width == 4 * parts * shard
        and hidden % 128 == 0
        and args[0].shape[:2] == (2, 128)
    )
    return fast_body(*args) if fitted else general_body(*args)


def solution(mesh):
    return jax.shard_map(
        body,
        mesh=mesh,
        in_specs=(
            P(None, "dp", None),
            P(None, "dp", None),
            P(),
            P(),
            P(),
            P(),
            P(),
            P(("dp", "mp"), None),
            P(("dp", "mp"), None),
            P(("dp", "mp"), None),
            P(("dp", "mp"), None),
            P(),
            P(),
            P(),
            P(("dp", "mp"), None),
            P(),
            P(),
            P(),
            P("dp", "mp"),
            P("dp", "mp"),
            P(("dp", "mp"), None),
            P(None, "dp", None),
        ),
        out_specs=(
            P(None, "dp", None),
            P(None, "dp", None),
            P("dp"),
            P("dp"),
            P("dp"),
            P("dp"),
            P("dp"),
            P(("dp", "mp"), None),
            P(("dp", "mp"), None),
            P(("dp", "mp"), None),
            P(("dp", "mp"), None),
            P("dp"),
            P("dp"),
            P("dp"),
            P(("dp", "mp"), None),
            P("dp"),
            P("dp"),
            P("dp"),
            P("dp", "mp"),
            P("dp", "mp"),
            P(("dp", "mp"), None),
        ),
        check_vma=False,
    )
```

```python
import functools
from functools import reduce

import jax
import jax.numpy as jnp
from jax import lax
from jax.experimental import pallas as pl
from jax.experimental.pallas import tpu as pltpu
from jax.sharding import PartitionSpec as P

LANE_WIDTH = 64
SPAN = 64


EPSILON = 1e-05
GROUP_EPSILON = 0.25
MIXED_MODE = lax.Precision.HIGH


def shortened(x):
    return jax.tree.map(lambda a: a.astype(jnp.bfloat16) if a.dtype == jnp.float32 else a, x)


def product(first_operand, second_operand):
    return jnp.dot(first_operand, second_operand, preferred_element_type=jnp.float32)


def product_rows(first_operand, second_operand):
    return lax.dot_general(
        first_operand, second_operand, (((0,), (0,)), ((), ())), preferred_element_type=jnp.float32
    )


def product_back(first_operand, second_operand):
    return lax.dot_general(
        first_operand, second_operand, (((1,), (1,)), ((), ())), preferred_element_type=jnp.float32
    )


def layer_norm(values, gain_entries):
    average = jnp.mean(values, axis=-1, keepdims=True)
    centered = values - average
    spread = jnp.mean(centered * centered, axis=-1, keepdims=True)
    return centered * lax.rsqrt(spread + EPSILON) * gain_entries


def group_norm(values, head_count):
    grouped = values.reshape(values.shape[0], head_count, -1)
    average = jnp.mean(grouped, axis=-1, keepdims=True)
    centered = grouped - average
    spread = jnp.mean(centered * centered, axis=-1, keepdims=True)
    return (centered * lax.rsqrt(spread + GROUP_EPSILON)).reshape(values.shape)


def segment_info(lengths, row_count):
    segment_ends = jnp.cumsum(lengths)
    places = jnp.arange(row_count, dtype=jnp.int32)
    sequence_label = jnp.sum((places[:, None] >= segment_ends[None, :]).astype(jnp.int32), axis=1)
    earlier = jnp.concatenate([jnp.full((1,), -1, jnp.int32), sequence_label[:-1]])
    common_series_filter = (sequence_label == earlier).astype(jnp.float32)
    valid_rows = (places < segment_ends[-1]).astype(jnp.float32)
    return (sequence_label, common_series_filter, valid_rows)


def shift_rows(values, common_series_filter):
    before = jnp.concatenate([jnp.zeros_like(values[:1]), values[:-1]], axis=0)
    return before * common_series_filter[:, None]


def iterative_renewal(
    accept_lines,
    lookup_weight_lines,
    payload_weight_lines,
    decay_logarithm,
    reward_scaler,
    sequence_label,
    layer_rows,
):
    row_count, head_count, head_width = accept_lines.shape
    block_count = row_count // layer_rows
    blocked = (block_count, layer_rows, head_count, head_width)
    accept_blocks = accept_lines.reshape(blocked)
    lookup_blocks = lookup_weight_lines.reshape(blocked)
    payload_blocks = payload_weight_lines.reshape(blocked)
    segment_blocks = sequence_label.reshape(block_count, layer_rows)
    positions = jnp.arange(layer_rows, dtype=jnp.float32)
    middle_step = float(layer_rows // 2)
    query_scale = jnp.exp(decay_logarithm[None] * (positions - middle_step)[:, None, None])
    key_scale = jnp.exp(decay_logarithm[None] * (middle_step - 1.0 - positions)[:, None, None])
    scores = jnp.einsum(
        "cthi,cshi->chts",
        accept_blocks * query_scale,
        lookup_blocks * key_scale,
        precision=MIXED_MODE,
    )
    causal = positions[:, None] > positions[None, :]
    within = segment_blocks[:, :, None] == segment_blocks[:, None, :]
    allowed = jnp.logical_and(causal[None], within).astype(jnp.float32)
    scores = scores * allowed[:, None]
    nested_routine = jnp.einsum("chts,cshj->cthj", scores, payload_blocks, precision=MIXED_MODE)
    reward_term = jnp.sum(accept_blocks * reward_scaler * lookup_blocks, axis=-1)
    nested_routine = nested_routine + reward_term[..., None] * payload_blocks
    last_segment = segment_blocks[:, -1]
    prior_segment = jnp.concatenate([jnp.full((1,), -1, jnp.int32), last_segment[:-1]])
    tail_scale = jnp.exp(decay_logarithm[None] * (layer_rows - 1.0 - positions)[:, None, None])
    tail_keep = (segment_blocks == last_segment[:, None]).astype(jnp.float32)
    added_state = jnp.einsum(
        "cshi,cshj->chij",
        lookup_blocks * tail_scale * tail_keep[:, :, None, None],
        payload_blocks,
        precision=MIXED_MODE,
    )
    carry_keep = (last_segment == prior_segment).astype(jnp.float32)
    whole_decay = jnp.exp(decay_logarithm * layer_rows)

    def advance(carry_state, piece_pair):
        addition, keep_flag = piece_pair
        return (whole_decay[:, :, None] * carry_state * keep_flag + addition, carry_state)

    initial = jnp.zeros((head_count, head_width, head_width), jnp.float32)
    unused, starts = lax.scan(advance, initial, (added_state, carry_keep))
    entry_keep = (segment_blocks == prior_segment[:, None]).astype(jnp.float32)
    entry_scale = jnp.exp(decay_logarithm[None] * positions[:, None, None])
    outside = jnp.einsum(
        "cthi,chij->cthj",
        accept_blocks * entry_scale * entry_keep[:, :, None, None],
        starts,
        precision=MIXED_MODE,
    )
    return (nested_routine + outside).reshape(row_count, head_count, head_width)


def add_terms(first_terms, second_terms):
    return jax.tree.map(jnp.add, first_terms, second_terms)


def general_body(
    block_arguments,
    bundled_spans,
    opening_normalize_scale,
    accept_lagmix,
    lookup_lagmix,
    payload_lagmix,
    valve_lagmix,
    accept_weights,
    lookup_weights,
    payload_weights,
    valve_weights,
    fading_speed_logs,
    present_reward,
    lane_normalize_scale,
    emission_weights,
    closing_normalize_scale,
    feedforward_lookup_lagmix,
    feedforward_accept_lagmix,
    feedforward_lookup_weights,
    feedforward_payload_weights,
    feedforward_accept_weights,
    upstream_sensitivity,
):
    micro_count, row_count, model_width = block_arguments.shape
    layer_rows = SPAN
    data_parts = lax.axis_size("dp")
    model_parts = lax.axis_size("mp")
    shard_rows = accept_weights.shape[0]
    model_place = lax.axis_index("mp")
    partition_lanes = model_width // LANE_WIDTH

    def own_columns(values):
        split_values = values.reshape(row_count, data_parts, model_parts, shard_rows)
        picked = lax.dynamic_index_in_dim(split_values, model_place, axis=2, keepdims=False)
        return picked.reshape(row_count, data_parts * shard_rows)

    outputs_list = []
    input_grads = []
    gradient_terms = []
    for micro_index in range(micro_count):
        projections = (
            lax.all_gather(accept_weights, ("dp", "mp"), axis=0, tiled=True),
            lax.all_gather(lookup_weights, ("dp", "mp"), axis=0, tiled=True),
            lax.all_gather(payload_weights, ("dp", "mp"), axis=0, tiled=True),
            lax.all_gather(valve_weights, ("dp", "mp"), axis=0, tiled=True),
            lax.all_gather(emission_weights, ("dp", "mp"), axis=0, tiled=True),
            lax.all_gather(feedforward_accept_weights, ("dp", "mp"), axis=0, tiled=True),
        )
        hidden_pair = (
            lax.all_gather(feedforward_lookup_weights, "dp", axis=0, tiled=True),
            lax.all_gather(feedforward_payload_weights, "dp", axis=0, tiled=True),
        )
        full_recept, full_key, full_value, full_gate, full_output, full_channel = projections
        hidden_key, hidden_value = hidden_pair
        sequence_label, common_series_filter, valid_rows = segment_info(
            bundled_spans[micro_index, 0], row_count
        )
        rows_float = block_arguments[micro_index].astype(jnp.float32)

        def front_part(rows_value, gain_entries, recept_mix, key_mix, value_mix, gate_mix):
            normed = layer_norm(rows_value, gain_entries)
            before = shift_rows(normed, common_series_filter)
            return tuple(
                (
                    normed * weight_mix + before * (1.0 - weight_mix)
                    for weight_mix in (recept_mix, key_mix, value_mix, gate_mix)
                )
            )

        front_values, front_pull = jax.vjp(
            front_part,
            rows_float,
            opening_normalize_scale,
            accept_lagmix,
            lookup_lagmix,
            payload_lagmix,
            valve_lagmix,
        )
        recept_in, key_in, value_in, gate_in = [
            front_piece.astype(jnp.bfloat16) for front_piece in front_values
        ]
        accept_lines = product(recept_in, full_recept).astype(jnp.bfloat16)
        lookup_weight_lines = product(key_in, full_key).astype(jnp.bfloat16)
        payload_weight_lines = product(value_in, full_value).astype(jnp.bfloat16)
        gate_raw = product(gate_in, full_gate)

        def middle_part(
            receptance_activation,
            key_value_product,
            value_activation,
            gate_activation,
            decay_parameter,
            reward_weight,
            gain_entries,
        ):
            decay_logarithm = -jnp.exp(decay_parameter).reshape(partition_lanes, -1)
            reward_scaler = reward_weight.reshape(partition_lanes, -1)
            reformed_array = (row_count, partition_lanes, model_width // partition_lanes)
            lane_answers = iterative_renewal(
                receptance_activation.reshape(reformed_array),
                key_value_product.reshape(reformed_array),
                value_activation.reshape(reformed_array),
                decay_logarithm,
                reward_scaler,
                sequence_label,
                layer_rows,
            )
            grouped = (
                group_norm(lane_answers.reshape(row_count, model_width), partition_lanes)
                * gain_entries
            )
            return grouped * jax.nn.silu(gate_activation)

        mixed_float, middle_pull = jax.vjp(
            middle_part,
            accept_lines.astype(jnp.float32),
            lookup_weight_lines.astype(jnp.float32),
            payload_weight_lines.astype(jnp.float32),
            gate_raw,
            fading_speed_logs,
            present_reward,
            lane_normalize_scale,
        )
        merged_lanes = mixed_float.astype(jnp.bfloat16)
        middle = rows_float + product(merged_lanes, full_output)

        def back_part(middle_value, gain_entries, key_mix, recept_mix):
            normed = layer_norm(middle_value, gain_entries)
            before = shift_rows(normed, common_series_filter)
            return (
                normed * key_mix + before * (1.0 - key_mix),
                normed * recept_mix + before * (1.0 - recept_mix),
            )

        channel_values, back_pull = jax.vjp(
            back_part,
            middle,
            closing_normalize_scale,
            feedforward_lookup_lagmix,
            feedforward_accept_lagmix,
        )
        channel_key_in = channel_values[0].astype(jnp.bfloat16)
        channel_recept_in = channel_values[1].astype(jnp.bfloat16)
        hidden_input = product(channel_key_in, hidden_key)
        hidden = jnp.square(jnp.maximum(hidden_input, 0.0)).astype(jnp.bfloat16)
        carried = lax.psum(product_back(hidden, hidden_value).astype(jnp.bfloat16), "mp").astype(
            jnp.float32
        )
        channel_gate = jax.nn.sigmoid(product(channel_recept_in, full_channel))
        outputs_list.append(
            ((middle + channel_gate * carried) * valid_rows[:, None]).astype(jnp.bfloat16)
        )
        top_grad = upstream_sensitivity[micro_index].astype(jnp.float32) * valid_rows[:, None]
        carried_grad = (top_grad * channel_gate).astype(jnp.bfloat16)
        gate_input_grad = (top_grad * carried * channel_gate * (1.0 - channel_gate)).astype(
            jnp.bfloat16
        )
        pre_grad = (
            product(carried_grad, hidden_value) * 2.0 * jnp.maximum(hidden_input, 0.0)
        ).astype(jnp.bfloat16)
        channel_key_grad = lax.psum(
            product_back(pre_grad, hidden_key).astype(jnp.bfloat16), "mp"
        ).astype(jnp.float32)
        channel_recept_grad = product_back(gate_input_grad, full_channel)
        middle_back, grad_second, feedforward_lookup_lagmix_sens, feedforward_accept_lagmix_sens = (
            back_pull((channel_key_grad, channel_recept_grad))
        )
        middle_grad = top_grad + middle_back
        branch_grad = middle_grad.astype(jnp.bfloat16)
        mixed_grad = product_back(branch_grad, full_output)
        output_term = product_rows(own_columns(merged_lanes), branch_grad)
        (
            receptance_single_precision,
            key_single_precision,
            value_single_precision,
            gate_single_precision,
            decay_gradient,
            reward_derivative,
            lane_normalize_derivative,
        ) = middle_pull(mixed_grad)
        recept_grad = receptance_single_precision.astype(jnp.bfloat16)
        key_grad = key_single_precision.astype(jnp.bfloat16)
        value_grad = value_single_precision.astype(jnp.bfloat16)
        gate_grad = gate_single_precision.astype(jnp.bfloat16)
        (
            line_derivatives,
            grad_first,
            grad_recept_mix,
            grad_key_mix,
            grad_value_mix,
            grad_gate_mix,
        ) = front_pull(
            (
                product_back(recept_grad, full_recept),
                product_back(key_grad, full_key),
                product_back(value_grad, full_value),
                product_back(gate_grad, full_gate),
            )
        )
        projection_terms = (
            product_rows(own_columns(recept_in), recept_grad),
            product_rows(own_columns(key_in), key_grad),
            product_rows(own_columns(value_in), value_grad),
            product_rows(own_columns(gate_in), gate_grad),
            output_term,
        )
        input_grads.append((middle_grad + line_derivatives).astype(jnp.bfloat16))
        local_terms = (
            grad_first,
            grad_recept_mix,
            grad_key_mix,
            grad_value_mix,
            grad_gate_mix,
            decay_gradient,
            reward_derivative,
            lane_normalize_derivative,
            grad_second,
            feedforward_lookup_lagmix_sens,
            feedforward_accept_lagmix_sens,
            product_rows(channel_key_in, pre_grad),
            product_rows(carried_grad, hidden),
            product_rows(own_columns(channel_recept_in), gate_input_grad),
        ) + projection_terms
        gradient_terms.append(local_terms)
    summed = reduce(add_terms, gradient_terms)
    summed = jax.tree.map(
        lambda part: part.astype(jnp.float32),
        lax.psum_scatter(shortened(summed), "dp", scatter_dimension=0, tiled=True),
    )
    (
        grad_first,
        grad_recept_mix,
        grad_key_mix,
        grad_value_mix,
        grad_gate_mix,
        decay_gradient,
        reward_derivative,
        lane_normalize_derivative,
        grad_second,
        feedforward_lookup_lagmix_sens,
        feedforward_accept_lagmix_sens,
        feedforward_lookup_derivative,
        feedforward_payload_derivative,
        feedforward_accept_derivative,
        grad_recept,
        grad_key,
        grad_value,
        grad_gate,
        grad_output,
    ) = summed
    return (
        jnp.stack(outputs_list),
        jnp.stack(input_grads),
        grad_first,
        grad_recept_mix,
        grad_key_mix,
        grad_value_mix,
        grad_gate_mix,
        grad_recept,
        grad_key,
        grad_value,
        grad_gate,
        decay_gradient,
        reward_derivative,
        lane_normalize_derivative,
        grad_output,
        grad_second,
        feedforward_lookup_lagmix_sens,
        feedforward_accept_lagmix_sens,
        feedforward_lookup_derivative,
        feedforward_payload_derivative,
        feedforward_accept_derivative,
    )


MESH = pl.DeviceIdType.MESH
BF = jnp.bfloat16
F32 = jnp.float32
VMEM_LIMIT = 63 << 20
OPENING, CLOSING, FADING, REWARD, LANE = 0, 5, 8, 9, 10


def struct(shape, dtype):
    return jax.ShapeDtypeStruct(shape, dtype)


def flip(place, other):
    low = lax.rem(lax.rem(place, 2) + lax.rem(other, 2), 2)
    high = lax.rem(lax.div(place, 2) + lax.div(other, 2), 2)
    return 2 * high + low


def nt(a, b):
    return lax.dot_general(a, b, (((1,), (1,)), ((), ())), preferred_element_type=F32)


def tn(a, b):
    return lax.dot_general(a, b, (((0,), (0,)), ((), ())), preferred_element_type=F32)


def nn(a, b):
    return lax.dot_general(a, b, (((1,), (0,)), ((), ())), preferred_element_type=F32)


def roll_rows(values, shift):
    return pltpu.roll(values, shift % values.shape[0], 0)


def swap_halves(tile):
    return pltpu.roll(tile, LANE_WIDTH, 1)


def head_sums(values, low):
    first = jnp.sum(jnp.where(low, values, 0.0), axis=1, keepdims=True)
    second = jnp.sum(jnp.where(low, 0.0, values), axis=1, keepdims=True)
    return jnp.where(low, first, second)


class Links:
    def __init__(self, send, recv):
        self.send, self.recv = send, recv
        self.used = 0
        self.open = []

    def push(self, source, target, peer):
        i = self.used
        self.used += 1
        copy = pltpu.make_async_remote_copy(
            source, target, self.send.at[i], self.recv.at[i], device_id=peer, device_id_type=MESH
        )
        copy.start()
        self.open.append(copy)
        return copy

    def group(self, sources, targets, peers, whole):
        i = self.used
        self.used += 1
        for source, target, peer in zip(sources, targets, peers):
            pltpu.make_async_remote_copy(
                source, target, self.send.at[i], self.recv.at[i], device_id=peer, device_id_type=MESH
            ).start()
        copy = pltpu.make_async_remote_copy(
            whole, whole, self.send.at[i], self.recv.at[i], device_id=peers[0], device_id_type=MESH
        )
        self.open.append(copy)
        return copy

    def sent(self, copy):
        if any(other is copy for other in self.open):
            copy.wait_send()
            self.open = [other for other in self.open if other is not copy]

    def finish(self):
        for copy in self.open:
            copy.wait_send()


COPIES = 196


def block_kernel(
    spans, x_ref, up_ref, v0, v1, v2, v3, v4, v5, v6, v7, v8, v9, v10, w_recept, w_key, w_value, w_gate, w_out, w_channel, fk, fv,
    out_full, gin_full, ffk_out, ffv_out, back_out, wo_out, vec_out,
    vec, blocks, g, fkb, fvb, wob, acts, mean1, rstd1, mean2, rstd2, order_vec, head_vec, seen,
    rkv, gate_raw, n_ref, n_scale, mixed, part, half, pair, far, small,
    mid_own, mid_own_b, mid, kin, cri, hid, pos, pre, channel_gate, cg_own, cg,
    out_own, gig, middle_grad, branch_own, branch, mixed_grad, time_grads, sens, head_small,
    ff_send, ff_got, ff_got2, tm_send, tm_got, tm_got2, channel_sum,
    wo_part, wo_got, gin_own, u_got, u2_own, u2_got, u3_own, u3_got,
    send, recv, local,
):
    d, m = lax.axis_index("dp"), lax.axis_index("mp")
    z, c = lax.div(m, 2), lax.rem(m, 2)
    chips, parts = 4, 8
    buckets, rows = 2, x_ref.shape[0] // 2
    width = x_ref.shape[1]
    own = width // parts
    block = width // 4
    shard = w_out.shape[0]
    pairs = own // 128
    links = Links(send, recv)
    mate = (d, 2 * z + 1 - c)
    chips_away = [lax.rem(z + i, chips) for i in range(1, chips)]
    others = [lax.rem(m + i, parts) for i in range(1, parts)]
    x_peer = (d + 1 - 2 * lax.rem(d, 2), m)
    y_peer = (d + 2 - 4 * lax.div(d, 2), m)
    diagonal = (3 - d, m)
    order = [d, x_peer[0], y_peer[0], diagonal[0]]

    def own_lanes(owner):
        return pl.ds(pl.multiple_of(owner * own, own), own)

    def moved_lanes(owner):
        place = 2 * flip(lax.div(owner, 2), d) + lax.rem(owner, 2)
        return pl.ds(pl.multiple_of(place * own, own), own)

    def bucket_rows(b):
        return slice(b * rows, (b + 1) * rows)

    barrier = pltpu.get_barrier_semaphore()
    greeted = [(d, other) for other in others] + [x_peer, y_peer, diagonal]
    for peer in greeted:
        pl.semaphore_signal(barrier, inc=1, device_id=peer, device_id_type=MESH)
    top_copy = pltpu.make_async_copy(up_ref.at[:, own_lanes(m)], seen, local)
    top_copy.start()
    low16 = lax.broadcasted_iota(jnp.int32, (shard, 128), 1) < LANE_WIDTH
    vec[...] = jnp.zeros_like(vec)
    for i, ref in enumerate((v0, v1, v2, v3, v4, v5, v6, v7, v8, v9, v10)):
        vec[i : i + 1] = ref[...]

    def head_blocks(w, weight):
        for to in range(parts):
            for q in range(pairs):
                tiles = []
                for j in (2 * q, 2 * q + 1):
                    start = j * block + (to // 2) * 128
                    tiles.append(weight[:, start : start + 128].astype(F32))
                if to % 2 == 0:
                    tile = jnp.where(low16, tiles[0], swap_halves(tiles[1]))
                else:
                    tile = jnp.where(low16, swap_halves(tiles[0]), tiles[1])
                blocks[w, to, :, q * 128 : (q + 1) * 128] = tile.astype(BF)

    head_blocks(0, w_recept)
    pl.semaphore_wait(barrier, len(greeted))
    top_copy.wait()

    my_rows = pl.ds(pl.multiple_of(m * shard, shard), shard)

    def exchange(w):
        if w < 4:
            sources = [blocks.at[w, other] for other in others]
        else:
            sources = [w_channel.at[:, own_lanes(other)] for other in others]
        return links.group(
            sources,
            [g.at[0, w, my_rows]] * (parts - 1),
            [(d, other) for other in others],
            g.at[0, w, pl.ds(0, (parts - 1) * shard)],
        )

    def relay_out(source, slot1, slot2):
        return links.push(source, slot1, x_peer), links.push(source, slot2, y_peer)

    arrivals = [exchange(0)]
    for w, weight in ((1, w_key), (2, w_value), (3, w_gate)):
        head_blocks(w, weight)
        arrivals.append(exchange(w))
    arrivals.append(exchange(4))
    for w in range(4):
        g[0, w, my_rows] = blocks[w, m]
    g[0, 4, my_rows] = w_channel[:, own_lanes(m)]
    out_rows = pl.ds(pl.multiple_of(d * shard, shard), shard)
    wo_arrivals = [links.push(w_out, wob.at[out_rows], peer) for peer in (x_peer, y_peer, diagonal)]
    wob[out_rows] = w_out[...]
    fk_first = relay_out(fk, fkb.at[0], fkb.at[1])

    for j in range(4):
        order_vec[:, j * block : (j + 1) * block] = vec[
            :, pl.ds(pl.multiple_of(order[j] * block, block), block)
        ]
    low_row = lax.broadcasted_iota(jnp.int32, (16, 128), 1) < LANE_WIDTH
    upper = lax.rem(m, 2) == 1

    def head_tile(j):
        start = pl.multiple_of(j * block + lax.div(m, 2) * 128, 128)
        return vec[:, pl.ds(start, 128)]

    for q in range(pairs):
        first, second = head_tile(2 * q), head_tile(2 * q + 1)
        first = jnp.where(upper, swap_halves(first), first)
        second = jnp.where(upper, second, swap_halves(second))
        head_vec[:, q * 128 : (q + 1) * 128] = jnp.where(low_row, first, second)

    def row_masks(b):
        t = lax.broadcasted_iota(jnp.int32, (rows, 1), 0)
        lane = lax.broadcasted_iota(jnp.int32, (1, rows), 1)
        label, past, ahead = (jnp.zeros((rows, 1), jnp.int32) for unused in range(3))
        label_row = jnp.zeros((1, rows), jnp.int32)
        end = jnp.int32(0)
        for j in range(spans.shape[1]):
            end = end + spans[b, j]
            label = label + jnp.where(t >= end, 1, 0)
            past = past + jnp.where(t - 1 >= end, 1, 0)
            ahead = ahead + jnp.where(t + 1 >= end, 1, 0)
            label_row = label_row + jnp.where(lane >= end, 1, 0)
        same = jnp.where(jnp.logical_and(label == past, t > 0), 1.0, 0.0)
        following = jnp.where(jnp.logical_and(label == ahead, t < rows - 1), 1.0, 0.0)
        valid = jnp.where(t < end, 1.0, 0.0)
        return label, label_row, same, following, valid

    masks = [row_masks(b) for b in range(buckets)]

    def mix(b, take, mean, rstd, gain_row, mix_row, outs):
        rs = bucket_rows(b)
        same = masks[b][2]
        total = jnp.zeros((rows, 1), F32)
        for j in range(4):
            total = total + jnp.sum(take(rs, j).astype(F32), axis=1, keepdims=True)
        average = total / width
        spread = jnp.zeros((rows, 1), F32)
        for j in range(4):
            centered = take(rs, j).astype(F32) - average
            spread = spread + jnp.sum(centered * centered, axis=1, keepdims=True)
        scale = lax.rsqrt(spread / width + EPSILON)
        mean[rs, :] = average
        rstd[rs, :] = scale
        for j in range(4):
            cols = slice(j * block, (j + 1) * block)
            normed = (take(rs, j).astype(F32) - average) * scale * order_vec[gain_row : gain_row + 1, cols]
            before = roll_rows(normed, 1) * same
            for i, out in enumerate(outs):
                weight = order_vec[mix_row + i : mix_row + i + 1, cols]
                out[rs, cols] = (normed * weight + before * (1.0 - weight)).astype(BF)

    def take_x(rs, j):
        return x_ref[rs, pl.ds(pl.multiple_of(order[j] * block, block), block)]

    def take_mid(rs, j):
        return mid[rs, j * block : (j + 1) * block]

    for b in range(buckets):
        mix(b, take_x, mean1, rstd1, OPENING, OPENING + 1, [acts.at[w] for w in range(4)])

    half_block = block // 2
    g_first = []
    for w in range(5):
        arrivals[w].wait_recv()
        g_first.append(relay_out(g.at[0, w], g.at[1, w], g.at[2, w]))

    def forward(copies, slot1, slot2, slot3):
        upper_half, lower_half = pl.ds(0, half_block), pl.ds(half_block, half_block)
        copies[0].wait_recv()
        one = links.push(slot1.at[upper_half], slot3.at[upper_half], y_peer)
        copies[1].wait_recv()
        return one, links.push(slot2.at[lower_half], slot3.at[lower_half], x_peer)

    g_second = [forward(g_first[w], g.at[1, w], g.at[2, w], g.at[3, w]) for w in range(4)]

    for w in range(4):
        for copy in g_second[w]:
            copy.wait_recv()
        for b in range(buckets):
            rs = bucket_rows(b)
            total = nn(acts[w, rs, 0:block], g[0, w])
            for j in range(1, 4):
                total = total + nn(acts[w, rs, j * block : (j + 1) * block], g[j, w])
            if w < 3:
                rkv[w, rs] = total.astype(BF)
            else:
                gate_raw[rs] = total
    g_second.append(forward(g_first[4], g.at[1, 4], g.at[2, 4], g.at[3, 4]))
    fk_second = forward(fk_first, fkb.at[0], fkb.at[1], fkb.at[2])

    low = lax.broadcasted_iota(jnp.int32, (rows, 128), 1) < LANE_WIDTH
    t_square = lax.broadcasted_iota(jnp.int32, (rows, rows), 0)
    s_square = lax.broadcasted_iota(jnp.int32, (rows, rows), 1)
    places = lax.broadcasted_iota(jnp.int32, (rows, 1), 0).astype(F32) - float(rows // 2)

    def decay_scales(cols):
        log_decay = -jnp.exp(head_vec[FADING : FADING + 1, cols])
        return jnp.exp(log_decay * places), jnp.exp(log_decay * (-1.0 - places))

    def allowed_pairs(b):
        return jnp.logical_and(s_square < t_square, masks[b][0] == masks[b][1])

    def scores_of(rt, kt, now, mine, allowed):
        scores = nt(jnp.where(mine, rt, 0.0).astype(BF), kt)
        here = jnp.sum(jnp.where(mine, now, 0.0), axis=1, keepdims=True)
        return jnp.where(allowed, scores, jnp.where(s_square == t_square, here, 0.0)).astype(BF)

    def time_forward(b):
        rs = bucket_rows(b)
        allowed = allowed_pairs(b)
        for p in range(pairs):
            cols = slice(p * 128, (p + 1) * 128)
            out_scale, in_scale = decay_scales(cols)
            r, k = rkv[0, rs, cols].astype(F32), rkv[1, rs, cols].astype(F32)
            v = rkv[2, rs, cols]
            rt, kt = r * out_scale, (k * in_scale).astype(BF)
            now = r * head_vec[REWARD : REWARD + 1, cols] * k
            first = nn(scores_of(rt, kt, now, low, allowed), v)
            second = nn(scores_of(rt, kt, now, jnp.logical_not(low), allowed), v)
            wkv = jnp.where(low, first, second)
            centered = wkv - head_sums(wkv, low) / LANE_WIDTH
            scale = lax.rsqrt(head_sums(centered * centered, low) / LANE_WIDTH + GROUP_EPSILON)
            n = centered * scale
            n_ref[rs, cols] = n
            n_scale[rs, cols] = scale
            gate = gate_raw[rs, cols]
            gained = n * head_vec[LANE : LANE + 1, cols] * gate * jax.nn.sigmoid(gate)
            mixed[rs, cols] = gained.astype(BF)

    pair_copies = {}

    def scatter_start(k, b, source, lanes):
        rs = pl.ds(b * rows, rows)
        return [
            links.push(source.at[rs, lanes(2 * other + 1 - c)], half.at[k, b, i], mate)
            for i, other in enumerate(chips_away + [z])
        ]

    def scatter_middle(k, b, source, lanes, first):
        rs = pl.ds(b * rows, rows)
        copies = []
        for i, other in enumerate(chips_away):
            if (b, i) in pair_copies:
                links.sent(pair_copies[b, i])
            first[i].wait_recv()
            value = source[rs, lanes(2 * other + c)].astype(F32) + half[k, b, i].astype(F32)
            pair[b, i] = value.astype(BF)
            copy = links.push(pair.at[b, i], far.at[k, b, i], (d, 2 * other + c))
            pair_copies[b, i] = copy
            copies.append(copy)
        return copies

    def scatter_end(k, b, source, lanes, first, second):
        rs = pl.ds(b * rows, rows)
        first[chips - 1].wait_recv()
        total = source[rs, lanes(m)].astype(F32) + half[k, b, chips - 1].astype(F32)
        for i, copy in enumerate(second):
            copy.wait_recv()
            total = total + far[k, b, i].astype(F32)
        return total

    def stats_start(k, b):
        return links.push(small.at[k, b, 0], small.at[k, b, 1], mate)

    def stats_middle(k, b, first):
        first.wait_recv()
        small[k, b, 2] = small[k, b, 0] + small[k, b, 1]
        return [
            links.push(small.at[k, b, 2], small.at[k, b, 3 + i], (d, 2 * other + c))
            for i, other in enumerate(chips_away)
        ]

    eye8 = jnp.where(lax.broadcasted_iota(jnp.int32, (16, 128), 0) == 0, 1.0, 0.0)
    eye16 = jnp.where(lax.broadcasted_iota(jnp.int32, (16, 128), 0) == 8, 1.0, 0.0)

    def stats_end(k, b, second):
        total = small[k, b, 2]
        for i, copy in enumerate(second):
            copy.wait_recv()
            total = total + small[k, b, 3 + i]
        total = total / width
        turn = lambda e: lax.dot_general(
            total, e, (((0,), (0,)), ((), ())), precision=lax.Precision.HIGHEST, preferred_element_type=F32
        )[:, 0:1]
        return turn(eye8), turn(eye16)

    def gather_start(source, target, lanes, rs):
        mine = target.at[rs, lanes(m)]
        copies = [links.push(source.at[rs], mine, (d, 2 * other + c)) for other in chips_away]
        copies.append(links.push(source.at[rs], mine, mate))
        target[rs, lanes(m)] = source[rs]
        return copies

    def gather_middle(target, lanes, rs, first):
        copies = []
        for i in range(chips - 1):
            source = 2 * lax.rem(z - (i + 1) + chips, chips) + c
            first[i].wait_recv()
            copies.append(links.push(target.at[rs, lanes(source)], target.at[rs, lanes(source)], mate))
        return copies

    def gather_end(first, second):
        first[-1].wait_recv()
        for copy in second:
            copy.wait_recv()

    both = (0, 1)
    slices = [pl.ds(b * rows, rows) for b in both]
    all_rows = pl.ds(0, buckets * rows)

    for copy in wo_arrivals:
        copy.wait_recv()
    first1 = []
    for b in both:
        time_forward(b)
        rs = bucket_rows(b)
        for j in range(4):
            cols = slice(j * block, (j + 1) * block)
            part[0, rs, cols] = nn(mixed[rs], wob[:, cols]).astype(BF)
        first1.append(scatter_start(0, b, part.at[0], own_lanes))
    fv_first = relay_out(fv, fvb.at[0], fvb.at[1])
    second1 = [scatter_middle(0, b, part.at[0], own_lanes, first1[b]) for b in both]
    gathers = []
    for b in both:
        rs = bucket_rows(b)
        total = scatter_end(0, b, part.at[0], own_lanes, first1[b], second1[b])
        middle = x_ref[rs, own_lanes(m)].astype(F32) + total
        mid_own[rs] = middle
        mid_own_b[rs] = middle.astype(BF)
        gathers.append(gather_start(mid_own_b, mid, moved_lanes, slices[b]))
    onward = [gather_middle(mid, moved_lanes, slices[b], gathers[b]) for b in both]
    for b in both:
        gather_end(gathers[b], onward[b])
        mix(b, take_mid, mean2, rstd2, CLOSING, CLOSING + 1, [kin, cri])
    for copy in g_second[4]:
        copy.wait_recv()

    def top(b):
        return seen[bucket_rows(b)].astype(F32) * masks[b][4]

    for b in both:
        rs = bucket_rows(b)
        total = nn(cri[rs, 0:block], g[0, 4])
        for j in range(1, 4):
            total = total + nn(cri[rs, j * block : (j + 1) * block], g[j, 4])
        gate = jax.nn.sigmoid(total)
        channel_gate[rs] = gate
        cg_own[rs] = (top(b) * gate).astype(BF)
    gathers = gather_start(cg_own, cg, moved_lanes, all_rows)
    for copy in fk_second:
        copy.wait_recv()

    def fk_piece(j):
        return fk if j == 0 else fkb.at[j - 1]

    def fv_piece(j):
        return fv if j == 0 else fvb.at[j - 1]

    for b in both:
        rs = bucket_rows(b)
        total = nn(kin[rs, 0:block], fk[...])
        for j in range(1, 4):
            total = total + nn(kin[rs, j * block : (j + 1) * block], fkb[j - 1])
        positive = jnp.maximum(total, 0.0)
        hid[rs] = (positive * positive).astype(BF)
        pos[rs] = positive.astype(BF)
    onward = gather_middle(cg, moved_lanes, all_rows, gathers)
    fv_second = forward(fv_first, fvb.at[0], fvb.at[1], fvb.at[2])
    gather_end(gathers, onward)

    piece = own

    def product_piece(lhs, rhs, i):
        return tn(lhs[:, i * piece : (i + 1) * piece], rhs[...])

    def ff_grad_start(k, lhs, rhs):
        for i, (way, slot) in ((2, (0, 0)), (6, (0, 1)), (5, (1, 0)), (7, (1, 1))):
            ff_send[k, way, slot] = product_piece(lhs, rhs, i).astype(BF)
        return (
            links.push(ff_send.at[k, 0], ff_got.at[k, 0], x_peer),
            links.push(ff_send.at[k, 1], ff_got.at[k, 1], y_peer),
        )

    def ff_grad_middle(k, lhs, rhs, first):
        first[0].wait_recv()
        links.sent(first[0])
        ff_send[k, 0, 0] = (product_piece(lhs, rhs, 4) + ff_got[k, 0, 1].astype(F32)).astype(BF)
        one = links.push(ff_send.at[k, 0, 0], ff_got2.at[k, 0], y_peer)
        first[1].wait_recv()
        links.sent(first[1])
        ff_send[k, 1, 0] = (product_piece(lhs, rhs, 3) + ff_got[k, 1, 1].astype(F32)).astype(BF)
        return one, links.push(ff_send.at[k, 1, 0], ff_got2.at[k, 1], x_peer)

    def ff_grad_end(k, lhs, rhs, second, out):
        for way in range(2):
            second[way].wait_recv()
            total = product_piece(lhs, rhs, way) + ff_got[k, way, 0].astype(F32) + ff_got2[k, way].astype(F32)
            out[way * piece : (way + 1) * piece] = total.astype(BF)

    tm_first, tm_second, back_copies = {}, {}, []

    def tm_lhs(w):
        return acts.at[w] if w < 4 else cri

    def tm_rhs(w):
        return time_grads.at[w] if w < 4 else gig

    def tm_grad_start(w):
        for i, (way, slot) in ((2, (0, 0)), (6, (0, 1)), (5, (1, 0)), (7, (1, 1))):
            tm_send[w, way, slot] = product_piece(tm_lhs(w), tm_rhs(w), i).astype(BF)
        tm_first[w] = (
            links.push(tm_send.at[w, 0], tm_got.at[w, 0], x_peer),
            links.push(tm_send.at[w, 1], tm_got.at[w, 1], y_peer),
        )

    def tm_grad_middle(w):
        copies = []
        for way, (i, peer) in enumerate(((4, y_peer), (3, x_peer))):
            value = product_piece(tm_lhs(w), tm_rhs(w), i)
            tm_first[w][way].wait_recv()
            links.sent(tm_first[w][way])
            tm_send[w, way, 0] = (value + tm_got[w, way, 1].astype(F32)).astype(BF)
            copies.append(links.push(tm_send.at[w, way, 0], tm_got2.at[w, way], peer))
        tm_second[w] = copies

    def tm_grad_end(w):
        links.sent(arrivals[w])
        sums = blocks.at[w] if w < 4 else channel_sum
        for way in range(2):
            value = product_piece(tm_lhs(w), tm_rhs(w), way)
            tm_second[w][way].wait_recv()
            value = value + tm_got[w, way, 0].astype(F32) + tm_got2[w, way].astype(F32)
            sums[4 * way : 4 * way + 4] = value.astype(BF).reshape(4, shard, own)
        back_copies.append(
            links.group(
                [sums.at[other] for other in others],
                [back_out.at[w, m]] * (parts - 1),
                [(d, other) for other in others],
                back_out.at[w, pl.ds(0, parts - 1)],
            )
        )
        back_out[w, m] = sums[m]

    fv_grad1 = ff_grad_start(0, cg, hid)

    for copy in fv_second:
        copy.wait_recv()
    first3 = []
    for b in both:
        rs = bucket_rows(b)
        for j in range(4):
            cols = slice(j * block, (j + 1) * block)
            part[1, rs, cols] = nt(hid[rs], fv_piece(j)[...]).astype(BF)
        first3.append(scatter_start(1, b, part.at[1], moved_lanes))
    second3 = []
    for b in both:
        rs = bucket_rows(b)
        total = nn(cg[rs, 0:block], fv[...])
        for j in range(1, 4):
            total = total + nn(cg[rs, j * block : (j + 1) * block], fvb[j - 1])
        pre[rs] = (total * 2.0 * pos[rs].astype(F32)).astype(BF)
        second3.append(scatter_middle(1, b, part.at[1], moved_lanes, first3[b]))
    fk_grad1 = ff_grad_start(1, kin, pre)
    sens[...] = jnp.zeros_like(sens)
    head_small[...] = jnp.zeros_like(head_small)
    gate_first = []
    out_first = []
    for b in both:
        rs = bucket_rows(b)
        gate = channel_gate[rs]
        total = scatter_end(1, b, part.at[1], moved_lanes, first3[b], second3[b])
        out_own[rs] = ((mid_own[rs] + gate * total) * masks[b][4]).astype(BF)
        gig[rs] = (top(b) * total * gate * (1.0 - gate)).astype(BF)
    tm_grad_start(4)

    ones = jnp.ones((8, own), BF)

    def back_mix(k, b, target, take, mean, rstd, gain_row, mix_row, sens_row, grads):
        rs = bucket_rows(b)
        same, following = masks[b][2], masks[b][3]
        average, scale = mean[rs, :], rstd[rs, :]
        one, two = jnp.zeros((8, rows), F32), jnp.zeros((8, rows), F32)
        for e in range(parts):
            cols = slice(e * own, (e + 1) * own)
            hat = (take(rs, e).astype(F32) - average) * scale
            gain = order_vec[gain_row : gain_row + 1, cols]
            normed = hat * gain
            change = normed - roll_rows(normed, 1) * same
            now = jnp.zeros((rows, own), F32)
            later = jnp.zeros((rows, own), F32)
            for i, (grad, weight_of) in enumerate(grads):
                value = nt(grad(rs), weight_of(e))
                at = slice(sens_row + i, sens_row + i + 1)
                sens[at, cols] += jnp.sum(value * change, axis=0, keepdims=True)
                weight = order_vec[mix_row + i : mix_row + i + 1, cols]
                now = now + value * weight
                later = later + value * (1.0 - weight)
            back = now + following * roll_rows(later, -1)
            target[rs, cols] = back.astype(BF)
            scaled = back * gain
            one = one + nt(ones, scaled.astype(BF))
            two = two + nt(ones, (scaled * hat).astype(BF))
        small[k, b, 0, 0:8] = one
        small[k, b, 0, 8:16] = two

    def piece_rows(e):
        return slice((e % 2) * own, (e % 2 + 1) * own)

    def take_mid_own(rs, e):
        return mid[rs, e * own : (e + 1) * own]

    def take_x_own(rs, e):
        start = pl.multiple_of(order[e // 2] * block + (e % 2) * own, own)
        return x_ref[rs, pl.ds(start, own)]

    def fk_rows(e):
        return fk_piece(e // 2)[piece_rows(e)]

    def g_rows(w):
        return lambda e: g[e // 2, w, piece_rows(e)]

    for copies in first1 + second1:
        for copy in copies:
            links.sent(copy)
    first4, stats4 = [], []
    for b in both:
        back_mix(
            0, b, part.at[0], take_mid_own, mean2, rstd2, CLOSING, CLOSING + 1, 4,
            [(lambda rs: pre[rs], fk_rows), (lambda rs: gig[rs], g_rows(4))],
        )
        first4.append(scatter_start(2, b, part.at[0], moved_lanes))
        stats4.append(stats_start(0, b))
    second4, stats4b = [], []
    for b in both:
        second4.append(scatter_middle(2, b, part.at[0], moved_lanes, first4[b]))
        stats4b.append(stats_middle(0, b, stats4[b]))
    fv_grad2 = ff_grad_middle(0, cg, hid, fv_grad1)

    def norm_back(b, back, hat, gain_row, rstd, means):
        gain = vec[gain_row : gain_row + 1, own_lanes(m)]
        return (back * gain - means[0] - hat * means[1]) * rstd[bucket_rows(b), :]

    closing = jnp.zeros((1, own), F32)
    gathers = []
    for b in both:
        rs = bucket_rows(b)
        back = scatter_end(2, b, part.at[0], moved_lanes, first4[b], second4[b])
        means = stats_end(0, b, stats4b[b])
        hat = (mid_own_b[rs].astype(F32) - mean2[rs, :]) * rstd2[rs, :]
        closing = closing + jnp.sum(back * hat, axis=0, keepdims=True)
        value = top(b) + norm_back(b, back, hat, CLOSING, rstd2, means)
        middle_grad[rs] = value
        branch_own[rs] = value.astype(BF)
        gathers.append(gather_start(branch_own, branch, own_lanes, slices[b]))
    onward = [gather_middle(branch, own_lanes, slices[b], gathers[b]) for b in both]
    fk_grad2 = ff_grad_middle(1, kin, pre, fk_grad1)

    def time_backward(b):
        rs = bucket_rows(b)
        allowed = allowed_pairs(b)
        for p in range(pairs):
            cols = slice(p * 128, (p + 1) * 128)
            out_scale, in_scale = decay_scales(cols)
            u, gn = head_vec[REWARD : REWARD + 1, cols], head_vec[LANE : LANE + 1, cols]
            g_in, gate, n = mixed_grad[rs, cols], gate_raw[rs, cols], n_ref[rs, cols]
            sg = jax.nn.sigmoid(gate)
            silu = gate * sg
            time_grads[3, rs, cols] = (g_in * n * gn * sg * (1.0 + gate * (1.0 - sg))).astype(BF)
            q = g_in * gn * silu
            dout = q - head_sums(q, low) / LANE_WIDTH - n * (head_sums(q * n, low) / LANE_WIDTH)
            dout = dout * n_scale[rs, cols]
            r, k = rkv[0, rs, cols].astype(F32), rkv[1, rs, cols].astype(F32)
            v = rkv[2, rs, cols]
            rt, kt = r * out_scale, (k * in_scale).astype(BF)
            rtb = rt.astype(BF)
            now = r * u * k
            diag = head_sums(dout * v.astype(F32), low)
            found = []
            for mine in (low, jnp.logical_not(low)):
                dmine = jnp.where(mine, dout, 0.0).astype(BF)
                scores = scores_of(rt, kt, now, mine, allowed)
                a = jnp.where(allowed, nt(dmine, v), 0.0).astype(BF)
                found.append((tn(scores, dmine), nn(a, kt), tn(a, rtb)))
            dv, drt, dkt = (jnp.where(low, one, two) for one, two in zip(*found))
            time_grads[0, rs, cols] = (drt * out_scale + u * k * diag).astype(BF)
            time_grads[1, rs, cols] = (dkt * in_scale + u * r * diag).astype(BF)
            time_grads[2, rs, cols] = dv.astype(BF)
            lags = places * rtb.astype(F32) * drt - (places + 1.0) * kt.astype(F32) * dkt
            log_decay = -jnp.exp(head_vec[FADING : FADING + 1, cols])
            head_small[0:1, cols] += jnp.sum(lags, axis=0, keepdims=True) * log_decay
            head_small[1:2, cols] += jnp.sum(r * k * diag, axis=0, keepdims=True)
            head_small[2:3, cols] += jnp.sum(g_in * n * silu, axis=0, keepdims=True)

    for copies in first3 + second3:
        for copy in copies:
            links.sent(copy)
    first6, stats6 = [], []
    for b in both:
        gather_end(gathers[b], onward[b])
        rs = bucket_rows(b)
        if b == 1:
            for j in range(4):
                wo_part[j] = tn(mixed[:, j * LANE_WIDTH : (j + 1) * LANE_WIDTH], branch[...]).astype(BF)
            wo_copies = [
                links.push(wo_part.at[peer[0]], wo_got.at[i], peer)
                for i, peer in enumerate((x_peer, y_peer, diagonal))
            ]
        mixed_grad[rs] = nt(branch[rs], wob[...])
        time_backward(b)
        back_mix(
            1, b, part.at[1], take_x_own, mean1, rstd1, OPENING, OPENING + 1, 0,
            [((lambda rs, w=w: time_grads[w, rs]), g_rows(w)) for w in range(4)],
        )
        first6.append(scatter_start(3, b, part.at[1], moved_lanes))
        stats6.append(stats_start(1, b))

    for w in (0, 1):
        tm_grad_start(w)
    second6, stats6b = [], []
    for b in both:
        second6.append(scatter_middle(3, b, part.at[1], moved_lanes, first6[b]))
        stats6b.append(stats_middle(1, b, stats6[b]))
    out_first = gather_start(out_own, out_full, own_lanes, all_rows)
    ff_grad_end(0, cg, hid, fv_grad2, ffv_out)
    tm_grad_middle(4)
    tm_grad_middle(0)
    tm_grad_start(2)
    out_second = gather_middle(out_full, own_lanes, all_rows, out_first)
    opening = jnp.zeros((1, own), F32)
    for b in both:
        rs = bucket_rows(b)
        back = scatter_end(3, b, part.at[1], moved_lanes, first6[b], second6[b])
        means = stats_end(1, b, stats6b[b])
        hat = (x_ref[rs, own_lanes(m)].astype(F32) - mean1[rs, :]) * rstd1[rs, :]
        opening = opening + jnp.sum(back * hat, axis=0, keepdims=True)
        value = middle_grad[rs] + norm_back(b, back, hat, OPENING, rstd1, means)
        gin_own[rs] = value.astype(BF)
    gin_first = gather_start(gin_own, gin_full, own_lanes, all_rows)
    tm_grad_middle(1)
    tm_grad_start(3)
    tm_grad_end(4)

    vec_copies = links.group(
        [sens.at[:, moved_lanes(other)] for other in others],
        [u_got.at[i] for i in range(parts - 1)],
        [(d, other) for other in others],
        u_got,
    )
    gin_second = gather_middle(gin_full, own_lanes, all_rows, gin_first)
    vec_copies.wait_recv()
    total = sens[:, moved_lanes(m)]
    for i in range(parts - 1):
        total = total + u_got[i]
    u2_own[0:8] = total
    u2_own[6:7] = opening
    u2_own[7:8] = closing
    u2_own[8:16] = head_small[...]
    dp_copies = links.group(
        [u2_own] * 3, [u2_got.at[i] for i in range(3)], [x_peer, y_peer, diagonal], u2_got
    )
    tm_grad_end(0)
    tm_grad_middle(2)
    tm_grad_end(1)
    tm_grad_middle(3)
    dp_copies.wait_recv()
    u3_own[...] = (u2_own[...] + u2_got[0]) + (u2_got[1] + u2_got[2])
    all_copies = links.group(
        [u3_own] * (parts - 1),
        [u3_got.at[m]] * (parts - 1),
        [(d, other) for other in others],
        u3_got.at[pl.ds(0, parts - 1)],
    )
    u3_got[m] = u3_own[...]

    ff_grad_end(1, kin, pre, fk_grad2, ffk_out)
    tm_grad_end(2)
    total = wo_part[d].astype(F32)
    for i, copy in enumerate(wo_copies):
        copy.wait_recv()
        total = total + wo_got[i].astype(F32)
    wo_out[...] = total.astype(BF)
    tm_grad_end(3)
    all_copies.wait_recv()
    upper_d = lax.rem(d, 2) == 1
    low_vec = lax.broadcasted_iota(jnp.int32, (8, 128), 1) < LANE_WIDTH
    for e in range(2):
        vec_out[0:8, e * own : (e + 1) * own] = u3_got[2 * d + e, 0:8]
    for u in range(4):
        lanes = pl.ds(pl.multiple_of(lax.div(d, 2) * 128, 128), 128)
        first, second = u3_got[2 * u, 8:16, lanes], u3_got[2 * u + 1, 8:16, lanes]
        first = jnp.where(upper_d, swap_halves(first), first)
        second = jnp.where(upper_d, second, swap_halves(second))
        vec_out[8:16, u * 128 : (u + 1) * 128] = jnp.where(low_vec, first, second)
    gather_end(gin_first, gin_second)
    gather_end(out_first, out_second)
    for copy in back_copies:
        copy.wait_recv()
    links.finish()
    assert links.used == COPIES, links.used


def finish_kernel(
    out, gin, ffk, ffv, back, wo, vec,
    out_o, gin_o, ffk_o, ffv_o, r_o, k_o, v_o, g_o, c_o, wo_o,
    y0, y1, y2, y3, y4, y5, y6, y7, y8, y9, y10,
    ffk_v, ffv_v, back_v, wo_v, ffk_f, ffv_f, square, read, write,
):
    buckets, rows = out_o.shape[:2]
    reads = [
        pltpu.make_async_copy(a, b, read.at[i])
        for i, (a, b) in enumerate(((ffv, ffv_v), (ffk, ffk_v), (wo, wo_v), (back, back_v)))
    ]
    for copy in reads:
        copy.start()
    writes = []

    def store(source, target):
        copy = pltpu.make_async_copy(source, target, write.at[len(writes)])
        copy.start()
        writes.append(copy)

    for source, target in ((out, out_o), (gin, gin_o)):
        for b in range(buckets):
            store(source.at[pl.ds(b * rows, rows)], target.at[b])
    for i, ref in enumerate((y0, y1, y2, y3, y4, y5, y6, y7, y8, y9, y10)):
        ref[...] = vec[i : i + 1]
    for copy, source, middle, target in zip(reads, (ffv_v, ffk_v, wo_v), (ffv_f, ffk_f, square.at[5]), (ffv_o, ffk_o, wo_o)):
        copy.wait()
        middle[...] = source[...].astype(F32)
        store(middle, target)
    reads[3].wait()
    parts, shard, own = back_v.shape[1:]
    low = lax.broadcasted_iota(jnp.int32, (shard, 128), 1) < LANE_WIDTH
    for to in range(parts):
        square[4, :, to * own : (to + 1) * own] = back_v[4, to].astype(F32)
    store(square.at[4], c_o)
    for w, target in enumerate((r_o, k_o, v_o, g_o)):
        for j in range(4):
            for u in range(4):
                lanes = slice((j // 2) * 128, (j // 2 + 1) * 128)
                first = back_v[w, 2 * u, :, lanes].astype(F32)
                second = back_v[w, 2 * u + 1, :, lanes].astype(F32)
                if j % 2 == 0:
                    tile = jnp.where(low, first, swap_halves(second))
                else:
                    tile = jnp.where(low, swap_halves(first), second)
                start = j * 4 * 128 + u * 128
                square[w, :, start : start + 128] = tile
        store(square.at[w], target)
    for copy in writes:
        copy.wait()


def fast_body(*args):
    (
        block_arguments, bundled_spans, opening_gain, mix_r, mix_k, mix_v, mix_g, w_recept, w_key, w_value, w_gate,
        fading, reward, lane_gain, w_out, closing_gain, mix_fk, mix_fr, fk, fv, w_channel, upstream,
    ) = args
    buckets, bucket_rows, width = block_arguments.shape
    rows = buckets * bucket_rows
    parts, chips = 8, 4
    own, block = width // parts, width // 4
    hidden = fk.shape[1]
    shard = w_out.shape[0]
    vectors = [
        opening_gain, mix_r, mix_k, mix_v, mix_g, closing_gain, mix_fk, mix_fr, fading, reward, lane_gain,
    ]
    vectors = [vector.reshape(1, width) for vector in vectors]
    v, sm = pltpu.VMEM, pltpu.SMEM
    vm = pl.BlockSpec(memory_space=pltpu.VMEM)
    half_block = block // 2
    scratch = [
        v((16, width), F32), v((4, parts, shard, own), BF), v((4, 5, block, own), BF), v((3, block, hidden), BF), v((3, block, hidden), BF),
        v((4 * shard, width), BF), v((4, rows, width), BF), v((rows, 1), F32), v((rows, 1), F32), v((rows, 1), F32),
        v((rows, 1), F32), v((16, width), F32), v((16, own), F32), v((rows, own), BF),
        v((3, rows, own), BF), v((rows, own), F32), v((rows, own), F32), v((rows, own), F32), v((rows, own), BF),
        v((2, rows, width), BF), v((4, buckets, chips, bucket_rows, own), BF),
        v((buckets, chips - 1, bucket_rows, own), BF), v((4, buckets, chips - 1, bucket_rows, own), BF),
        v((2, buckets, chips + 2, 16, bucket_rows), F32),
        v((rows, own), F32), v((rows, own), BF), v((rows, width), BF), v((rows, width), BF), v((rows, width), BF),
        v((rows, hidden), BF), v((rows, hidden), BF), v((rows, hidden), BF), v((rows, own), F32), v((rows, own), BF),
        v((rows, width), BF),
        v((rows, own), BF), v((rows, own), BF), v((rows, own), F32), v((rows, own), BF),
        v((rows, width), BF), v((rows, own), F32), v((4, rows, own), BF), v((8, width), F32), v((8, own), F32),
        v((2, 2, 2, own, hidden), BF), v((2, 2, 2, own, hidden), BF), v((2, 2, own, hidden), BF),
        v((5, 2, 2, own, own), BF), v((5, 2, 2, own, own), BF), v((5, 2, own, own), BF),
        v((parts, shard, own), BF),
        v((4, shard, width), BF), v((3, shard, width), BF), v((rows, own), BF),
        v((parts - 1, 8, own), F32), v((16, own), F32), v((3, 16, own), F32), v((16, own), F32),
        v((parts, 16, own), F32),
        pltpu.SemaphoreType.DMA((COPIES,)), pltpu.SemaphoreType.DMA((COPIES,)), pltpu.SemaphoreType.DMA,
    ]
    out = pl.pallas_call(
        block_kernel,
        out_shape=[
            struct((rows, width), BF), struct((rows, width), BF), struct((block, hidden), BF),
            struct((block, hidden), BF), struct((5, parts, shard, own), BF), struct((shard, width), BF),
            struct((16, block), F32),
        ],
        in_specs=[pl.BlockSpec(memory_space=sm), vm, pl.BlockSpec(memory_space=pl.ANY)] + [vm] * 19,
        out_specs=[vm] * 7,
        scratch_shapes=scratch,
        compiler_params=pltpu.CompilerParams(
            collective_id=0, has_side_effects=True, vmem_limit_bytes=VMEM_LIMIT
        ),
        name="whole_block",
    )(
        bundled_spans.reshape(buckets, -1), block_arguments.reshape(rows, width), upstream.reshape(rows, width), *vectors,
        w_recept, w_key, w_value, w_gate, w_out, w_channel, fk, fv,
    )
    square = struct((shard, width), F32)
    hbm = pl.BlockSpec(memory_space=pl.ANY)
    done = pl.pallas_call(
        finish_kernel,
        out_shape=[
            struct(block_arguments.shape, BF), struct(block_arguments.shape, BF), struct(fk.shape, F32),
            struct(fv.shape, F32), square, square, square, square, square, square,
        ]
        + [struct((1, block), F32)] * 11,
        in_specs=[hbm] * 6 + [vm],
        out_specs=[hbm] * 10 + [vm] * 11,
        scratch_shapes=[
            v(fk.shape, BF), v(fv.shape, BF), v((5, parts, shard, own), BF), v((shard, width), BF),
            v(fk.shape, F32), v(fv.shape, F32), v((6, shard, width), F32),
            pltpu.SemaphoreType.DMA((4,)), pltpu.SemaphoreType.DMA((2 * buckets + 8,)),
        ],
        compiler_params=pltpu.CompilerParams(vmem_limit_bytes=VMEM_LIMIT),
        name="finish",
    )(*out)
    outputs, grad_inputs, d_fk, d_fv, d_r, d_k, d_v, d_g, d_c, d_o = done[:10]
    small = [vector.reshape(block) for vector in done[10:]]
    return (
        outputs, grad_inputs, small[6], small[0], small[1], small[2], small[3], d_r, d_k, d_v, d_g,
        small[8], small[9], small[10], d_o, small[7], small[4], small[5], d_fk, d_fv, d_c,
    )


def body(*args):
    data_parts, parts = lax.axis_size("dp"), lax.axis_size("mp")
    width, shard, hidden = args[0].shape[2], args[7].shape[0], args[18].shape[1]
    fitted = (
        data_parts == 4
        and parts == 8
        and shard == LANE_WIDTH
        and width == 4 * parts * shard
        and hidden % 128 == 0
        and args[0].shape[:2] == (2, 128)
    )
    return fast_body(*args) if fitted else general_body(*args)


def solution(mesh):
    return jax.shard_map(
        body,
        mesh=mesh,
        in_specs=(
            P(None, "dp", None),
            P(None, "dp", None),
            P(),
            P(),
            P(),
            P(),
            P(),
            P(("dp", "mp"), None),
            P(("dp", "mp"), None),
            P(("dp", "mp"), None),
            P(("dp", "mp"), None),
            P(),
            P(),
            P(),
            P(("dp", "mp"), None),
            P(),
            P(),
            P(),
            P("dp", "mp"),
            P("dp", "mp"),
            P(("dp", "mp"), None),
            P(None, "dp", None),
        ),
        out_specs=(
            P(None, "dp", None),
            P(None, "dp", None),
            P("dp"),
            P("dp"),
            P("dp"),
            P("dp"),
            P("dp"),
            P(("dp", "mp"), None),
            P(("dp", "mp"), None),
            P(("dp", "mp"), None),
            P(("dp", "mp"), None),
            P("dp"),
            P("dp"),
            P("dp"),
            P(("dp", "mp"), None),
            P("dp"),
            P("dp"),
            P("dp"),
            P("dp", "mp"),
            P("dp", "mp"),
            P(("dp", "mp"), None),
        ),
        check_vma=False,
    )
```

```python
import functools
from functools import reduce

import jax
import jax.numpy as jnp
from jax import lax
from jax.experimental import pallas as pl
from jax.experimental.pallas import tpu as pltpu
from jax.sharding import PartitionSpec as P

LANE_WIDTH = 64
SPAN = 64


EPSILON = 1e-05
GROUP_EPSILON = 0.25
MIXED_MODE = lax.Precision.HIGH


def shortened(x):
    return jax.tree.map(lambda a: a.astype(jnp.bfloat16) if a.dtype == jnp.float32 else a, x)


def product(first_operand, second_operand):
    return jnp.dot(first_operand, second_operand, preferred_element_type=jnp.float32)


def product_rows(first_operand, second_operand):
    return lax.dot_general(
        first_operand, second_operand, (((0,), (0,)), ((), ())), preferred_element_type=jnp.float32
    )


def product_back(first_operand, second_operand):
    return lax.dot_general(
        first_operand, second_operand, (((1,), (1,)), ((), ())), preferred_element_type=jnp.float32
    )


def layer_norm(values, gain_entries):
    average = jnp.mean(values, axis=-1, keepdims=True)
    centered = values - average
    spread = jnp.mean(centered * centered, axis=-1, keepdims=True)
    return centered * lax.rsqrt(spread + EPSILON) * gain_entries


def group_norm(values, head_count):
    grouped = values.reshape(values.shape[0], head_count, -1)
    average = jnp.mean(grouped, axis=-1, keepdims=True)
    centered = grouped - average
    spread = jnp.mean(centered * centered, axis=-1, keepdims=True)
    return (centered * lax.rsqrt(spread + GROUP_EPSILON)).reshape(values.shape)


def segment_info(lengths, row_count):
    segment_ends = jnp.cumsum(lengths)
    places = jnp.arange(row_count, dtype=jnp.int32)
    sequence_label = jnp.sum((places[:, None] >= segment_ends[None, :]).astype(jnp.int32), axis=1)
    earlier = jnp.concatenate([jnp.full((1,), -1, jnp.int32), sequence_label[:-1]])
    common_series_filter = (sequence_label == earlier).astype(jnp.float32)
    valid_rows = (places < segment_ends[-1]).astype(jnp.float32)
    return (sequence_label, common_series_filter, valid_rows)


def shift_rows(values, common_series_filter):
    before = jnp.concatenate([jnp.zeros_like(values[:1]), values[:-1]], axis=0)
    return before * common_series_filter[:, None]


def iterative_renewal(
    accept_lines,
    lookup_weight_lines,
    payload_weight_lines,
    decay_logarithm,
    reward_scaler,
    sequence_label,
    layer_rows,
):
    row_count, head_count, head_width = accept_lines.shape
    block_count = row_count // layer_rows
    blocked = (block_count, layer_rows, head_count, head_width)
    accept_blocks = accept_lines.reshape(blocked)
    lookup_blocks = lookup_weight_lines.reshape(blocked)
    payload_blocks = payload_weight_lines.reshape(blocked)
    segment_blocks = sequence_label.reshape(block_count, layer_rows)
    positions = jnp.arange(layer_rows, dtype=jnp.float32)
    middle_step = float(layer_rows // 2)
    query_scale = jnp.exp(decay_logarithm[None] * (positions - middle_step)[:, None, None])
    key_scale = jnp.exp(decay_logarithm[None] * (middle_step - 1.0 - positions)[:, None, None])
    scores = jnp.einsum(
        "cthi,cshi->chts",
        accept_blocks * query_scale,
        lookup_blocks * key_scale,
        precision=MIXED_MODE,
    )
    causal = positions[:, None] > positions[None, :]
    within = segment_blocks[:, :, None] == segment_blocks[:, None, :]
    allowed = jnp.logical_and(causal[None], within).astype(jnp.float32)
    scores = scores * allowed[:, None]
    nested_routine = jnp.einsum("chts,cshj->cthj", scores, payload_blocks, precision=MIXED_MODE)
    reward_term = jnp.sum(accept_blocks * reward_scaler * lookup_blocks, axis=-1)
    nested_routine = nested_routine + reward_term[..., None] * payload_blocks
    last_segment = segment_blocks[:, -1]
    prior_segment = jnp.concatenate([jnp.full((1,), -1, jnp.int32), last_segment[:-1]])
    tail_scale = jnp.exp(decay_logarithm[None] * (layer_rows - 1.0 - positions)[:, None, None])
    tail_keep = (segment_blocks == last_segment[:, None]).astype(jnp.float32)
    added_state = jnp.einsum(
        "cshi,cshj->chij",
        lookup_blocks * tail_scale * tail_keep[:, :, None, None],
        payload_blocks,
        precision=MIXED_MODE,
    )
    carry_keep = (last_segment == prior_segment).astype(jnp.float32)
    whole_decay = jnp.exp(decay_logarithm * layer_rows)

    def advance(carry_state, piece_pair):
        addition, keep_flag = piece_pair
        return (whole_decay[:, :, None] * carry_state * keep_flag + addition, carry_state)

    initial = jnp.zeros((head_count, head_width, head_width), jnp.float32)
    unused, starts = lax.scan(advance, initial, (added_state, carry_keep))
    entry_keep = (segment_blocks == prior_segment[:, None]).astype(jnp.float32)
    entry_scale = jnp.exp(decay_logarithm[None] * positions[:, None, None])
    outside = jnp.einsum(
        "cthi,chij->cthj",
        accept_blocks * entry_scale * entry_keep[:, :, None, None],
        starts,
        precision=MIXED_MODE,
    )
    return (nested_routine + outside).reshape(row_count, head_count, head_width)


def add_terms(first_terms, second_terms):
    return jax.tree.map(jnp.add, first_terms, second_terms)


def general_body(
    block_arguments,
    bundled_spans,
    opening_normalize_scale,
    accept_lagmix,
    lookup_lagmix,
    payload_lagmix,
    valve_lagmix,
    accept_weights,
    lookup_weights,
    payload_weights,
    valve_weights,
    fading_speed_logs,
    present_reward,
    lane_normalize_scale,
    emission_weights,
    closing_normalize_scale,
    feedforward_lookup_lagmix,
    feedforward_accept_lagmix,
    feedforward_lookup_weights,
    feedforward_payload_weights,
    feedforward_accept_weights,
    upstream_sensitivity,
):
    micro_count, row_count, model_width = block_arguments.shape
    layer_rows = SPAN
    data_parts = lax.axis_size("dp")
    model_parts = lax.axis_size("mp")
    shard_rows = accept_weights.shape[0]
    model_place = lax.axis_index("mp")
    partition_lanes = model_width // LANE_WIDTH

    def own_columns(values):
        split_values = values.reshape(row_count, data_parts, model_parts, shard_rows)
        picked = lax.dynamic_index_in_dim(split_values, model_place, axis=2, keepdims=False)
        return picked.reshape(row_count, data_parts * shard_rows)

    outputs_list = []
    input_grads = []
    gradient_terms = []
    for micro_index in range(micro_count):
        projections = (
            lax.all_gather(accept_weights, ("dp", "mp"), axis=0, tiled=True),
            lax.all_gather(lookup_weights, ("dp", "mp"), axis=0, tiled=True),
            lax.all_gather(payload_weights, ("dp", "mp"), axis=0, tiled=True),
            lax.all_gather(valve_weights, ("dp", "mp"), axis=0, tiled=True),
            lax.all_gather(emission_weights, ("dp", "mp"), axis=0, tiled=True),
            lax.all_gather(feedforward_accept_weights, ("dp", "mp"), axis=0, tiled=True),
        )
        hidden_pair = (
            lax.all_gather(feedforward_lookup_weights, "dp", axis=0, tiled=True),
            lax.all_gather(feedforward_payload_weights, "dp", axis=0, tiled=True),
        )
        full_recept, full_key, full_value, full_gate, full_output, full_channel = projections
        hidden_key, hidden_value = hidden_pair
        sequence_label, common_series_filter, valid_rows = segment_info(
            bundled_spans[micro_index, 0], row_count
        )
        rows_float = block_arguments[micro_index].astype(jnp.float32)

        def front_part(rows_value, gain_entries, recept_mix, key_mix, value_mix, gate_mix):
            normed = layer_norm(rows_value, gain_entries)
            before = shift_rows(normed, common_series_filter)
            return tuple(
                (
                    normed * weight_mix + before * (1.0 - weight_mix)
                    for weight_mix in (recept_mix, key_mix, value_mix, gate_mix)
                )
            )

        front_values, front_pull = jax.vjp(
            front_part,
            rows_float,
            opening_normalize_scale,
            accept_lagmix,
            lookup_lagmix,
            payload_lagmix,
            valve_lagmix,
        )
        recept_in, key_in, value_in, gate_in = [
            front_piece.astype(jnp.bfloat16) for front_piece in front_values
        ]
        accept_lines = product(recept_in, full_recept).astype(jnp.bfloat16)
        lookup_weight_lines = product(key_in, full_key).astype(jnp.bfloat16)
        payload_weight_lines = product(value_in, full_value).astype(jnp.bfloat16)
        gate_raw = product(gate_in, full_gate)

        def middle_part(
            receptance_activation,
            key_value_product,
            value_activation,
            gate_activation,
            decay_parameter,
            reward_weight,
            gain_entries,
        ):
            decay_logarithm = -jnp.exp(decay_parameter).reshape(partition_lanes, -1)
            reward_scaler = reward_weight.reshape(partition_lanes, -1)
            reformed_array = (row_count, partition_lanes, model_width // partition_lanes)
            lane_answers = iterative_renewal(
                receptance_activation.reshape(reformed_array),
                key_value_product.reshape(reformed_array),
                value_activation.reshape(reformed_array),
                decay_logarithm,
                reward_scaler,
                sequence_label,
                layer_rows,
            )
            grouped = (
                group_norm(lane_answers.reshape(row_count, model_width), partition_lanes)
                * gain_entries
            )
            return grouped * jax.nn.silu(gate_activation)

        mixed_float, middle_pull = jax.vjp(
            middle_part,
            accept_lines.astype(jnp.float32),
            lookup_weight_lines.astype(jnp.float32),
            payload_weight_lines.astype(jnp.float32),
            gate_raw,
            fading_speed_logs,
            present_reward,
            lane_normalize_scale,
        )
        merged_lanes = mixed_float.astype(jnp.bfloat16)
        middle = rows_float + product(merged_lanes, full_output)

        def back_part(middle_value, gain_entries, key_mix, recept_mix):
            normed = layer_norm(middle_value, gain_entries)
            before = shift_rows(normed, common_series_filter)
            return (
                normed * key_mix + before * (1.0 - key_mix),
                normed * recept_mix + before * (1.0 - recept_mix),
            )

        channel_values, back_pull = jax.vjp(
            back_part,
            middle,
            closing_normalize_scale,
            feedforward_lookup_lagmix,
            feedforward_accept_lagmix,
        )
        channel_key_in = channel_values[0].astype(jnp.bfloat16)
        channel_recept_in = channel_values[1].astype(jnp.bfloat16)
        hidden_input = product(channel_key_in, hidden_key)
        hidden = jnp.square(jnp.maximum(hidden_input, 0.0)).astype(jnp.bfloat16)
        carried = lax.psum(product_back(hidden, hidden_value).astype(jnp.bfloat16), "mp").astype(
            jnp.float32
        )
        channel_gate = jax.nn.sigmoid(product(channel_recept_in, full_channel))
        outputs_list.append(
            ((middle + channel_gate * carried) * valid_rows[:, None]).astype(jnp.bfloat16)
        )
        top_grad = upstream_sensitivity[micro_index].astype(jnp.float32) * valid_rows[:, None]
        carried_grad = (top_grad * channel_gate).astype(jnp.bfloat16)
        gate_input_grad = (top_grad * carried * channel_gate * (1.0 - channel_gate)).astype(
            jnp.bfloat16
        )
        pre_grad = (
            product(carried_grad, hidden_value) * 2.0 * jnp.maximum(hidden_input, 0.0)
        ).astype(jnp.bfloat16)
        channel_key_grad = lax.psum(
            product_back(pre_grad, hidden_key).astype(jnp.bfloat16), "mp"
        ).astype(jnp.float32)
        channel_recept_grad = product_back(gate_input_grad, full_channel)
        middle_back, grad_second, feedforward_lookup_lagmix_sens, feedforward_accept_lagmix_sens = (
            back_pull((channel_key_grad, channel_recept_grad))
        )
        middle_grad = top_grad + middle_back
        branch_grad = middle_grad.astype(jnp.bfloat16)
        mixed_grad = product_back(branch_grad, full_output)
        output_term = product_rows(own_columns(merged_lanes), branch_grad)
        (
            receptance_single_precision,
            key_single_precision,
            value_single_precision,
            gate_single_precision,
            decay_gradient,
            reward_derivative,
            lane_normalize_derivative,
        ) = middle_pull(mixed_grad)
        recept_grad = receptance_single_precision.astype(jnp.bfloat16)
        key_grad = key_single_precision.astype(jnp.bfloat16)
        value_grad = value_single_precision.astype(jnp.bfloat16)
        gate_grad = gate_single_precision.astype(jnp.bfloat16)
        (
            line_derivatives,
            grad_first,
            grad_recept_mix,
            grad_key_mix,
            grad_value_mix,
            grad_gate_mix,
        ) = front_pull(
            (
                product_back(recept_grad, full_recept),
                product_back(key_grad, full_key),
                product_back(value_grad, full_value),
                product_back(gate_grad, full_gate),
            )
        )
        projection_terms = (
            product_rows(own_columns(recept_in), recept_grad),
            product_rows(own_columns(key_in), key_grad),
            product_rows(own_columns(value_in), value_grad),
            product_rows(own_columns(gate_in), gate_grad),
            output_term,
        )
        input_grads.append((middle_grad + line_derivatives).astype(jnp.bfloat16))
        local_terms = (
            grad_first,
            grad_recept_mix,
            grad_key_mix,
            grad_value_mix,
            grad_gate_mix,
            decay_gradient,
            reward_derivative,
            lane_normalize_derivative,
            grad_second,
            feedforward_lookup_lagmix_sens,
            feedforward_accept_lagmix_sens,
            product_rows(channel_key_in, pre_grad),
            product_rows(carried_grad, hidden),
            product_rows(own_columns(channel_recept_in), gate_input_grad),
        ) + projection_terms
        gradient_terms.append(local_terms)
    summed = reduce(add_terms, gradient_terms)
    summed = jax.tree.map(
        lambda part: part.astype(jnp.float32),
        lax.psum_scatter(shortened(summed), "dp", scatter_dimension=0, tiled=True),
    )
    (
        grad_first,
        grad_recept_mix,
        grad_key_mix,
        grad_value_mix,
        grad_gate_mix,
        decay_gradient,
        reward_derivative,
        lane_normalize_derivative,
        grad_second,
        feedforward_lookup_lagmix_sens,
        feedforward_accept_lagmix_sens,
        feedforward_lookup_derivative,
        feedforward_payload_derivative,
        feedforward_accept_derivative,
        grad_recept,
        grad_key,
        grad_value,
        grad_gate,
        grad_output,
    ) = summed
    return (
        jnp.stack(outputs_list),
        jnp.stack(input_grads),
        grad_first,
        grad_recept_mix,
        grad_key_mix,
        grad_value_mix,
        grad_gate_mix,
        grad_recept,
        grad_key,
        grad_value,
        grad_gate,
        decay_gradient,
        reward_derivative,
        lane_normalize_derivative,
        grad_output,
        grad_second,
        feedforward_lookup_lagmix_sens,
        feedforward_accept_lagmix_sens,
        feedforward_lookup_derivative,
        feedforward_payload_derivative,
        feedforward_accept_derivative,
    )


MESH = pl.DeviceIdType.MESH
BF = jnp.bfloat16
F32 = jnp.float32
VMEM_LIMIT = 63 << 20
OPENING, CLOSING, FADING, REWARD, LANE = 0, 5, 8, 9, 10


def struct(shape, dtype):
    return jax.ShapeDtypeStruct(shape, dtype)


def flip(place, other):
    low = lax.rem(lax.rem(place, 2) + lax.rem(other, 2), 2)
    high = lax.rem(lax.div(place, 2) + lax.div(other, 2), 2)
    return 2 * high + low


def nt(a, b):
    return lax.dot_general(a, b, (((1,), (1,)), ((), ())), preferred_element_type=F32)


def tn(a, b):
    return lax.dot_general(a, b, (((0,), (0,)), ((), ())), preferred_element_type=F32)


def nn(a, b):
    return lax.dot_general(a, b, (((1,), (0,)), ((), ())), preferred_element_type=F32)


def roll_rows(values, shift):
    return pltpu.roll(values, shift % values.shape[0], 0)


def swap_halves(tile):
    return pltpu.roll(tile, LANE_WIDTH, 1)


def head_sums(values, low):
    first = jnp.sum(jnp.where(low, values, 0.0), axis=1, keepdims=True)
    second = jnp.sum(jnp.where(low, 0.0, values), axis=1, keepdims=True)
    return jnp.where(low, first, second)


class Links:
    def __init__(self, send, recv):
        self.send, self.recv = send, recv
        self.used = 0
        self.open = []

    def push(self, source, target, peer):
        i = self.used
        self.used += 1
        copy = pltpu.make_async_remote_copy(
            source, target, self.send.at[i], self.recv.at[i], device_id=peer, device_id_type=MESH
        )
        copy.start()
        self.open.append(copy)
        return copy

    def group(self, sources, targets, peers, whole):
        i = self.used
        self.used += 1
        for source, target, peer in zip(sources, targets, peers):
            pltpu.make_async_remote_copy(
                source, target, self.send.at[i], self.recv.at[i], device_id=peer, device_id_type=MESH
            ).start()
        copy = pltpu.make_async_remote_copy(
            whole, whole, self.send.at[i], self.recv.at[i], device_id=peers[0], device_id_type=MESH
        )
        self.open.append(copy)
        return copy

    def sent(self, copy):
        if any(other is copy for other in self.open):
            copy.wait_send()
            self.open = [other for other in self.open if other is not copy]

    def finish(self):
        for copy in self.open:
            copy.wait_send()


COPIES = 204


def block_kernel(
    spans, x_ref, up_ref, v0, v1, v2, v3, v4, v5, v6, v7, v8, v9, v10, w_recept, w_key, w_value, w_gate, w_out, w_channel, fk, fv,
    out_full, gin_full, ffk_out, ffv_out, back_out, wo_out, vec_out,
    vec, blocks, g, fkb, fvb, wob, acts, mean1, rstd1, mean2, rstd2, order_vec, head_vec, seen,
    rkv, gate_raw, n_ref, n_scale, mixed, part, half, pair, far, small,
    mid_own, mid_own_b, mid, kin, cri, hid, pos, pre, channel_gate, cg_own, cg,
    out_own, gig, middle_grad, branch_own, branch, mixed_grad, time_grads, sens, head_small,
    ff_send, ff_got, ff_got2, tm_send, tm_got, tm_got2, channel_sum,
    wo_part, wo_got, wo_send, wo_got2, gin_own, u_got, u2_own, u2_got, u3_own, u3_got,
    send, recv, local,
):
    d, m = lax.axis_index("dp"), lax.axis_index("mp")
    z, c = lax.div(m, 2), lax.rem(m, 2)
    chips, parts = 4, 8
    buckets, rows = 2, x_ref.shape[0] // 2
    width = x_ref.shape[1]
    own = width // parts
    block = width // 4
    shard = w_out.shape[0]
    pairs = own // 128
    links = Links(send, recv)
    mate = (d, 2 * z + 1 - c)
    chips_away = [lax.rem(z + i, chips) for i in range(1, chips)]
    others = [lax.rem(m + i, parts) for i in range(1, parts)]
    x_peer = (d + 1 - 2 * lax.rem(d, 2), m)
    y_peer = (d + 2 - 4 * lax.div(d, 2), m)
    diagonal = (3 - d, m)
    order = [d, x_peer[0], y_peer[0], diagonal[0]]

    def own_lanes(owner):
        return pl.ds(pl.multiple_of(owner * own, own), own)

    def moved_lanes(owner):
        place = 2 * flip(lax.div(owner, 2), d) + lax.rem(owner, 2)
        return pl.ds(pl.multiple_of(place * own, own), own)

    def bucket_rows(b):
        return slice(b * rows, (b + 1) * rows)

    barrier = pltpu.get_barrier_semaphore()
    greeted = [(d, other) for other in others] + [x_peer, y_peer, diagonal]
    for peer in greeted:
        pl.semaphore_signal(barrier, inc=1, device_id=peer, device_id_type=MESH)
    top_copy = pltpu.make_async_copy(up_ref.at[:, own_lanes(m)], seen, local.at[0])
    top_copy.start()
    low16 = lax.broadcasted_iota(jnp.int32, (shard, 128), 1) < LANE_WIDTH
    vec[...] = jnp.zeros_like(vec)
    for i, ref in enumerate((v0, v1, v2, v3, v4, v5, v6, v7, v8, v9, v10)):
        vec[i : i + 1] = ref[...]

    def head_blocks(w, weight):
        for to in range(parts):
            for q in range(pairs):
                tiles = []
                for j in (2 * q, 2 * q + 1):
                    start = j * block + (to // 2) * 128
                    tiles.append(weight[:, start : start + 128].astype(F32))
                if to % 2 == 0:
                    tile = jnp.where(low16, tiles[0], swap_halves(tiles[1]))
                else:
                    tile = jnp.where(low16, swap_halves(tiles[0]), tiles[1])
                blocks[w, to, :, q * 128 : (q + 1) * 128] = tile.astype(BF)

    for w, weight in enumerate((w_recept, w_key, w_value, w_gate)):
        head_blocks(w, weight)
    pl.semaphore_wait(barrier, len(greeted))
    top_copy.wait()

    my_rows = pl.ds(pl.multiple_of(m * shard, shard), shard)

    def exchange(w):
        if w < 4:
            sources = [blocks.at[w, other] for other in others]
        else:
            sources = [w_channel.at[:, own_lanes(other)] for other in others]
        return links.group(
            sources,
            [g.at[0, w, my_rows]] * (parts - 1),
            [(d, other) for other in others],
            g.at[0, w, pl.ds(0, (parts - 1) * shard)],
        )

    half_block = block // 2
    upper_half, lower_half = pl.ds(0, half_block), pl.ds(half_block, half_block)

    def relay_out(source, slot1, slot2, which):
        return (
            links.push(source.at[which], slot1.at[which], x_peer),
            links.push(source.at[which], slot2.at[which], y_peer),
        )

    def forward(upper_copies, lower_copies, slot1, slot2, slot3):
        upper_copies[0].wait_recv()
        one = links.push(slot1.at[upper_half], slot3.at[upper_half], y_peer)
        lower_copies[1].wait_recv()
        two = links.push(slot2.at[lower_half], slot3.at[lower_half], x_peer)
        return (one, two) + (() if upper_copies is lower_copies else (upper_copies[1], lower_copies[0]))

    fk_upper = relay_out(fk, fkb.at[0], fkb.at[1], upper_half)
    arrivals = [exchange(w) for w in range(4)]
    arrivals.append(exchange(4))
    for w in range(4):
        g[0, w, my_rows] = blocks[w, m]
    g[0, 4, my_rows] = w_channel[:, own_lanes(m)]

    def out_rows(dp_place, start, size):
        return pl.ds(pl.multiple_of(dp_place * shard + start, 32), size)

    wo_first = [links.push(w_out, wob.at[out_rows(d, 0, shard)], peer) for peer in (x_peer, y_peer)]
    wob[out_rows(d, 0, shard)] = w_out[...]

    for j in range(4):
        order_vec[:, j * block : (j + 1) * block] = vec[
            :, pl.ds(pl.multiple_of(order[j] * block, block), block)
        ]
    low_row = lax.broadcasted_iota(jnp.int32, (16, 128), 1) < LANE_WIDTH
    upper = lax.rem(m, 2) == 1

    def head_tile(j):
        start = pl.multiple_of(j * block + lax.div(m, 2) * 128, 128)
        return vec[:, pl.ds(start, 128)]

    for q in range(pairs):
        first, second = head_tile(2 * q), head_tile(2 * q + 1)
        first = jnp.where(upper, swap_halves(first), first)
        second = jnp.where(upper, second, swap_halves(second))
        head_vec[:, q * 128 : (q + 1) * 128] = jnp.where(low_row, first, second)

    def row_masks(b):
        t = lax.broadcasted_iota(jnp.int32, (rows, 1), 0)
        lane = lax.broadcasted_iota(jnp.int32, (1, rows), 1)
        label, past, ahead = (jnp.zeros((rows, 1), jnp.int32) for unused in range(3))
        label_row = jnp.zeros((1, rows), jnp.int32)
        end = jnp.int32(0)
        for j in range(spans.shape[1]):
            end = end + spans[b, j]
            label = label + jnp.where(t >= end, 1, 0)
            past = past + jnp.where(t - 1 >= end, 1, 0)
            ahead = ahead + jnp.where(t + 1 >= end, 1, 0)
            label_row = label_row + jnp.where(lane >= end, 1, 0)
        same = jnp.where(jnp.logical_and(label == past, t > 0), 1.0, 0.0)
        following = jnp.where(jnp.logical_and(label == ahead, t < rows - 1), 1.0, 0.0)
        valid = jnp.where(t < end, 1.0, 0.0)
        return label, label_row, same, following, valid

    masks = [row_masks(b) for b in range(buckets)]

    def mix(b, take, mean, rstd, gain_row, mix_row, outs):
        rs = bucket_rows(b)
        same = masks[b][2]
        total = jnp.zeros((rows, 1), F32)
        for j in range(4):
            total = total + jnp.sum(take(rs, j).astype(F32), axis=1, keepdims=True)
        average = total / width
        spread = jnp.zeros((rows, 1), F32)
        for j in range(4):
            centered = take(rs, j).astype(F32) - average
            spread = spread + jnp.sum(centered * centered, axis=1, keepdims=True)
        scale = lax.rsqrt(spread / width + EPSILON)
        mean[rs, :] = average
        rstd[rs, :] = scale
        for j in range(4):
            cols = slice(j * block, (j + 1) * block)
            normed = (take(rs, j).astype(F32) - average) * scale * order_vec[gain_row : gain_row + 1, cols]
            before = roll_rows(normed, 1) * same
            change = normed - before
            for i, out in enumerate(outs):
                weight = order_vec[mix_row + i : mix_row + i + 1, cols]
                out[rs, cols] = (before + change * weight).astype(BF)

    def take_x(rs, j):
        return x_ref[rs, pl.ds(pl.multiple_of(order[j] * block, block), block)]

    def take_mid(rs, j):
        return mid[rs, j * block : (j + 1) * block]

    for b in range(buckets):
        mix(b, take_x, mean1, rstd1, OPENING, OPENING + 1, [acts.at[w] for w in range(4)])

    g_first = []
    everything = pl.ds(0, block)
    for w in range(4):
        arrivals[w].wait_recv()
        g_first.append(relay_out(g.at[0, w], g.at[1, w], g.at[2, w], everything))
    g_second = [forward(g_first[w], g_first[w], g.at[1, w], g.at[2, w], g.at[3, w]) for w in range(4)]
    wo_first[0].wait_recv()
    wo_rows = out_rows(x_peer[0], 0, shard // 2)
    wo_second = [links.push(wob.at[wo_rows], wob.at[wo_rows], y_peer)]
    wo_first[1].wait_recv()
    wo_rows = out_rows(y_peer[0], shard // 2, shard // 2)
    wo_second.append(links.push(wob.at[wo_rows], wob.at[wo_rows], x_peer))
    fk_lower = relay_out(fk, fkb.at[0], fkb.at[1], lower_half)
    arrivals[4].wait_recv()
    g_first.append(relay_out(g.at[0, 4], g.at[1, 4], g.at[2, 4], everything))

    for w in range(4):
        for copy in g_second[w]:
            copy.wait_recv()
        for b in range(buckets):
            rs = bucket_rows(b)
            total = nn(acts[w, rs, 0:block], g[0, w])
            for j in range(1, 4):
                total = total + nn(acts[w, rs, j * block : (j + 1) * block], g[j, w])
            if w < 3:
                rkv[w, rs] = total.astype(BF)
            else:
                gate_raw[rs] = total
    fv_upper = relay_out(fv, fvb.at[0], fvb.at[1], upper_half)

    low = lax.broadcasted_iota(jnp.int32, (rows, 128), 1) < LANE_WIDTH
    t_square = lax.broadcasted_iota(jnp.int32, (rows, rows), 0)
    s_square = lax.broadcasted_iota(jnp.int32, (rows, rows), 1)
    places = lax.broadcasted_iota(jnp.int32, (rows, 1), 0).astype(F32) - float(rows // 2)

    def decay_scales(cols):
        log_decay = -jnp.exp(head_vec[FADING : FADING + 1, cols])
        return jnp.exp(log_decay * places), jnp.exp(log_decay * (-1.0 - places))

    def allowed_pairs(b):
        return jnp.logical_and(s_square < t_square, masks[b][0] == masks[b][1])

    def scores_of(rt, kt, now, mine, allowed):
        scores = nt(jnp.where(mine, rt, 0.0).astype(BF), kt)
        here = jnp.sum(jnp.where(mine, now, 0.0), axis=1, keepdims=True)
        return jnp.where(allowed, scores, jnp.where(s_square == t_square, here, 0.0)).astype(BF)

    def time_forward(b):
        rs = bucket_rows(b)
        allowed = allowed_pairs(b)
        for p in range(pairs):
            cols = slice(p * 128, (p + 1) * 128)
            out_scale, in_scale = decay_scales(cols)
            r, k = rkv[0, rs, cols].astype(F32), rkv[1, rs, cols].astype(F32)
            v = rkv[2, rs, cols]
            rt, kt = r * out_scale, (k * in_scale).astype(BF)
            now = r * head_vec[REWARD : REWARD + 1, cols] * k
            first = nn(scores_of(rt, kt, now, low, allowed), v)
            second = nn(scores_of(rt, kt, now, jnp.logical_not(low), allowed), v)
            wkv = jnp.where(low, first, second)
            centered = wkv - head_sums(wkv, low) / LANE_WIDTH
            scale = lax.rsqrt(head_sums(centered * centered, low) / LANE_WIDTH + GROUP_EPSILON)
            n = centered * scale
            n_ref[rs, cols] = n
            n_scale[rs, cols] = scale
            gate = gate_raw[rs, cols]
            gained = n * head_vec[LANE : LANE + 1, cols] * gate * jax.nn.sigmoid(gate)
            mixed[rs, cols] = gained.astype(BF)

    pair_copies = {}
    own_copies = []

    def scatter_start(k, b, source, lanes):
        rs = pl.ds(b * rows, rows)
        return [
            links.push(source.at[rs, lanes(2 * other + 1 - c)], half.at[k, b, i], mate)
            for i, other in enumerate(chips_away + [z])
        ]

    def scatter_middle(k, b, source, lanes, first):
        rs = pl.ds(b * rows, rows)
        copies = []
        for i, other in enumerate(chips_away):
            if (b, i) in pair_copies:
                links.sent(pair_copies[b, i])
            first[i].wait_recv()
            value = source[rs, lanes(2 * other + c)].astype(F32) + half[k, b, i].astype(F32)
            pair[b, i] = value.astype(BF)
            copy = links.push(pair.at[b, i], far.at[k, b, i], (d, 2 * other + c))
            pair_copies[b, i] = copy
            copies.append(copy)
        return copies

    def scatter_end(k, b, source, lanes, first, second):
        rs = pl.ds(b * rows, rows)
        first[chips - 1].wait_recv()
        total = source[rs, lanes(m)].astype(F32) + half[k, b, chips - 1].astype(F32)
        for i, copy in enumerate(second):
            copy.wait_recv()
            total = total + far[k, b, i].astype(F32)
        return total

    def stats_start(k, b):
        return links.push(small.at[k, b, 0], small.at[k, b, 1], mate)

    def stats_middle(k, b, first):
        first.wait_recv()
        small[k, b, 2] = small[k, b, 0] + small[k, b, 1]
        return [
            links.push(small.at[k, b, 2], small.at[k, b, 3 + i], (d, 2 * other + c))
            for i, other in enumerate(chips_away)
        ]

    eye8 = jnp.where(lax.broadcasted_iota(jnp.int32, (16, 128), 0) == 0, 1.0, 0.0)
    eye16 = jnp.where(lax.broadcasted_iota(jnp.int32, (16, 128), 0) == 8, 1.0, 0.0)

    def stats_end(k, b, second):
        total = small[k, b, 2]
        for i, copy in enumerate(second):
            copy.wait_recv()
            total = total + small[k, b, 3 + i]
        total = total / width
        turn = lambda e: lax.dot_general(
            total, e, (((0,), (0,)), ((), ())), precision=lax.Precision.HIGHEST, preferred_element_type=F32
        )[:, 0:1]
        return turn(eye8), turn(eye16)

    def gather_start(source, target, lanes, rs, keep=None):
        mine = target.at[rs, lanes(m)]
        copies = [links.push(source.at[rs], mine, (d, 2 * other + c)) for other in chips_away]
        copies.append(links.push(source.at[rs], mine, mate))
        if keep is None:
            target[rs, lanes(m)] = source[rs]
        else:
            own_copies.append(pltpu.make_async_copy(source.at[rs], mine, local.at[keep]))
            own_copies[-1].start()
        return copies

    def gather_middle(target, lanes, rs, first):
        copies = []
        for i in range(chips - 1):
            source = 2 * lax.rem(z - (i + 1) + chips, chips) + c
            first[i].wait_recv()
            copies.append(links.push(target.at[rs, lanes(source)], target.at[rs, lanes(source)], mate))
        return copies

    def gather_end(first, second):
        first[-1].wait_recv()
        for copy in second:
            copy.wait_recv()

    both = (0, 1)
    slices = [pl.ds(b * rows, rows) for b in both]
    all_rows = pl.ds(0, buckets * rows)

    for copy in wo_second:
        copy.wait_recv()
    first1 = []
    for b in both:
        time_forward(b)
        rs = bucket_rows(b)
        for j in range(4):
            cols = slice(j * block, (j + 1) * block)
            part[0, rs, cols] = nn(mixed[rs], wob[:, cols]).astype(BF)
        first1.append(scatter_start(0, b, part.at[0], own_lanes))
    g_second.append(forward(g_first[4], g_first[4], g.at[1, 4], g.at[2, 4], g.at[3, 4]))
    fk_second = forward(fk_upper, fk_lower, fkb.at[0], fkb.at[1], fkb.at[2])
    fv_lower = relay_out(fv, fvb.at[0], fvb.at[1], lower_half)
    second1 = [scatter_middle(0, b, part.at[0], own_lanes, first1[b]) for b in both]
    gathers = []
    for b in both:
        rs = bucket_rows(b)
        total = scatter_end(0, b, part.at[0], own_lanes, first1[b], second1[b])
        middle = x_ref[rs, own_lanes(m)].astype(F32) + total
        mid_own[rs] = middle
        mid_own_b[rs] = middle.astype(BF)
        gathers.append(gather_start(mid_own_b, mid, moved_lanes, slices[b]))
    onward = [gather_middle(mid, moved_lanes, slices[b], gathers[b]) for b in both]
    for b in both:
        gather_end(gathers[b], onward[b])
        mix(b, take_mid, mean2, rstd2, CLOSING, CLOSING + 1, [kin, cri])
    for copy in g_second[4]:
        copy.wait_recv()

    def top(b):
        return seen[bucket_rows(b)].astype(F32) * masks[b][4]

    for b in both:
        rs = bucket_rows(b)
        total = nn(cri[rs, 0:block], g[0, 4])
        for j in range(1, 4):
            total = total + nn(cri[rs, j * block : (j + 1) * block], g[j, 4])
        gate = jax.nn.sigmoid(total)
        channel_gate[rs] = gate
        cg_own[rs] = (top(b) * gate).astype(BF)
    gathers = gather_start(cg_own, cg, moved_lanes, all_rows)
    for copy in fk_second:
        copy.wait_recv()

    def fk_piece(j):
        return fk if j == 0 else fkb.at[j - 1]

    def fv_piece(j):
        return fv if j == 0 else fvb.at[j - 1]

    for b in both:
        rs = bucket_rows(b)
        total = nn(kin[rs, 0:block], fk[...])
        for j in range(1, 4):
            total = total + nn(kin[rs, j * block : (j + 1) * block], fkb[j - 1])
        positive = jnp.maximum(total, 0.0)
        hid[rs] = (positive * positive).astype(BF)
        pos[rs] = positive.astype(BF)
    onward = gather_middle(cg, moved_lanes, all_rows, gathers)
    fv_second = forward(fv_upper, fv_lower, fvb.at[0], fvb.at[1], fvb.at[2])
    gather_end(gathers, onward)

    piece = own

    def product_piece(lhs, rhs, i):
        return tn(lhs[:, i * piece : (i + 1) * piece], rhs[...])

    def ff_grad_start(k, lhs, rhs):
        for i, (way, slot) in ((2, (0, 0)), (6, (0, 1)), (5, (1, 0)), (7, (1, 1))):
            ff_send[k, way, slot] = product_piece(lhs, rhs, i).astype(BF)
        return (
            links.push(ff_send.at[k, 0], ff_got.at[k, 0], x_peer),
            links.push(ff_send.at[k, 1], ff_got.at[k, 1], y_peer),
        )

    def ff_grad_middle(k, lhs, rhs, first):
        first[0].wait_recv()
        links.sent(first[0])
        ff_send[k, 0, 0] = (product_piece(lhs, rhs, 4) + ff_got[k, 0, 1].astype(F32)).astype(BF)
        one = links.push(ff_send.at[k, 0, 0], ff_got2.at[k, 0], y_peer)
        first[1].wait_recv()
        links.sent(first[1])
        ff_send[k, 1, 0] = (product_piece(lhs, rhs, 3) + ff_got[k, 1, 1].astype(F32)).astype(BF)
        return one, links.push(ff_send.at[k, 1, 0], ff_got2.at[k, 1], x_peer)

    def ff_grad_end(k, lhs, rhs, second, out):
        for way in range(2):
            second[way].wait_recv()
            total = product_piece(lhs, rhs, way) + ff_got[k, way, 0].astype(F32) + ff_got2[k, way].astype(F32)
            ff_send[k, way, 1] = total.astype(BF)
            own_copies.append(
                pltpu.make_async_copy(
                    ff_send.at[k, way, 1], out.at[pl.ds(way * piece, piece)], local.at[1 + 2 * k + way]
                )
            )
            own_copies[-1].start()

    tm_first, tm_second, back_copies = {}, {}, []

    def tm_lhs(w):
        return acts.at[w] if w < 4 else cri

    def tm_rhs(w):
        return time_grads.at[w] if w < 4 else gig

    def tm_grad_start(w):
        for i, (way, slot) in ((2, (0, 0)), (6, (0, 1)), (5, (1, 0)), (7, (1, 1))):
            tm_send[w, way, slot] = product_piece(tm_lhs(w), tm_rhs(w), i).astype(BF)
        tm_first[w] = (
            links.push(tm_send.at[w, 0], tm_got.at[w, 0], x_peer),
            links.push(tm_send.at[w, 1], tm_got.at[w, 1], y_peer),
        )

    def tm_grad_middle(w):
        copies = []
        for way, (i, peer) in enumerate(((4, y_peer), (3, x_peer))):
            value = product_piece(tm_lhs(w), tm_rhs(w), i)
            tm_first[w][way].wait_recv()
            links.sent(tm_first[w][way])
            tm_send[w, way, 0] = (value + tm_got[w, way, 1].astype(F32)).astype(BF)
            copies.append(links.push(tm_send.at[w, way, 0], tm_got2.at[w, way], peer))
        tm_second[w] = copies

    def tm_grad_end(w):
        links.sent(arrivals[w])
        sums = blocks.at[w] if w < 4 else channel_sum
        for way in range(2):
            value = product_piece(tm_lhs(w), tm_rhs(w), way)
            tm_second[w][way].wait_recv()
            value = value + tm_got[w, way, 0].astype(F32) + tm_got2[w, way].astype(F32)
            sums[4 * way : 4 * way + 4] = value.astype(BF).reshape(4, shard, own)
        back_copies.append(
            links.group(
                [sums.at[other] for other in others],
                [back_out.at[w, m]] * (parts - 1),
                [(d, other) for other in others],
                back_out.at[w, pl.ds(0, parts - 1)],
            )
        )
        own_copies.append(pltpu.make_async_copy(sums.at[m], back_out.at[w, m], local.at[5 + w]))
        own_copies[-1].start()

    fv_grad1 = ff_grad_start(0, cg, hid)

    for copy in fv_second:
        copy.wait_recv()
    first3 = []
    for b in both:
        rs = bucket_rows(b)
        for j in range(4):
            cols = slice(j * block, (j + 1) * block)
            part[1, rs, cols] = nt(hid[rs], fv_piece(j)[...]).astype(BF)
        first3.append(scatter_start(1, b, part.at[1], moved_lanes))
    second3 = []
    for b in both:
        rs = bucket_rows(b)
        total = nn(cg[rs, 0:block], fv[...])
        for j in range(1, 4):
            total = total + nn(cg[rs, j * block : (j + 1) * block], fvb[j - 1])
        pre[rs] = (total * 2.0 * pos[rs].astype(F32)).astype(BF)
        second3.append(scatter_middle(1, b, part.at[1], moved_lanes, first3[b]))
    fk_grad1 = ff_grad_start(1, kin, pre)
    sens[...] = jnp.zeros_like(sens)
    head_small[...] = jnp.zeros_like(head_small)
    gate_first = []
    for b in both:
        rs = bucket_rows(b)
        gate = channel_gate[rs]
        total = scatter_end(1, b, part.at[1], moved_lanes, first3[b], second3[b])
        out_own[rs] = ((mid_own[rs] + gate * total) * masks[b][4]).astype(BF)
        gig[rs] = (top(b) * total * gate * (1.0 - gate)).astype(BF)
    tm_grad_start(4)

    ones = jnp.ones((8, own), BF)

    def back_mix(k, b, target, take, mean, rstd, gain_row, mix_row, sens_row, grads):
        rs = bucket_rows(b)
        same, following = masks[b][2], masks[b][3]
        average, scale = mean[rs, :], rstd[rs, :]
        one, two = jnp.zeros((8, rows), F32), jnp.zeros((8, rows), F32)
        for e in range(parts):
            cols = slice(e * own, (e + 1) * own)
            hat = (take(rs, e).astype(F32) - average) * scale
            gain = order_vec[gain_row : gain_row + 1, cols]
            normed = hat * gain
            change = normed - roll_rows(normed, 1) * same
            now = jnp.zeros((rows, own), F32)
            whole = jnp.zeros((rows, own), F32)
            for i, (grad, weight_of) in enumerate(grads):
                value = nt(grad(rs), weight_of(e))
                at = slice(sens_row + i, sens_row + i + 1)
                sens[at, cols] += jnp.sum(value * change, axis=0, keepdims=True)
                weight = order_vec[mix_row + i : mix_row + i + 1, cols]
                now = now + value * weight
                whole = whole + value
            back = now + following * roll_rows(whole - now, -1)
            target[rs, cols] = back.astype(BF)
            scaled = back * gain
            one = one + nt(ones, scaled.astype(BF))
            two = two + nt(ones, (scaled * hat).astype(BF))
        small[k, b, 0, 0:8] = one
        small[k, b, 0, 8:16] = two

    def piece_rows(e):
        return slice((e % 2) * own, (e % 2 + 1) * own)

    def take_mid_own(rs, e):
        return mid[rs, e * own : (e + 1) * own]

    def take_x_own(rs, e):
        start = pl.multiple_of(order[e // 2] * block + (e % 2) * own, own)
        return x_ref[rs, pl.ds(start, own)]

    def fk_rows(e):
        return fk_piece(e // 2)[piece_rows(e)]

    def g_rows(w):
        return lambda e: g[e // 2, w, piece_rows(e)]

    for copies in first1 + second1:
        for copy in copies:
            links.sent(copy)
    first4, stats4 = [], []
    for b in both:
        back_mix(
            0, b, part.at[0], take_mid_own, mean2, rstd2, CLOSING, CLOSING + 1, 4,
            [(lambda rs: pre[rs], fk_rows), (lambda rs: gig[rs], g_rows(4))],
        )
        first4.append(scatter_start(2, b, part.at[0], moved_lanes))
        stats4.append(stats_start(0, b))
    second4, stats4b = [], []
    for b in both:
        second4.append(scatter_middle(2, b, part.at[0], moved_lanes, first4[b]))
        stats4b.append(stats_middle(0, b, stats4[b]))
    fv_grad2 = ff_grad_middle(0, cg, hid, fv_grad1)

    def norm_back(b, back, hat, gain_row, rstd, means):
        gain = vec[gain_row : gain_row + 1, own_lanes(m)]
        return (back * gain - means[0] - hat * means[1]) * rstd[bucket_rows(b), :]

    closing = jnp.zeros((1, own), F32)
    gathers = []
    for b in both:
        rs = bucket_rows(b)
        back = scatter_end(2, b, part.at[0], moved_lanes, first4[b], second4[b])
        means = stats_end(0, b, stats4b[b])
        hat = (mid_own_b[rs].astype(F32) - mean2[rs, :]) * rstd2[rs, :]
        closing = closing + jnp.sum(back * hat, axis=0, keepdims=True)
        value = top(b) + norm_back(b, back, hat, CLOSING, rstd2, means)
        middle_grad[rs] = value
        branch_own[rs] = value.astype(BF)
        gathers.append(gather_start(branch_own, branch, own_lanes, slices[b]))
    onward = [gather_middle(branch, own_lanes, slices[b], gathers[b]) for b in both]
    fk_grad2 = ff_grad_middle(1, kin, pre, fk_grad1)

    def time_backward(b):
        rs = bucket_rows(b)
        allowed = allowed_pairs(b)
        for p in range(pairs):
            cols = slice(p * 128, (p + 1) * 128)
            out_scale, in_scale = decay_scales(cols)
            u, gn = head_vec[REWARD : REWARD + 1, cols], head_vec[LANE : LANE + 1, cols]
            g_in, gate, n = mixed_grad[rs, cols], gate_raw[rs, cols], n_ref[rs, cols]
            sg = jax.nn.sigmoid(gate)
            silu = gate * sg
            time_grads[3, rs, cols] = (g_in * n * gn * sg * (1.0 + gate * (1.0 - sg))).astype(BF)
            q = g_in * gn * silu
            dout = q - head_sums(q, low) / LANE_WIDTH - n * (head_sums(q * n, low) / LANE_WIDTH)
            dout = dout * n_scale[rs, cols]
            r, k = rkv[0, rs, cols].astype(F32), rkv[1, rs, cols].astype(F32)
            v = rkv[2, rs, cols]
            rt, kt = r * out_scale, (k * in_scale).astype(BF)
            rtb = rt.astype(BF)
            now = r * u * k
            diag = head_sums(dout * v.astype(F32), low)
            found = []
            for mine in (low, jnp.logical_not(low)):
                dmine = jnp.where(mine, dout, 0.0).astype(BF)
                scores = scores_of(rt, kt, now, mine, allowed)
                a = jnp.where(allowed, nt(dmine, v), 0.0).astype(BF)
                found.append((tn(scores, dmine), nn(a, kt), tn(a, rtb)))
            dv, drt, dkt = (jnp.where(low, one, two) for one, two in zip(*found))
            time_grads[0, rs, cols] = (drt * out_scale + u * k * diag).astype(BF)
            time_grads[1, rs, cols] = (dkt * in_scale + u * r * diag).astype(BF)
            time_grads[2, rs, cols] = dv.astype(BF)
            lags = places * rtb.astype(F32) * drt - (places + 1.0) * kt.astype(F32) * dkt
            log_decay = -jnp.exp(head_vec[FADING : FADING + 1, cols])
            head_small[0:1, cols] += jnp.sum(lags, axis=0, keepdims=True) * log_decay
            head_small[1:2, cols] += jnp.sum(r * k * diag, axis=0, keepdims=True)
            head_small[2:3, cols] += jnp.sum(g_in * n * silu, axis=0, keepdims=True)

    for copies in first3 + second3:
        for copy in copies:
            links.sent(copy)
    left, right = pl.ds(0, width // 2), pl.ds(width // 2, width // 2)
    first6, stats6 = [], []
    for b in both:
        gather_end(gathers[b], onward[b])
        rs = bucket_rows(b)
        if b == 1:
            for j in range(4):
                wo_part[j] = tn(mixed[:, j * LANE_WIDTH : (j + 1) * LANE_WIDTH], branch[...]).astype(BF)
            wo_first = [
                links.push(wo_part.at[peer[0], :, lanes], wo_got.at[way, i], way_peer)
                for way, lanes, way_peer, near in ((0, left, x_peer, x_peer), (1, right, y_peer, y_peer))
                for i, peer in enumerate((near, diagonal))
            ]
            out_first = gather_start(out_own, out_full, own_lanes, all_rows, keep=11)
        mixed_grad[rs] = nt(branch[rs], wob[...])
        time_backward(b)
        back_mix(
            1, b, part.at[1], take_x_own, mean1, rstd1, OPENING, OPENING + 1, 0,
            [((lambda rs, w=w: time_grads[w, rs]), g_rows(w)) for w in range(4)],
        )
        first6.append(scatter_start(3, b, part.at[1], moved_lanes))
        stats6.append(stats_start(1, b))

    for w in (0, 1):
        tm_grad_start(w)
    second6, stats6b = [], []
    for b in both:
        second6.append(scatter_middle(3, b, part.at[1], moved_lanes, first6[b]))
        stats6b.append(stats_middle(1, b, stats6[b]))
    tm_grad_middle(4)
    for copy in wo_first[:2]:
        copy.wait_recv()
    wo_send[0] = (wo_part[y_peer[0], :, left].astype(F32) + wo_got[0, 1].astype(F32)).astype(BF)
    wo_second = [links.push(wo_send.at[0], wo_got2.at[0], y_peer)]
    for copy in wo_first[2:]:
        copy.wait_recv()
    wo_send[1] = (wo_part[x_peer[0], :, right].astype(F32) + wo_got[1, 1].astype(F32)).astype(BF)
    wo_second.append(links.push(wo_send.at[1], wo_got2.at[1], x_peer))
    tm_grad_middle(0)
    tm_grad_start(2)
    tm_grad_end(4)
    out_second = gather_middle(out_full, own_lanes, all_rows, out_first)
    opening = jnp.zeros((1, own), F32)
    for b in both:
        rs = bucket_rows(b)
        back = scatter_end(3, b, part.at[1], moved_lanes, first6[b], second6[b])
        means = stats_end(1, b, stats6b[b])
        hat = (x_ref[rs, own_lanes(m)].astype(F32) - mean1[rs, :]) * rstd1[rs, :]
        opening = opening + jnp.sum(back * hat, axis=0, keepdims=True)
        value = middle_grad[rs] + norm_back(b, back, hat, OPENING, rstd1, means)
        gin_own[rs] = value.astype(BF)
    gin_first = gather_start(gin_own, gin_full, own_lanes, all_rows, keep=10)
    tm_grad_middle(1)
    tm_grad_start(3)
    tm_grad_end(0)

    vec_copies = links.group(
        [sens.at[:, moved_lanes(other)] for other in others],
        [u_got.at[i] for i in range(parts - 1)],
        [(d, other) for other in others],
        u_got,
    )
    gin_second = gather_middle(gin_full, own_lanes, all_rows, gin_first)
    vec_copies.wait_recv()
    total = sens[:, moved_lanes(m)]
    for i in range(parts - 1):
        total = total + u_got[i]
    u2_own[0:8] = total
    u2_own[6:7] = opening
    u2_own[7:8] = closing
    u2_own[8:16] = head_small[...]
    dp_copies = links.group(
        [u2_own] * 3, [u2_got.at[i] for i in range(3)], [x_peer, y_peer, diagonal], u2_got
    )
    tm_grad_middle(2)
    tm_grad_end(1)
    tm_grad_middle(3)
    tm_grad_end(2)
    dp_copies.wait_recv()
    u3_own[...] = (u2_own[...] + u2_got[0]) + (u2_got[1] + u2_got[2])
    all_copies = links.group(
        [u3_own] * (parts - 1),
        [u3_got.at[m]] * (parts - 1),
        [(d, other) for other in others],
        u3_got.at[pl.ds(0, parts - 1)],
    )
    u3_got[m] = u3_own[...]

    ff_grad_end(0, cg, hid, fv_grad2, ffv_out)
    ff_grad_end(1, kin, pre, fk_grad2, ffk_out)
    for way, lanes in enumerate((left, right)):
        wo_second[way].wait_recv()
        total = wo_part[d, :, lanes].astype(F32) + wo_got[way, 0].astype(F32) + wo_got2[way].astype(F32)
        wo_out[:, lanes] = total.astype(BF)
    tm_grad_end(3)
    all_copies.wait_recv()
    upper_d = lax.rem(d, 2) == 1
    low_vec = lax.broadcasted_iota(jnp.int32, (8, 128), 1) < LANE_WIDTH
    for e in range(2):
        vec_out[0:8, e * own : (e + 1) * own] = u3_got[2 * d + e, 0:8]
    for u in range(4):
        lanes = pl.ds(pl.multiple_of(lax.div(d, 2) * 128, 128), 128)
        first, second = u3_got[2 * u, 8:16, lanes], u3_got[2 * u + 1, 8:16, lanes]
        first = jnp.where(upper_d, swap_halves(first), first)
        second = jnp.where(upper_d, second, swap_halves(second))
        vec_out[8:16, u * 128 : (u + 1) * 128] = jnp.where(low_vec, first, second)
    gather_end(gin_first, gin_second)
    gather_end(out_first, out_second)
    for copy in back_copies:
        copy.wait_recv()
    for copy in own_copies:
        copy.wait()
    links.finish()
    assert links.used == COPIES, links.used


def finish_kernel(
    out, gin, ffk, ffv, back, wo, vec,
    out_o, gin_o, ffk_o, ffv_o, r_o, k_o, v_o, g_o, c_o, wo_o,
    y0, y1, y2, y3, y4, y5, y6, y7, y8, y9, y10,
    out_v, gin_v, ffk_v, ffv_v, back_v, wo_v, ffk_f, ffv_f, square, read, write,
):
    buckets, rows = out_o.shape[:2]
    reads = [
        pltpu.make_async_copy(a, b, read.at[i])
        for i, (a, b) in enumerate(
            ((ffv, ffv_v), (ffk, ffk_v), (wo, wo_v), (back, back_v), (out, out_v), (gin, gin_v))
        )
    ]
    for copy in reads:
        copy.start()
    writes = []

    def store(source, target):
        copy = pltpu.make_async_copy(source, target, write.at[len(writes)])
        copy.start()
        writes.append(copy)

    for i, ref in enumerate((y0, y1, y2, y3, y4, y5, y6, y7, y8, y9, y10)):
        ref[...] = vec[i : i + 1]
    for copy, source, middle, target in zip(reads, (ffv_v, ffk_v, wo_v), (ffv_f, ffk_f, square.at[5]), (ffv_o, ffk_o, wo_o)):
        copy.wait()
        middle[...] = source[...].astype(F32)
        store(middle, target)
    reads[3].wait()
    parts, shard, own = back_v.shape[1:]
    low = lax.broadcasted_iota(jnp.int32, (shard, 128), 1) < LANE_WIDTH
    for to in range(parts):
        square[4, :, to * own : (to + 1) * own] = back_v[4, to].astype(F32)
    store(square.at[4], c_o)
    for w, target in enumerate((r_o, k_o, v_o, g_o)):
        for j in range(4):
            for u in range(4):
                lanes = slice((j // 2) * 128, (j // 2 + 1) * 128)
                first = back_v[w, 2 * u, :, lanes].astype(F32)
                second = back_v[w, 2 * u + 1, :, lanes].astype(F32)
                if j % 2 == 0:
                    tile = jnp.where(low, first, swap_halves(second))
                else:
                    tile = jnp.where(low, swap_halves(first), second)
                start = j * 4 * 128 + u * 128
                square[w, :, start : start + 128] = tile
        store(square.at[w], target)
    for copy, source, target in ((reads[4], out_v, out_o), (reads[5], gin_v, gin_o)):
        copy.wait()
        for b in range(buckets):
            store(source.at[pl.ds(b * rows, rows)], target.at[b])
    for copy in writes:
        copy.wait()


def fast_body(*args):
    (
        block_arguments, bundled_spans, opening_gain, mix_r, mix_k, mix_v, mix_g, w_recept, w_key, w_value, w_gate,
        fading, reward, lane_gain, w_out, closing_gain, mix_fk, mix_fr, fk, fv, w_channel, upstream,
    ) = args
    buckets, bucket_rows, width = block_arguments.shape
    rows = buckets * bucket_rows
    parts, chips = 8, 4
    own, block = width // parts, width // 4
    hidden = fk.shape[1]
    shard = w_out.shape[0]
    vectors = [
        opening_gain, mix_r, mix_k, mix_v, mix_g, closing_gain, mix_fk, mix_fr, fading, reward, lane_gain,
    ]
    vectors = [vector.reshape(1, width) for vector in vectors]
    v, sm = pltpu.VMEM, pltpu.SMEM
    vm = pl.BlockSpec(memory_space=pltpu.VMEM)
    half_block = block // 2
    scratch = [
        v((16, width), F32), v((4, parts, shard, own), BF), v((4, 5, block, own), BF), v((3, block, hidden), BF), v((3, block, hidden), BF),
        v((4 * shard, width), BF), v((4, rows, width), BF), v((rows, 1), F32), v((rows, 1), F32), v((rows, 1), F32),
        v((rows, 1), F32), v((16, width), F32), v((16, own), F32), v((rows, own), BF),
        v((3, rows, own), BF), v((rows, own), F32), v((rows, own), F32), v((rows, own), F32), v((rows, own), BF),
        v((2, rows, width), BF), v((4, buckets, chips, bucket_rows, own), BF),
        v((buckets, chips - 1, bucket_rows, own), BF), v((4, buckets, chips - 1, bucket_rows, own), BF),
        v((2, buckets, chips + 2, 16, bucket_rows), F32),
        v((rows, own), F32), v((rows, own), BF), v((rows, width), BF), v((rows, width), BF), v((rows, width), BF),
        v((rows, hidden), BF), v((rows, hidden), BF), v((rows, hidden), BF), v((rows, own), F32), v((rows, own), BF),
        v((rows, width), BF),
        v((rows, own), BF), v((rows, own), BF), v((rows, own), F32), v((rows, own), BF),
        v((rows, width), BF), v((rows, own), F32), v((4, rows, own), BF), v((8, width), F32), v((8, own), F32),
        v((2, 2, 2, own, hidden), BF), v((2, 2, 2, own, hidden), BF), v((2, 2, own, hidden), BF),
        v((5, 2, 2, own, own), BF), v((5, 2, 2, own, own), BF), v((5, 2, own, own), BF),
        v((parts, shard, own), BF),
        v((4, shard, width), BF), v((2, 2, shard, width // 2), BF), v((2, shard, width // 2), BF),
        v((2, shard, width // 2), BF), v((rows, own), BF),
        v((parts - 1, 8, own), F32), v((16, own), F32), v((3, 16, own), F32), v((16, own), F32),
        v((parts, 16, own), F32),
        pltpu.SemaphoreType.DMA((COPIES,)), pltpu.SemaphoreType.DMA((COPIES,)), pltpu.SemaphoreType.DMA((12,)),
    ]
    out = pl.pallas_call(
        block_kernel,
        out_shape=[
            struct((rows, width), BF), struct((rows, width), BF), struct((block, hidden), BF),
            struct((block, hidden), BF), struct((5, parts, shard, own), BF), struct((shard, width), BF),
            struct((16, block), F32),
        ],
        in_specs=[pl.BlockSpec(memory_space=sm), vm, pl.BlockSpec(memory_space=pl.ANY)] + [vm] * 19,
        out_specs=[pl.BlockSpec(memory_space=pl.ANY)] * 5 + [vm] * 2,
        scratch_shapes=scratch,
        compiler_params=pltpu.CompilerParams(
            collective_id=0, has_side_effects=True, vmem_limit_bytes=VMEM_LIMIT
        ),
        name="whole_block",
    )(
        bundled_spans.reshape(buckets, -1), block_arguments.reshape(rows, width), upstream.reshape(rows, width), *vectors,
        w_recept, w_key, w_value, w_gate, w_out, w_channel, fk, fv,
    )
    square = struct((shard, width), F32)
    hbm = pl.BlockSpec(memory_space=pl.ANY)
    done = pl.pallas_call(
        finish_kernel,
        out_shape=[
            struct(block_arguments.shape, BF), struct(block_arguments.shape, BF), struct(fk.shape, F32),
            struct(fv.shape, F32), square, square, square, square, square, square,
        ]
        + [struct((1, block), F32)] * 11,
        in_specs=[hbm] * 6 + [vm],
        out_specs=[hbm] * 10 + [vm] * 11,
        scratch_shapes=[
            v((rows, width), BF), v((rows, width), BF), v(fk.shape, BF), v(fv.shape, BF), v((5, parts, shard, own), BF), v((shard, width), BF),
            v(fk.shape, F32), v(fv.shape, F32), v((6, shard, width), F32),
            pltpu.SemaphoreType.DMA((6,)), pltpu.SemaphoreType.DMA((2 * buckets + 8,)),
        ],
        compiler_params=pltpu.CompilerParams(vmem_limit_bytes=VMEM_LIMIT),
        name="finish",
    )(*out)
    outputs, grad_inputs, d_fk, d_fv, d_r, d_k, d_v, d_g, d_c, d_o = done[:10]
    small = [vector.reshape(block) for vector in done[10:]]
    return (
        outputs, grad_inputs, small[6], small[0], small[1], small[2], small[3], d_r, d_k, d_v, d_g,
        small[8], small[9], small[10], d_o, small[7], small[4], small[5], d_fk, d_fv, d_c,
    )


def body(*args):
    data_parts, parts = lax.axis_size("dp"), lax.axis_size("mp")
    width, shard, hidden = args[0].shape[2], args[7].shape[0], args[18].shape[1]
    fitted = (
        data_parts == 4
        and parts == 8
        and shard == LANE_WIDTH
        and width == 4 * parts * shard
        and hidden % 128 == 0
        and args[0].shape[:2] == (2, 128)
    )
    return fast_body(*args) if fitted else general_body(*args)


def solution(mesh):
    return jax.shard_map(
        body,
        mesh=mesh,
        in_specs=(
            P(None, "dp", None),
            P(None, "dp", None),
            P(),
            P(),
            P(),
            P(),
            P(),
            P(("dp", "mp"), None),
            P(("dp", "mp"), None),
            P(("dp", "mp"), None),
            P(("dp", "mp"), None),
            P(),
            P(),
            P(),
            P(("dp", "mp"), None),
            P(),
            P(),
            P(),
            P("dp", "mp"),
            P("dp", "mp"),
            P(("dp", "mp"), None),
            P(None, "dp", None),
        ),
        out_specs=(
            P(None, "dp", None),
            P(None, "dp", None),
            P("dp"),
            P("dp"),
            P("dp"),
            P("dp"),
            P("dp"),
            P(("dp", "mp"), None),
            P(("dp", "mp"), None),
            P(("dp", "mp"), None),
            P(("dp", "mp"), None),
            P("dp"),
            P("dp"),
            P("dp"),
            P(("dp", "mp"), None),
            P("dp"),
            P("dp"),
            P("dp"),
            P("dp", "mp"),
            P("dp", "mp"),
            P(("dp", "mp"), None),
        ),
        check_vma=False,
    )
```

```python
import functools
from functools import reduce

import jax
import jax.numpy as jnp
from jax import lax
from jax.experimental import pallas as pl
from jax.experimental.pallas import tpu as pltpu
from jax.sharding import PartitionSpec as P

LANE_WIDTH = 64
SPAN = 64


EPSILON = 1e-05
GROUP_EPSILON = 0.25
MIXED_MODE = lax.Precision.HIGH


def shortened(x):
    return jax.tree.map(lambda a: a.astype(jnp.bfloat16) if a.dtype == jnp.float32 else a, x)


def product(first_operand, second_operand):
    return jnp.dot(first_operand, second_operand, preferred_element_type=jnp.float32)


def product_rows(first_operand, second_operand):
    return lax.dot_general(
        first_operand, second_operand, (((0,), (0,)), ((), ())), preferred_element_type=jnp.float32
    )


def product_back(first_operand, second_operand):
    return lax.dot_general(
        first_operand, second_operand, (((1,), (1,)), ((), ())), preferred_element_type=jnp.float32
    )


def layer_norm(values, gain_entries):
    average = jnp.mean(values, axis=-1, keepdims=True)
    centered = values - average
    spread = jnp.mean(centered * centered, axis=-1, keepdims=True)
    return centered * lax.rsqrt(spread + EPSILON) * gain_entries


def group_norm(values, head_count):
    grouped = values.reshape(values.shape[0], head_count, -1)
    average = jnp.mean(grouped, axis=-1, keepdims=True)
    centered = grouped - average
    spread = jnp.mean(centered * centered, axis=-1, keepdims=True)
    return (centered * lax.rsqrt(spread + GROUP_EPSILON)).reshape(values.shape)


def segment_info(lengths, row_count):
    segment_ends = jnp.cumsum(lengths)
    places = jnp.arange(row_count, dtype=jnp.int32)
    sequence_label = jnp.sum((places[:, None] >= segment_ends[None, :]).astype(jnp.int32), axis=1)
    earlier = jnp.concatenate([jnp.full((1,), -1, jnp.int32), sequence_label[:-1]])
    common_series_filter = (sequence_label == earlier).astype(jnp.float32)
    valid_rows = (places < segment_ends[-1]).astype(jnp.float32)
    return (sequence_label, common_series_filter, valid_rows)


def shift_rows(values, common_series_filter):
    before = jnp.concatenate([jnp.zeros_like(values[:1]), values[:-1]], axis=0)
    return before * common_series_filter[:, None]


def iterative_renewal(
    accept_lines,
    lookup_weight_lines,
    payload_weight_lines,
    decay_logarithm,
    reward_scaler,
    sequence_label,
    layer_rows,
):
    row_count, head_count, head_width = accept_lines.shape
    block_count = row_count // layer_rows
    blocked = (block_count, layer_rows, head_count, head_width)
    accept_blocks = accept_lines.reshape(blocked)
    lookup_blocks = lookup_weight_lines.reshape(blocked)
    payload_blocks = payload_weight_lines.reshape(blocked)
    segment_blocks = sequence_label.reshape(block_count, layer_rows)
    positions = jnp.arange(layer_rows, dtype=jnp.float32)
    middle_step = float(layer_rows // 2)
    query_scale = jnp.exp(decay_logarithm[None] * (positions - middle_step)[:, None, None])
    key_scale = jnp.exp(decay_logarithm[None] * (middle_step - 1.0 - positions)[:, None, None])
    scores = jnp.einsum(
        "cthi,cshi->chts",
        accept_blocks * query_scale,
        lookup_blocks * key_scale,
        precision=MIXED_MODE,
    )
    causal = positions[:, None] > positions[None, :]
    within = segment_blocks[:, :, None] == segment_blocks[:, None, :]
    allowed = jnp.logical_and(causal[None], within).astype(jnp.float32)
    scores = scores * allowed[:, None]
    nested_routine = jnp.einsum("chts,cshj->cthj", scores, payload_blocks, precision=MIXED_MODE)
    reward_term = jnp.sum(accept_blocks * reward_scaler * lookup_blocks, axis=-1)
    nested_routine = nested_routine + reward_term[..., None] * payload_blocks
    last_segment = segment_blocks[:, -1]
    prior_segment = jnp.concatenate([jnp.full((1,), -1, jnp.int32), last_segment[:-1]])
    tail_scale = jnp.exp(decay_logarithm[None] * (layer_rows - 1.0 - positions)[:, None, None])
    tail_keep = (segment_blocks == last_segment[:, None]).astype(jnp.float32)
    added_state = jnp.einsum(
        "cshi,cshj->chij",
        lookup_blocks * tail_scale * tail_keep[:, :, None, None],
        payload_blocks,
        precision=MIXED_MODE,
    )
    carry_keep = (last_segment == prior_segment).astype(jnp.float32)
    whole_decay = jnp.exp(decay_logarithm * layer_rows)

    def advance(carry_state, piece_pair):
        addition, keep_flag = piece_pair
        return (whole_decay[:, :, None] * carry_state * keep_flag + addition, carry_state)

    initial = jnp.zeros((head_count, head_width, head_width), jnp.float32)
    unused, starts = lax.scan(advance, initial, (added_state, carry_keep))
    entry_keep = (segment_blocks == prior_segment[:, None]).astype(jnp.float32)
    entry_scale = jnp.exp(decay_logarithm[None] * positions[:, None, None])
    outside = jnp.einsum(
        "cthi,chij->cthj",
        accept_blocks * entry_scale * entry_keep[:, :, None, None],
        starts,
        precision=MIXED_MODE,
    )
    return (nested_routine + outside).reshape(row_count, head_count, head_width)


def add_terms(first_terms, second_terms):
    return jax.tree.map(jnp.add, first_terms, second_terms)


def general_body(
    block_arguments,
    bundled_spans,
    opening_normalize_scale,
    accept_lagmix,
    lookup_lagmix,
    payload_lagmix,
    valve_lagmix,
    accept_weights,
    lookup_weights,
    payload_weights,
    valve_weights,
    fading_speed_logs,
    present_reward,
    lane_normalize_scale,
    emission_weights,
    closing_normalize_scale,
    feedforward_lookup_lagmix,
    feedforward_accept_lagmix,
    feedforward_lookup_weights,
    feedforward_payload_weights,
    feedforward_accept_weights,
    upstream_sensitivity,
):
    micro_count, row_count, model_width = block_arguments.shape
    layer_rows = SPAN
    data_parts = lax.axis_size("dp")
    model_parts = lax.axis_size("mp")
    shard_rows = accept_weights.shape[0]
    model_place = lax.axis_index("mp")
    partition_lanes = model_width // LANE_WIDTH

    def own_columns(values):
        split_values = values.reshape(row_count, data_parts, model_parts, shard_rows)
        picked = lax.dynamic_index_in_dim(split_values, model_place, axis=2, keepdims=False)
        return picked.reshape(row_count, data_parts * shard_rows)

    outputs_list = []
    input_grads = []
    gradient_terms = []
    for micro_index in range(micro_count):
        projections = (
            lax.all_gather(accept_weights, ("dp", "mp"), axis=0, tiled=True),
            lax.all_gather(lookup_weights, ("dp", "mp"), axis=0, tiled=True),
            lax.all_gather(payload_weights, ("dp", "mp"), axis=0, tiled=True),
            lax.all_gather(valve_weights, ("dp", "mp"), axis=0, tiled=True),
            lax.all_gather(emission_weights, ("dp", "mp"), axis=0, tiled=True),
            lax.all_gather(feedforward_accept_weights, ("dp", "mp"), axis=0, tiled=True),
        )
        hidden_pair = (
            lax.all_gather(feedforward_lookup_weights, "dp", axis=0, tiled=True),
            lax.all_gather(feedforward_payload_weights, "dp", axis=0, tiled=True),
        )
        full_recept, full_key, full_value, full_gate, full_output, full_channel = projections
        hidden_key, hidden_value = hidden_pair
        sequence_label, common_series_filter, valid_rows = segment_info(
            bundled_spans[micro_index, 0], row_count
        )
        rows_float = block_arguments[micro_index].astype(jnp.float32)

        def front_part(rows_value, gain_entries, recept_mix, key_mix, value_mix, gate_mix):
            normed = layer_norm(rows_value, gain_entries)
            before = shift_rows(normed, common_series_filter)
            return tuple(
                (
                    normed * weight_mix + before * (1.0 - weight_mix)
                    for weight_mix in (recept_mix, key_mix, value_mix, gate_mix)
                )
            )

        front_values, front_pull = jax.vjp(
            front_part,
            rows_float,
            opening_normalize_scale,
            accept_lagmix,
            lookup_lagmix,
            payload_lagmix,
            valve_lagmix,
        )
        recept_in, key_in, value_in, gate_in = [
            front_piece.astype(jnp.bfloat16) for front_piece in front_values
        ]
        accept_lines = product(recept_in, full_recept).astype(jnp.bfloat16)
        lookup_weight_lines = product(key_in, full_key).astype(jnp.bfloat16)
        payload_weight_lines = product(value_in, full_value).astype(jnp.bfloat16)
        gate_raw = product(gate_in, full_gate)

        def middle_part(
            receptance_activation,
            key_value_product,
            value_activation,
            gate_activation,
            decay_parameter,
            reward_weight,
            gain_entries,
        ):
            decay_logarithm = -jnp.exp(decay_parameter).reshape(partition_lanes, -1)
            reward_scaler = reward_weight.reshape(partition_lanes, -1)
            reformed_array = (row_count, partition_lanes, model_width // partition_lanes)
            lane_answers = iterative_renewal(
                receptance_activation.reshape(reformed_array),
                key_value_product.reshape(reformed_array),
                value_activation.reshape(reformed_array),
                decay_logarithm,
                reward_scaler,
                sequence_label,
                layer_rows,
            )
            grouped = (
                group_norm(lane_answers.reshape(row_count, model_width), partition_lanes)
                * gain_entries
            )
            return grouped * jax.nn.silu(gate_activation)

        mixed_float, middle_pull = jax.vjp(
            middle_part,
            accept_lines.astype(jnp.float32),
            lookup_weight_lines.astype(jnp.float32),
            payload_weight_lines.astype(jnp.float32),
            gate_raw,
            fading_speed_logs,
            present_reward,
            lane_normalize_scale,
        )
        merged_lanes = mixed_float.astype(jnp.bfloat16)
        middle = rows_float + product(merged_lanes, full_output)

        def back_part(middle_value, gain_entries, key_mix, recept_mix):
            normed = layer_norm(middle_value, gain_entries)
            before = shift_rows(normed, common_series_filter)
            return (
                normed * key_mix + before * (1.0 - key_mix),
                normed * recept_mix + before * (1.0 - recept_mix),
            )

        channel_values, back_pull = jax.vjp(
            back_part,
            middle,
            closing_normalize_scale,
            feedforward_lookup_lagmix,
            feedforward_accept_lagmix,
        )
        channel_key_in = channel_values[0].astype(jnp.bfloat16)
        channel_recept_in = channel_values[1].astype(jnp.bfloat16)
        hidden_input = product(channel_key_in, hidden_key)
        hidden = jnp.square(jnp.maximum(hidden_input, 0.0)).astype(jnp.bfloat16)
        carried = lax.psum(product_back(hidden, hidden_value).astype(jnp.bfloat16), "mp").astype(
            jnp.float32
        )
        channel_gate = jax.nn.sigmoid(product(channel_recept_in, full_channel))
        outputs_list.append(
            ((middle + channel_gate * carried) * valid_rows[:, None]).astype(jnp.bfloat16)
        )
        top_grad = upstream_sensitivity[micro_index].astype(jnp.float32) * valid_rows[:, None]
        carried_grad = (top_grad * channel_gate).astype(jnp.bfloat16)
        gate_input_grad = (top_grad * carried * channel_gate * (1.0 - channel_gate)).astype(
            jnp.bfloat16
        )
        pre_grad = (
            product(carried_grad, hidden_value) * 2.0 * jnp.maximum(hidden_input, 0.0)
        ).astype(jnp.bfloat16)
        channel_key_grad = lax.psum(
            product_back(pre_grad, hidden_key).astype(jnp.bfloat16), "mp"
        ).astype(jnp.float32)
        channel_recept_grad = product_back(gate_input_grad, full_channel)
        middle_back, grad_second, feedforward_lookup_lagmix_sens, feedforward_accept_lagmix_sens = (
            back_pull((channel_key_grad, channel_recept_grad))
        )
        middle_grad = top_grad + middle_back
        branch_grad = middle_grad.astype(jnp.bfloat16)
        mixed_grad = product_back(branch_grad, full_output)
        output_term = product_rows(own_columns(merged_lanes), branch_grad)
        (
            receptance_single_precision,
            key_single_precision,
            value_single_precision,
            gate_single_precision,
            decay_gradient,
            reward_derivative,
            lane_normalize_derivative,
        ) = middle_pull(mixed_grad)
        recept_grad = receptance_single_precision.astype(jnp.bfloat16)
        key_grad = key_single_precision.astype(jnp.bfloat16)
        value_grad = value_single_precision.astype(jnp.bfloat16)
        gate_grad = gate_single_precision.astype(jnp.bfloat16)
        (
            line_derivatives,
            grad_first,
            grad_recept_mix,
            grad_key_mix,
            grad_value_mix,
            grad_gate_mix,
        ) = front_pull(
            (
                product_back(recept_grad, full_recept),
                product_back(key_grad, full_key),
                product_back(value_grad, full_value),
                product_back(gate_grad, full_gate),
            )
        )
        projection_terms = (
            product_rows(own_columns(recept_in), recept_grad),
            product_rows(own_columns(key_in), key_grad),
            product_rows(own_columns(value_in), value_grad),
            product_rows(own_columns(gate_in), gate_grad),
            output_term,
        )
        input_grads.append((middle_grad + line_derivatives).astype(jnp.bfloat16))
        local_terms = (
            grad_first,
            grad_recept_mix,
            grad_key_mix,
            grad_value_mix,
            grad_gate_mix,
            decay_gradient,
            reward_derivative,
            lane_normalize_derivative,
            grad_second,
            feedforward_lookup_lagmix_sens,
            feedforward_accept_lagmix_sens,
            product_rows(channel_key_in, pre_grad),
            product_rows(carried_grad, hidden),
            product_rows(own_columns(channel_recept_in), gate_input_grad),
        ) + projection_terms
        gradient_terms.append(local_terms)
    summed = reduce(add_terms, gradient_terms)
    summed = jax.tree.map(
        lambda part: part.astype(jnp.float32),
        lax.psum_scatter(shortened(summed), "dp", scatter_dimension=0, tiled=True),
    )
    (
        grad_first,
        grad_recept_mix,
        grad_key_mix,
        grad_value_mix,
        grad_gate_mix,
        decay_gradient,
        reward_derivative,
        lane_normalize_derivative,
        grad_second,
        feedforward_lookup_lagmix_sens,
        feedforward_accept_lagmix_sens,
        feedforward_lookup_derivative,
        feedforward_payload_derivative,
        feedforward_accept_derivative,
        grad_recept,
        grad_key,
        grad_value,
        grad_gate,
        grad_output,
    ) = summed
    return (
        jnp.stack(outputs_list),
        jnp.stack(input_grads),
        grad_first,
        grad_recept_mix,
        grad_key_mix,
        grad_value_mix,
        grad_gate_mix,
        grad_recept,
        grad_key,
        grad_value,
        grad_gate,
        decay_gradient,
        reward_derivative,
        lane_normalize_derivative,
        grad_output,
        grad_second,
        feedforward_lookup_lagmix_sens,
        feedforward_accept_lagmix_sens,
        feedforward_lookup_derivative,
        feedforward_payload_derivative,
        feedforward_accept_derivative,
    )


MESH = pl.DeviceIdType.MESH
BF = jnp.bfloat16
F32 = jnp.float32
VMEM_LIMIT = 63 << 20
OPENING, CLOSING, FADING, REWARD, LANE = 0, 5, 8, 9, 10


def struct(shape, dtype):
    return jax.ShapeDtypeStruct(shape, dtype)


def flip(place, other):
    low = lax.rem(lax.rem(place, 2) + lax.rem(other, 2), 2)
    high = lax.rem(lax.div(place, 2) + lax.div(other, 2), 2)
    return 2 * high + low


def nt(a, b):
    return lax.dot_general(a, b, (((1,), (1,)), ((), ())), preferred_element_type=F32)


def tn(a, b):
    return lax.dot_general(a, b, (((0,), (0,)), ((), ())), preferred_element_type=F32)


def nn(a, b):
    return lax.dot_general(a, b, (((1,), (0,)), ((), ())), preferred_element_type=F32)


def roll_rows(values, shift):
    return pltpu.roll(values, shift % values.shape[0], 0)


def swap_halves(tile):
    return pltpu.roll(tile, LANE_WIDTH, 1)


def head_sums(values, low):
    first = jnp.sum(jnp.where(low, values, 0.0), axis=1, keepdims=True)
    second = jnp.sum(jnp.where(low, 0.0, values), axis=1, keepdims=True)
    return jnp.where(low, first, second)


class Links:
    def __init__(self, send, recv):
        self.send, self.recv = send, recv
        self.used = 0
        self.open = []

    def push(self, source, target, peer):
        i = self.used
        self.used += 1
        copy = pltpu.make_async_remote_copy(
            source, target, self.send.at[i], self.recv.at[i], device_id=peer, device_id_type=MESH
        )
        copy.start()
        self.open.append(copy)
        return copy

    def group(self, sources, targets, peers, whole):
        i = self.used
        self.used += 1
        for source, target, peer in zip(sources, targets, peers):
            pltpu.make_async_remote_copy(
                source, target, self.send.at[i], self.recv.at[i], device_id=peer, device_id_type=MESH
            ).start()
        copy = pltpu.make_async_remote_copy(
            whole, whole, self.send.at[i], self.recv.at[i], device_id=peers[0], device_id_type=MESH
        )
        self.open.append(copy)
        return copy

    def sent(self, copy):
        if any(other is copy for other in self.open):
            copy.wait_send()
            self.open = [other for other in self.open if other is not copy]

    def finish(self):
        for copy in self.open:
            copy.wait_send()


COPIES = 204


def block_kernel(
    spans, x_ref, up_ref, v0, v1, v2, v3, v4, v5, v6, v7, v8, v9, v10, w_recept, w_key, w_value, w_gate, w_out, w_channel, fk, fv,
    out_full, gin_full, ffk_out, ffv_out, back_out, wo_out, vec_out,
    vec, blocks, g, fkb, fvb, wob, acts, mean1, rstd1, mean2, rstd2, order_vec, head_vec, seen,
    rkv, gate_raw, n_ref, n_scale, mixed, part, half, pair, far, small,
    mid_own, mid_own_b, mid, kin, cri, hid, pos, pre, channel_gate, cg_own, cg,
    out_own, gig, middle_grad, branch_own, branch, mixed_grad, time_grads, sens, head_small,
    ff_send, ff_got, ff_got2, tm_send, tm_got, tm_got2, channel_sum,
    wo_part, wo_got, wo_send, wo_got2, gin_own, u_got, u2_own, u2_got, u3_own, u3_got,
    send, recv, local,
):
    d, m = lax.axis_index("dp"), lax.axis_index("mp")
    z, c = lax.div(m, 2), lax.rem(m, 2)
    chips, parts = 4, 8
    buckets, rows = 2, x_ref.shape[0] // 2
    width = x_ref.shape[1]
    own = width // parts
    block = width // 4
    shard = w_out.shape[0]
    pairs = own // 128
    links = Links(send, recv)
    mate = (d, 2 * z + 1 - c)
    chips_away = [lax.rem(z + i, chips) for i in range(1, chips)]
    others = [lax.rem(m + i, parts) for i in range(1, parts)]
    x_peer = (d + 1 - 2 * lax.rem(d, 2), m)
    y_peer = (d + 2 - 4 * lax.div(d, 2), m)
    diagonal = (3 - d, m)
    order = [d, x_peer[0], y_peer[0], diagonal[0]]

    def own_lanes(owner):
        return pl.ds(pl.multiple_of(owner * own, own), own)

    def moved_lanes(owner):
        place = 2 * flip(lax.div(owner, 2), d) + lax.rem(owner, 2)
        return pl.ds(pl.multiple_of(place * own, own), own)

    def bucket_rows(b):
        return slice(b * rows, (b + 1) * rows)

    barrier = pltpu.get_barrier_semaphore()
    greeted = [(d, other) for other in others] + [x_peer, y_peer, diagonal]
    for peer in greeted:
        pl.semaphore_signal(barrier, inc=1, device_id=peer, device_id_type=MESH)
    top_copy = pltpu.make_async_copy(up_ref.at[:, own_lanes(m)], seen, local.at[0])
    top_copy.start()
    low16 = lax.broadcasted_iota(jnp.int32, (shard, 128), 1) < LANE_WIDTH
    vec[...] = jnp.zeros_like(vec)
    for i, ref in enumerate((v0, v1, v2, v3, v4, v5, v6, v7, v8, v9, v10)):
        vec[i : i + 1] = ref[...]

    def head_blocks(w, weight):
        for to in range(parts):
            for q in range(pairs):
                tiles = []
                for j in (2 * q, 2 * q + 1):
                    start = j * block + (to // 2) * 128
                    tiles.append(weight[:, start : start + 128].astype(F32))
                if to % 2 == 0:
                    tile = jnp.where(low16, tiles[0], swap_halves(tiles[1]))
                else:
                    tile = jnp.where(low16, swap_halves(tiles[0]), tiles[1])
                blocks[w, to, :, q * 128 : (q + 1) * 128] = tile.astype(BF)

    pl.semaphore_wait(barrier, len(greeted))
    top_copy.wait()

    my_rows = pl.ds(pl.multiple_of(m * shard, shard), shard)

    def exchange(w):
        if w < 4:
            sources = [blocks.at[w, other] for other in others]
        else:
            sources = [w_channel.at[:, own_lanes(other)] for other in others]
        return links.group(
            sources,
            [g.at[0, w, my_rows]] * (parts - 1),
            [(d, other) for other in others],
            g.at[0, w, pl.ds(0, (parts - 1) * shard)],
        )

    half_block = block // 2
    upper_half, lower_half = pl.ds(0, half_block), pl.ds(half_block, half_block)

    def relay_out(source, slot1, slot2, which):
        return (
            links.push(source.at[which], slot1.at[which], x_peer),
            links.push(source.at[which], slot2.at[which], y_peer),
        )

    def forward(upper_copies, lower_copies, slot1, slot2, slot3):
        upper_copies[0].wait_recv()
        one = links.push(slot1.at[upper_half], slot3.at[upper_half], y_peer)
        lower_copies[1].wait_recv()
        two = links.push(slot2.at[lower_half], slot3.at[lower_half], x_peer)
        return (one, two) + (() if upper_copies is lower_copies else (upper_copies[1], lower_copies[0]))

    fk_upper = relay_out(fk, fkb.at[0], fkb.at[1], upper_half)

    def out_rows(dp_place, start, size):
        return pl.ds(pl.multiple_of(dp_place * shard + start, 32), size)

    wo_first = [links.push(w_out, wob.at[out_rows(d, 0, shard)], peer) for peer in (x_peer, y_peer)]
    arrivals = []
    for w, weight in enumerate((w_recept, w_key, w_value, w_gate)):
        head_blocks(w, weight)
        arrivals.append(exchange(w))
    arrivals.append(exchange(4))
    for w in range(4):
        g[0, w, my_rows] = blocks[w, m]
    g[0, 4, my_rows] = w_channel[:, own_lanes(m)]
    wob[out_rows(d, 0, shard)] = w_out[...]

    for j in range(4):
        order_vec[:, j * block : (j + 1) * block] = vec[
            :, pl.ds(pl.multiple_of(order[j] * block, block), block)
        ]
    low_row = lax.broadcasted_iota(jnp.int32, (16, 128), 1) < LANE_WIDTH
    upper = lax.rem(m, 2) == 1

    def head_tile(j):
        start = pl.multiple_of(j * block + lax.div(m, 2) * 128, 128)
        return vec[:, pl.ds(start, 128)]

    for q in range(pairs):
        first, second = head_tile(2 * q), head_tile(2 * q + 1)
        first = jnp.where(upper, swap_halves(first), first)
        second = jnp.where(upper, second, swap_halves(second))
        head_vec[:, q * 128 : (q + 1) * 128] = jnp.where(low_row, first, second)

    def row_masks(b):
        t = lax.broadcasted_iota(jnp.int32, (rows, 1), 0)
        lane = lax.broadcasted_iota(jnp.int32, (1, rows), 1)
        label, past, ahead = (jnp.zeros((rows, 1), jnp.int32) for unused in range(3))
        label_row = jnp.zeros((1, rows), jnp.int32)
        end = jnp.int32(0)
        for j in range(spans.shape[1]):
            end = end + spans[b, j]
            label = label + jnp.where(t >= end, 1, 0)
            past = past + jnp.where(t - 1 >= end, 1, 0)
            ahead = ahead + jnp.where(t + 1 >= end, 1, 0)
            label_row = label_row + jnp.where(lane >= end, 1, 0)
        same = jnp.where(jnp.logical_and(label == past, t > 0), 1.0, 0.0)
        following = jnp.where(jnp.logical_and(label == ahead, t < rows - 1), 1.0, 0.0)
        valid = jnp.where(t < end, 1.0, 0.0)
        return label, label_row, same, following, valid

    masks = [row_masks(b) for b in range(buckets)]

    def mix(b, take, mean, rstd, gain_row, mix_row, outs):
        rs = bucket_rows(b)
        same = masks[b][2]
        total = jnp.zeros((rows, 1), F32)
        for j in range(4):
            total = total + jnp.sum(take(rs, j).astype(F32), axis=1, keepdims=True)
        average = total / width
        spread = jnp.zeros((rows, 1), F32)
        for j in range(4):
            centered = take(rs, j).astype(F32) - average
            spread = spread + jnp.sum(centered * centered, axis=1, keepdims=True)
        scale = lax.rsqrt(spread / width + EPSILON)
        mean[rs, :] = average
        rstd[rs, :] = scale
        for j in range(4):
            cols = slice(j * block, (j + 1) * block)
            normed = (take(rs, j).astype(F32) - average) * scale * order_vec[gain_row : gain_row + 1, cols]
            before = roll_rows(normed, 1) * same
            change = normed - before
            for i, out in enumerate(outs):
                weight = order_vec[mix_row + i : mix_row + i + 1, cols]
                out[rs, cols] = (before + change * weight).astype(BF)

    def take_x(rs, j):
        return x_ref[rs, pl.ds(pl.multiple_of(order[j] * block, block), block)]

    def take_mid(rs, j):
        return mid[rs, j * block : (j + 1) * block]

    for b in range(buckets):
        mix(b, take_x, mean1, rstd1, OPENING, OPENING + 1, [acts.at[w] for w in range(4)])

    g_first = []
    everything = pl.ds(0, block)
    for w in range(4):
        arrivals[w].wait_recv()
        g_first.append(relay_out(g.at[0, w], g.at[1, w], g.at[2, w], everything))
    g_second = [forward(g_first[w], g_first[w], g.at[1, w], g.at[2, w], g.at[3, w]) for w in range(4)]
    wo_first[0].wait_recv()
    wo_rows = out_rows(x_peer[0], 0, shard // 2)
    wo_second = [links.push(wob.at[wo_rows], wob.at[wo_rows], y_peer)]
    wo_first[1].wait_recv()
    wo_rows = out_rows(y_peer[0], shard // 2, shard // 2)
    wo_second.append(links.push(wob.at[wo_rows], wob.at[wo_rows], x_peer))
    fk_lower = relay_out(fk, fkb.at[0], fkb.at[1], lower_half)
    arrivals[4].wait_recv()
    g_first.append(relay_out(g.at[0, 4], g.at[1, 4], g.at[2, 4], everything))

    for w in range(4):
        for copy in g_second[w]:
            copy.wait_recv()
        for b in range(buckets):
            rs = bucket_rows(b)
            total = nn(acts[w, rs, 0:block], g[0, w])
            for j in range(1, 4):
                total = total + nn(acts[w, rs, j * block : (j + 1) * block], g[j, w])
            if w < 3:
                rkv[w, rs] = total.astype(BF)
            else:
                gate_raw[rs] = total
    fv_upper = relay_out(fv, fvb.at[0], fvb.at[1], upper_half)

    low = lax.broadcasted_iota(jnp.int32, (rows, 128), 1) < LANE_WIDTH
    t_square = lax.broadcasted_iota(jnp.int32, (rows, rows), 0)
    s_square = lax.broadcasted_iota(jnp.int32, (rows, rows), 1)
    places = lax.broadcasted_iota(jnp.int32, (rows, 1), 0).astype(F32) - float(rows // 2)

    def decay_scales(cols):
        log_decay = -jnp.exp(head_vec[FADING : FADING + 1, cols])
        return jnp.exp(log_decay * places), jnp.exp(log_decay * (-1.0 - places))

    def allowed_pairs(b):
        return jnp.logical_and(s_square < t_square, masks[b][0] == masks[b][1])

    def scores_of(rt, kt, now, mine, allowed):
        scores = nt(jnp.where(mine, rt, 0.0).astype(BF), kt)
        here = jnp.sum(jnp.where(mine, now, 0.0), axis=1, keepdims=True)
        return jnp.where(allowed, scores, jnp.where(s_square == t_square, here, 0.0)).astype(BF)

    def time_forward(b):
        rs = bucket_rows(b)
        allowed = allowed_pairs(b)
        for p in range(pairs):
            cols = slice(p * 128, (p + 1) * 128)
            out_scale, in_scale = decay_scales(cols)
            r, k = rkv[0, rs, cols].astype(F32), rkv[1, rs, cols].astype(F32)
            v = rkv[2, rs, cols]
            rt, kt = r * out_scale, (k * in_scale).astype(BF)
            now = r * head_vec[REWARD : REWARD + 1, cols] * k
            first = nn(scores_of(rt, kt, now, low, allowed), v)
            second = nn(scores_of(rt, kt, now, jnp.logical_not(low), allowed), v)
            wkv = jnp.where(low, first, second)
            centered = wkv - head_sums(wkv, low) / LANE_WIDTH
            scale = lax.rsqrt(head_sums(centered * centered, low) / LANE_WIDTH + GROUP_EPSILON)
            n = centered * scale
            n_ref[rs, cols] = n
            n_scale[rs, cols] = scale
            gate = gate_raw[rs, cols]
            gained = n * head_vec[LANE : LANE + 1, cols] * gate * jax.nn.sigmoid(gate)
            mixed[rs, cols] = gained.astype(BF)

    pair_copies = {}
    own_copies = []

    def scatter_start(k, b, source, lanes):
        rs = pl.ds(b * rows, rows)
        return [
            links.push(source.at[rs, lanes(2 * other + 1 - c)], half.at[k, b, i], mate)
            for i, other in enumerate(chips_away + [z])
        ]

    def scatter_middle(k, b, source, lanes, first):
        rs = pl.ds(b * rows, rows)
        copies = []
        for i, other in enumerate(chips_away):
            if (b, i) in pair_copies:
                links.sent(pair_copies[b, i])
            first[i].wait_recv()
            value = source[rs, lanes(2 * other + c)].astype(F32) + half[k, b, i].astype(F32)
            pair[b, i] = value.astype(BF)
            copy = links.push(pair.at[b, i], far.at[k, b, i], (d, 2 * other + c))
            pair_copies[b, i] = copy
            copies.append(copy)
        return copies

    def scatter_end(k, b, source, lanes, first, second):
        rs = pl.ds(b * rows, rows)
        first[chips - 1].wait_recv()
        total = source[rs, lanes(m)].astype(F32) + half[k, b, chips - 1].astype(F32)
        for i, copy in enumerate(second):
            copy.wait_recv()
            total = total + far[k, b, i].astype(F32)
        return total

    def stats_start(k, b):
        return links.push(small.at[k, b, 0], small.at[k, b, 1], mate)

    def stats_middle(k, b, first):
        first.wait_recv()
        small[k, b, 2] = small[k, b, 0] + small[k, b, 1]
        return [
            links.push(small.at[k, b, 2], small.at[k, b, 3 + i], (d, 2 * other + c))
            for i, other in enumerate(chips_away)
        ]

    eye8 = jnp.where(lax.broadcasted_iota(jnp.int32, (16, 128), 0) == 0, 1.0, 0.0)
    eye16 = jnp.where(lax.broadcasted_iota(jnp.int32, (16, 128), 0) == 8, 1.0, 0.0)

    def stats_end(k, b, second):
        total = small[k, b, 2]
        for i, copy in enumerate(second):
            copy.wait_recv()
            total = total + small[k, b, 3 + i]
        total = total / width
        turn = lambda e: lax.dot_general(
            total, e, (((0,), (0,)), ((), ())), precision=lax.Precision.HIGHEST, preferred_element_type=F32
        )[:, 0:1]
        return turn(eye8), turn(eye16)

    def gather_start(source, target, lanes, rs, keep=None):
        mine = target.at[rs, lanes(m)]
        copies = [links.push(source.at[rs], mine, (d, 2 * other + c)) for other in chips_away]
        copies.append(links.push(source.at[rs], mine, mate))
        if keep is None:
            target[rs, lanes(m)] = source[rs]
        else:
            own_copies.append(pltpu.make_async_copy(source.at[rs], mine, local.at[keep]))
            own_copies[-1].start()
        return copies

    def gather_middle(target, lanes, rs, first):
        copies = []
        for i in range(chips - 1):
            source = 2 * lax.rem(z - (i + 1) + chips, chips) + c
            first[i].wait_recv()
            copies.append(links.push(target.at[rs, lanes(source)], target.at[rs, lanes(source)], mate))
        return copies

    def gather_end(first, second):
        first[-1].wait_recv()
        for copy in second:
            copy.wait_recv()

    both = (0, 1)
    slices = [pl.ds(b * rows, rows) for b in both]
    all_rows = pl.ds(0, buckets * rows)

    for copy in wo_second:
        copy.wait_recv()
    first1 = []
    for b in both:
        time_forward(b)
        rs = bucket_rows(b)
        for j in range(4):
            cols = slice(j * block, (j + 1) * block)
            part[0, rs, cols] = nn(mixed[rs], wob[:, cols]).astype(BF)
        first1.append(scatter_start(0, b, part.at[0], own_lanes))
    g_second.append(forward(g_first[4], g_first[4], g.at[1, 4], g.at[2, 4], g.at[3, 4]))
    fk_second = forward(fk_upper, fk_lower, fkb.at[0], fkb.at[1], fkb.at[2])
    fv_lower = relay_out(fv, fvb.at[0], fvb.at[1], lower_half)
    second1 = [scatter_middle(0, b, part.at[0], own_lanes, first1[b]) for b in both]
    gathers = []
    for b in both:
        rs = bucket_rows(b)
        total = scatter_end(0, b, part.at[0], own_lanes, first1[b], second1[b])
        middle = x_ref[rs, own_lanes(m)].astype(F32) + total
        mid_own[rs] = middle
        mid_own_b[rs] = middle.astype(BF)
        gathers.append(gather_start(mid_own_b, mid, moved_lanes, slices[b]))
    onward = [gather_middle(mid, moved_lanes, slices[b], gathers[b]) for b in both]
    for b in both:
        gather_end(gathers[b], onward[b])
        mix(b, take_mid, mean2, rstd2, CLOSING, CLOSING + 1, [kin, cri])
    for copy in g_second[4]:
        copy.wait_recv()

    def top(b):
        return seen[bucket_rows(b)].astype(F32) * masks[b][4]

    for b in both:
        rs = bucket_rows(b)
        total = nn(cri[rs, 0:block], g[0, 4])
        for j in range(1, 4):
            total = total + nn(cri[rs, j * block : (j + 1) * block], g[j, 4])
        gate = jax.nn.sigmoid(total)
        channel_gate[rs] = gate
        cg_own[rs] = (top(b) * gate).astype(BF)
    gathers = gather_start(cg_own, cg, moved_lanes, all_rows)
    for copy in fk_second:
        copy.wait_recv()

    def fk_piece(j):
        return fk if j == 0 else fkb.at[j - 1]

    def fv_piece(j):
        return fv if j == 0 else fvb.at[j - 1]

    for b in both:
        rs = bucket_rows(b)
        total = nn(kin[rs, 0:block], fk[...])
        for j in range(1, 4):
            total = total + nn(kin[rs, j * block : (j + 1) * block], fkb[j - 1])
        positive = jnp.maximum(total, 0.0)
        hid[rs] = (positive * positive).astype(BF)
        pos[rs] = positive.astype(BF)
    fv_second = forward(fv_upper, fv_lower, fvb.at[0], fvb.at[1], fvb.at[2])
    onward = gather_middle(cg, moved_lanes, all_rows, gathers)
    gather_end(gathers, onward)

    piece = own

    def product_piece(lhs, rhs, i):
        return tn(lhs[:, i * piece : (i + 1) * piece], rhs[...])

    def ff_grad_start(k, lhs, rhs):
        for i, (way, slot) in ((2, (0, 0)), (6, (0, 1)), (5, (1, 0)), (7, (1, 1))):
            ff_send[k, way, slot] = product_piece(lhs, rhs, i).astype(BF)
        return (
            links.push(ff_send.at[k, 0], ff_got.at[k, 0], x_peer),
            links.push(ff_send.at[k, 1], ff_got.at[k, 1], y_peer),
        )

    def ff_grad_middle(k, lhs, rhs, first):
        for way, i in ((0, 4), (1, 3)):
            value = product_piece(lhs, rhs, i)
            first[way].wait_recv()
            links.sent(first[way])
            ff_send[k, way, 0] = (value + ff_got[k, way, 1].astype(F32)).astype(BF)

    def ff_grad_relay(k):
        return (
            links.push(ff_send.at[k, 0, 0], ff_got2.at[k, 0], y_peer),
            links.push(ff_send.at[k, 1, 0], ff_got2.at[k, 1], x_peer),
        )

    def ff_grad_end(k, lhs, rhs, second, out):
        for way in range(2):
            second[way].wait_recv()
            total = product_piece(lhs, rhs, way) + ff_got[k, way, 0].astype(F32) + ff_got2[k, way].astype(F32)
            ff_send[k, way, 1] = total.astype(BF)
            own_copies.append(
                pltpu.make_async_copy(
                    ff_send.at[k, way, 1], out.at[pl.ds(way * piece, piece)], local.at[1 + 2 * k + way]
                )
            )
            own_copies[-1].start()

    tm_first, tm_second, back_copies = {}, {}, []

    def tm_lhs(w):
        return acts.at[w] if w < 4 else cri

    def tm_rhs(w):
        return time_grads.at[w] if w < 4 else gig

    def tm_grad_start(w):
        for i, (way, slot) in ((2, (0, 0)), (6, (0, 1)), (5, (1, 0)), (7, (1, 1))):
            tm_send[w, way, slot] = product_piece(tm_lhs(w), tm_rhs(w), i).astype(BF)
        tm_first[w] = (
            links.push(tm_send.at[w, 0], tm_got.at[w, 0], x_peer),
            links.push(tm_send.at[w, 1], tm_got.at[w, 1], y_peer),
        )

    def tm_grad_middle(w):
        copies = []
        for way, (i, peer) in enumerate(((4, y_peer), (3, x_peer))):
            value = product_piece(tm_lhs(w), tm_rhs(w), i)
            tm_first[w][way].wait_recv()
            links.sent(tm_first[w][way])
            tm_send[w, way, 0] = (value + tm_got[w, way, 1].astype(F32)).astype(BF)
            copies.append(links.push(tm_send.at[w, way, 0], tm_got2.at[w, way], peer))
        tm_second[w] = copies

    def tm_grad_end(w):
        links.sent(arrivals[w])
        sums = blocks.at[w] if w < 4 else channel_sum
        for way in range(2):
            value = product_piece(tm_lhs(w), tm_rhs(w), way)
            tm_second[w][way].wait_recv()
            value = value + tm_got[w, way, 0].astype(F32) + tm_got2[w, way].astype(F32)
            sums[4 * way : 4 * way + 4] = value.astype(BF).reshape(4, shard, own)
        back_copies.append(
            links.group(
                [sums.at[other] for other in others],
                [back_out.at[w, m]] * (parts - 1),
                [(d, other) for other in others],
                back_out.at[w, pl.ds(0, parts - 1)],
            )
        )
        own_copies.append(pltpu.make_async_copy(sums.at[m], back_out.at[w, m], local.at[5 + w]))
        own_copies[-1].start()

    fv_grad1 = ff_grad_start(0, cg, hid)

    for copy in fv_second:
        copy.wait_recv()
    first3 = []
    for b in both:
        rs = bucket_rows(b)
        for j in range(4):
            cols = slice(j * block, (j + 1) * block)
            part[1, rs, cols] = nt(hid[rs], fv_piece(j)[...]).astype(BF)
        first3.append(scatter_start(1, b, part.at[1], moved_lanes))
    second3 = []
    for b in both:
        rs = bucket_rows(b)
        total = nn(cg[rs, 0:block], fv[...])
        for j in range(1, 4):
            total = total + nn(cg[rs, j * block : (j + 1) * block], fvb[j - 1])
        pre[rs] = (total * 2.0 * pos[rs].astype(F32)).astype(BF)
        second3.append(scatter_middle(1, b, part.at[1], moved_lanes, first3[b]))
    fk_grad1 = ff_grad_start(1, kin, pre)
    sens[...] = jnp.zeros_like(sens)
    head_small[...] = jnp.zeros_like(head_small)
    gate_first = []
    for b in both:
        rs = bucket_rows(b)
        gate = channel_gate[rs]
        total = scatter_end(1, b, part.at[1], moved_lanes, first3[b], second3[b])
        out_own[rs] = ((mid_own[rs] + gate * total) * masks[b][4]).astype(BF)
        gig[rs] = (top(b) * total * gate * (1.0 - gate)).astype(BF)
    tm_grad_start(4)

    ones = jnp.ones((8, own), BF)

    def back_mix(k, b, target, take, mean, rstd, gain_row, mix_row, sens_row, grads):
        rs = bucket_rows(b)
        same, following = masks[b][2], masks[b][3]
        average, scale = mean[rs, :], rstd[rs, :]
        one, two = jnp.zeros((8, rows), F32), jnp.zeros((8, rows), F32)
        for e in range(parts):
            cols = slice(e * own, (e + 1) * own)
            hat = (take(rs, e).astype(F32) - average) * scale
            gain = order_vec[gain_row : gain_row + 1, cols]
            normed = hat * gain
            change = normed - roll_rows(normed, 1) * same
            now = jnp.zeros((rows, own), F32)
            whole = jnp.zeros((rows, own), F32)
            for i, (grad, weight_of) in enumerate(grads):
                value = nt(grad(rs), weight_of(e))
                at = slice(sens_row + i, sens_row + i + 1)
                sens[at, cols] += jnp.sum(value * change, axis=0, keepdims=True)
                weight = order_vec[mix_row + i : mix_row + i + 1, cols]
                now = now + value * weight
                whole = whole + value
            back = now + following * roll_rows(whole - now, -1)
            target[rs, cols] = back.astype(BF)
            scaled = back * gain
            one = one + nt(ones, scaled.astype(BF))
            two = two + nt(ones, (scaled * hat).astype(BF))
        small[k, b, 0, 0:8] = one
        small[k, b, 0, 8:16] = two

    def piece_rows(e):
        return slice((e % 2) * own, (e % 2 + 1) * own)

    def take_mid_own(rs, e):
        return mid[rs, e * own : (e + 1) * own]

    def take_x_own(rs, e):
        start = pl.multiple_of(order[e // 2] * block + (e % 2) * own, own)
        return x_ref[rs, pl.ds(start, own)]

    def fk_rows(e):
        return fk_piece(e // 2)[piece_rows(e)]

    def g_rows(w):
        return lambda e: g[e // 2, w, piece_rows(e)]

    for copies in first1 + second1:
        for copy in copies:
            links.sent(copy)
    first4, stats4 = [], []
    for b in both:
        back_mix(
            0, b, part.at[0], take_mid_own, mean2, rstd2, CLOSING, CLOSING + 1, 4,
            [(lambda rs: pre[rs], fk_rows), (lambda rs: gig[rs], g_rows(4))],
        )
        first4.append(scatter_start(2, b, part.at[0], moved_lanes))
        stats4.append(stats_start(0, b))
    second4, stats4b = [], []
    for b in both:
        second4.append(scatter_middle(2, b, part.at[0], moved_lanes, first4[b]))
        stats4b.append(stats_middle(0, b, stats4[b]))
    ff_grad_middle(0, cg, hid, fv_grad1)
    fv_grad2 = ff_grad_relay(0)

    def norm_back(b, back, hat, gain_row, rstd, means):
        gain = vec[gain_row : gain_row + 1, own_lanes(m)]
        return (back * gain - means[0] - hat * means[1]) * rstd[bucket_rows(b), :]

    closing = jnp.zeros((1, own), F32)
    gathers = []
    for b in both:
        rs = bucket_rows(b)
        back = scatter_end(2, b, part.at[0], moved_lanes, first4[b], second4[b])
        means = stats_end(0, b, stats4b[b])
        hat = (mid_own_b[rs].astype(F32) - mean2[rs, :]) * rstd2[rs, :]
        closing = closing + jnp.sum(back * hat, axis=0, keepdims=True)
        value = top(b) + norm_back(b, back, hat, CLOSING, rstd2, means)
        middle_grad[rs] = value
        branch_own[rs] = value.astype(BF)
        gathers.append(gather_start(branch_own, branch, own_lanes, slices[b]))
    onward = [gather_middle(branch, own_lanes, slices[b], gathers[b]) for b in both]
    out_first = gather_start(out_own, out_full, own_lanes, all_rows, keep=11)

    def time_backward(b):
        rs = bucket_rows(b)
        allowed = allowed_pairs(b)
        for p in range(pairs):
            cols = slice(p * 128, (p + 1) * 128)
            out_scale, in_scale = decay_scales(cols)
            u, gn = head_vec[REWARD : REWARD + 1, cols], head_vec[LANE : LANE + 1, cols]
            g_in, gate, n = mixed_grad[rs, cols], gate_raw[rs, cols], n_ref[rs, cols]
            sg = jax.nn.sigmoid(gate)
            silu = gate * sg
            time_grads[3, rs, cols] = (g_in * n * gn * sg * (1.0 + gate * (1.0 - sg))).astype(BF)
            q = g_in * gn * silu
            dout = q - head_sums(q, low) / LANE_WIDTH - n * (head_sums(q * n, low) / LANE_WIDTH)
            dout = dout * n_scale[rs, cols]
            r, k = rkv[0, rs, cols].astype(F32), rkv[1, rs, cols].astype(F32)
            v = rkv[2, rs, cols]
            rt, kt = r * out_scale, (k * in_scale).astype(BF)
            rtb = rt.astype(BF)
            now = r * u * k
            diag = head_sums(dout * v.astype(F32), low)
            found = []
            for mine in (low, jnp.logical_not(low)):
                dmine = jnp.where(mine, dout, 0.0).astype(BF)
                scores = scores_of(rt, kt, now, mine, allowed)
                a = jnp.where(allowed, nt(dmine, v), 0.0).astype(BF)
                found.append((tn(scores, dmine), nn(a, kt), tn(a, rtb)))
            dv, drt, dkt = (jnp.where(low, one, two) for one, two in zip(*found))
            time_grads[0, rs, cols] = (drt * out_scale + u * k * diag).astype(BF)
            time_grads[1, rs, cols] = (dkt * in_scale + u * r * diag).astype(BF)
            time_grads[2, rs, cols] = dv.astype(BF)
            lags = places * rtb.astype(F32) * drt - (places + 1.0) * kt.astype(F32) * dkt
            log_decay = -jnp.exp(head_vec[FADING : FADING + 1, cols])
            head_small[0:1, cols] += jnp.sum(lags, axis=0, keepdims=True) * log_decay
            head_small[1:2, cols] += jnp.sum(r * k * diag, axis=0, keepdims=True)
            head_small[2:3, cols] += jnp.sum(g_in * n * silu, axis=0, keepdims=True)

    for copies in first3 + second3:
        for copy in copies:
            links.sent(copy)
    wo_second = []
    left, right = pl.ds(0, width // 2), pl.ds(width // 2, width // 2)
    first6, stats6 = [], []
    for b in both:
        gather_end(gathers[b], onward[b])
        rs = bucket_rows(b)
        if b == 1:
            for j in range(4):
                wo_part[j] = tn(mixed[:, j * LANE_WIDTH : (j + 1) * LANE_WIDTH], branch[...]).astype(BF)
            wo_first = [
                links.push(wo_part.at[peer[0], :, lanes], wo_got.at[way, i], way_peer)
                for way, lanes, way_peer, near in ((0, left, x_peer, x_peer), (1, right, y_peer, y_peer))
                for i, peer in enumerate((near, diagonal))
            ]
        mixed_grad[rs] = nt(branch[rs], wob[...])
        time_backward(b)
        back_mix(
            1, b, part.at[1], take_x_own, mean1, rstd1, OPENING, OPENING + 1, 0,
            [((lambda rs, w=w: time_grads[w, rs]), g_rows(w)) for w in range(4)],
        )
        first6.append(scatter_start(3, b, part.at[1], moved_lanes))
        stats6.append(stats_start(1, b))

    for w in (0, 1):
        tm_grad_start(w)
    vec_copies = links.group(
        [sens.at[:, moved_lanes(other)] for other in others],
        [u_got.at[i] for i in range(parts - 1)],
        [(d, other) for other in others],
        u_got,
    )
    second6, stats6b = [], []
    for b in both:
        second6.append(scatter_middle(3, b, part.at[1], moved_lanes, first6[b]))
        stats6b.append(stats_middle(1, b, stats6[b]))
    out_second = gather_middle(out_full, own_lanes, all_rows, out_first)
    tm_grad_middle(4)
    ff_grad_middle(1, kin, pre, fk_grad1)
    for way, (lanes, near, peer) in enumerate(((left, y_peer, y_peer), (right, x_peer, x_peer))):
        for copy in wo_first[2 * way : 2 * way + 2]:
            copy.wait_recv()
        value = wo_part[near[0], :, lanes].astype(F32) + wo_got[way, 1].astype(F32)
        wo_send[way] = value.astype(BF)
        wo_second.append(links.push(wo_send.at[way], wo_got2.at[way], peer))
    opening = jnp.zeros((1, own), F32)
    for b in both:
        rs = bucket_rows(b)
        back = scatter_end(3, b, part.at[1], moved_lanes, first6[b], second6[b])
        means = stats_end(1, b, stats6b[b])
        hat = (x_ref[rs, own_lanes(m)].astype(F32) - mean1[rs, :]) * rstd1[rs, :]
        opening = opening + jnp.sum(back * hat, axis=0, keepdims=True)
        value = middle_grad[rs] + norm_back(b, back, hat, OPENING, rstd1, means)
        gin_own[rs] = value.astype(BF)
    gin_first = gather_start(gin_own, gin_full, own_lanes, all_rows, keep=10)
    tm_grad_middle(0)
    tm_grad_start(2)
    tm_grad_middle(1)
    tm_grad_start(3)
    tm_grad_end(4)
    gin_second = gather_middle(gin_full, own_lanes, all_rows, gin_first)

    vec_copies.wait_recv()
    total = sens[:, moved_lanes(m)]
    for i in range(parts - 1):
        total = total + u_got[i]
    u2_own[0:8] = total
    u2_own[6:7] = opening
    u2_own[7:8] = closing
    u2_own[8:16] = head_small[...]
    dp_copies = links.group(
        [u2_own] * 3, [u2_got.at[i] for i in range(3)], [x_peer, y_peer, diagonal], u2_got
    )
    tm_grad_end(0)
    tm_grad_middle(2)
    tm_grad_middle(3)
    tm_grad_end(1)
    tm_grad_end(2)
    fk_grad2 = ff_grad_relay(1)
    dp_copies.wait_recv()
    u3_own[...] = (u2_own[...] + u2_got[0]) + (u2_got[1] + u2_got[2])
    all_copies = links.group(
        [u3_own] * (parts - 1),
        [u3_got.at[m]] * (parts - 1),
        [(d, other) for other in others],
        u3_got.at[pl.ds(0, parts - 1)],
    )
    u3_got[m] = u3_own[...]

    tm_grad_end(3)
    ff_grad_end(0, cg, hid, fv_grad2, ffv_out)
    for way, lanes in enumerate((left, right)):
        wo_second[way].wait_recv()
        total = wo_part[d, :, lanes].astype(F32) + wo_got[way, 0].astype(F32) + wo_got2[way].astype(F32)
        wo_out[:, lanes] = total.astype(BF)
    ff_grad_end(1, kin, pre, fk_grad2, ffk_out)
    all_copies.wait_recv()
    upper_d = lax.rem(d, 2) == 1
    low_vec = lax.broadcasted_iota(jnp.int32, (8, 128), 1) < LANE_WIDTH
    for e in range(2):
        vec_out[0:8, e * own : (e + 1) * own] = u3_got[2 * d + e, 0:8]
    for u in range(4):
        lanes = pl.ds(pl.multiple_of(lax.div(d, 2) * 128, 128), 128)
        first, second = u3_got[2 * u, 8:16, lanes], u3_got[2 * u + 1, 8:16, lanes]
        first = jnp.where(upper_d, swap_halves(first), first)
        second = jnp.where(upper_d, second, swap_halves(second))
        vec_out[8:16, u * 128 : (u + 1) * 128] = jnp.where(low_vec, first, second)
    gather_end(gin_first, gin_second)
    gather_end(out_first, out_second)
    for copy in back_copies:
        copy.wait_recv()
    for copy in own_copies:
        copy.wait()
    links.finish()
    assert links.used == COPIES, links.used


def finish_kernel(
    out, gin, ffk, ffv, back, wo, vec,
    out_o, gin_o, ffk_o, ffv_o, r_o, k_o, v_o, g_o, c_o, wo_o,
    y0, y1, y2, y3, y4, y5, y6, y7, y8, y9, y10,
    out_v, gin_v, ffk_v, ffv_v, back_v, wo_v, ffk_f, ffv_f, square, read, write,
):
    buckets, rows = out_o.shape[:2]
    reads = [
        pltpu.make_async_copy(a, b, read.at[i])
        for i, (a, b) in enumerate(
            ((ffv, ffv_v), (ffk, ffk_v), (wo, wo_v), (back, back_v), (out, out_v), (gin, gin_v))
        )
    ]
    for copy in reads:
        copy.start()
    writes = []

    def store(source, target):
        copy = pltpu.make_async_copy(source, target, write.at[len(writes)])
        copy.start()
        writes.append(copy)

    for i, ref in enumerate((y0, y1, y2, y3, y4, y5, y6, y7, y8, y9, y10)):
        ref[...] = vec[i : i + 1]
    for copy, source, middle, target in zip(reads, (ffv_v, ffk_v, wo_v), (ffv_f, ffk_f, square.at[5]), (ffv_o, ffk_o, wo_o)):
        copy.wait()
        middle[...] = source[...].astype(F32)
        store(middle, target)
    reads[3].wait()
    parts, shard, own = back_v.shape[1:]
    low = lax.broadcasted_iota(jnp.int32, (shard, 128), 1) < LANE_WIDTH
    for to in range(parts):
        square[4, :, to * own : (to + 1) * own] = back_v[4, to].astype(F32)
    store(square.at[4], c_o)
    for w, target in enumerate((r_o, k_o, v_o, g_o)):
        for j in range(4):
            for u in range(4):
                lanes = slice((j // 2) * 128, (j // 2 + 1) * 128)
                first = back_v[w, 2 * u, :, lanes].astype(F32)
                second = back_v[w, 2 * u + 1, :, lanes].astype(F32)
                if j % 2 == 0:
                    tile = jnp.where(low, first, swap_halves(second))
                else:
                    tile = jnp.where(low, swap_halves(first), second)
                start = j * 4 * 128 + u * 128
                square[w, :, start : start + 128] = tile
        store(square.at[w], target)
    for copy, source, target in ((reads[4], out_v, out_o), (reads[5], gin_v, gin_o)):
        copy.wait()
        for b in range(buckets):
            store(source.at[pl.ds(b * rows, rows)], target.at[b])
    for copy in writes:
        copy.wait()


def fast_body(*args):
    (
        block_arguments, bundled_spans, opening_gain, mix_r, mix_k, mix_v, mix_g, w_recept, w_key, w_value, w_gate,
        fading, reward, lane_gain, w_out, closing_gain, mix_fk, mix_fr, fk, fv, w_channel, upstream,
    ) = args
    buckets, bucket_rows, width = block_arguments.shape
    rows = buckets * bucket_rows
    parts, chips = 8, 4
    own, block = width // parts, width // 4
    hidden = fk.shape[1]
    shard = w_out.shape[0]
    vectors = [
        opening_gain, mix_r, mix_k, mix_v, mix_g, closing_gain, mix_fk, mix_fr, fading, reward, lane_gain,
    ]
    vectors = [vector.reshape(1, width) for vector in vectors]
    v, sm = pltpu.VMEM, pltpu.SMEM
    vm = pl.BlockSpec(memory_space=pltpu.VMEM)
    half_block = block // 2
    scratch = [
        v((16, width), F32), v((4, parts, shard, own), BF), v((4, 5, block, own), BF), v((3, block, hidden), BF), v((3, block, hidden), BF),
        v((4 * shard, width), BF), v((4, rows, width), BF), v((rows, 1), F32), v((rows, 1), F32), v((rows, 1), F32),
        v((rows, 1), F32), v((16, width), F32), v((16, own), F32), v((rows, own), BF),
        v((3, rows, own), BF), v((rows, own), F32), v((rows, own), F32), v((rows, own), F32), v((rows, own), BF),
        v((2, rows, width), BF), v((4, buckets, chips, bucket_rows, own), BF),
        v((buckets, chips - 1, bucket_rows, own), BF), v((4, buckets, chips - 1, bucket_rows, own), BF),
        v((2, buckets, chips + 2, 16, bucket_rows), F32),
        v((rows, own), F32), v((rows, own), BF), v((rows, width), BF), v((rows, width), BF), v((rows, width), BF),
        v((rows, hidden), BF), v((rows, hidden), BF), v((rows, hidden), BF), v((rows, own), F32), v((rows, own), BF),
        v((rows, width), BF),
        v((rows, own), BF), v((rows, own), BF), v((rows, own), F32), v((rows, own), BF),
        v((rows, width), BF), v((rows, own), F32), v((4, rows, own), BF), v((8, width), F32), v((8, own), F32),
        v((2, 2, 2, own, hidden), BF), v((2, 2, 2, own, hidden), BF), v((2, 2, own, hidden), BF),
        v((5, 2, 2, own, own), BF), v((5, 2, 2, own, own), BF), v((5, 2, own, own), BF),
        v((parts, shard, own), BF),
        v((4, shard, width), BF), v((2, 2, shard, width // 2), BF), v((2, shard, width // 2), BF),
        v((2, shard, width // 2), BF), v((rows, own), BF),
        v((parts - 1, 8, own), F32), v((16, own), F32), v((3, 16, own), F32), v((16, own), F32),
        v((parts, 16, own), F32),
        pltpu.SemaphoreType.DMA((COPIES,)), pltpu.SemaphoreType.DMA((COPIES,)), pltpu.SemaphoreType.DMA((12,)),
    ]
    out = pl.pallas_call(
        block_kernel,
        out_shape=[
            struct((rows, width), BF), struct((rows, width), BF), struct((block, hidden), BF),
            struct((block, hidden), BF), struct((5, parts, shard, own), BF), struct((shard, width), BF),
            struct((16, block), F32),
        ],
        in_specs=[pl.BlockSpec(memory_space=sm), vm, pl.BlockSpec(memory_space=pl.ANY)] + [vm] * 19,
        out_specs=[pl.BlockSpec(memory_space=pl.ANY)] * 5 + [vm] * 2,
        scratch_shapes=scratch,
        compiler_params=pltpu.CompilerParams(
            collective_id=0, has_side_effects=True, vmem_limit_bytes=VMEM_LIMIT
        ),
        name="whole_block",
    )(
        bundled_spans.reshape(buckets, -1), block_arguments.reshape(rows, width), upstream.reshape(rows, width), *vectors,
        w_recept, w_key, w_value, w_gate, w_out, w_channel, fk, fv,
    )
    square = struct((shard, width), F32)
    hbm = pl.BlockSpec(memory_space=pl.ANY)
    done = pl.pallas_call(
        finish_kernel,
        out_shape=[
            struct(block_arguments.shape, BF), struct(block_arguments.shape, BF), struct(fk.shape, F32),
            struct(fv.shape, F32), square, square, square, square, square, square,
        ]
        + [struct((1, block), F32)] * 11,
        in_specs=[hbm] * 6 + [vm],
        out_specs=[hbm] * 10 + [vm] * 11,
        scratch_shapes=[
            v((rows, width), BF), v((rows, width), BF), v(fk.shape, BF), v(fv.shape, BF), v((5, parts, shard, own), BF), v((shard, width), BF),
            v(fk.shape, F32), v(fv.shape, F32), v((6, shard, width), F32),
            pltpu.SemaphoreType.DMA((6,)), pltpu.SemaphoreType.DMA((2 * buckets + 8,)),
        ],
        compiler_params=pltpu.CompilerParams(vmem_limit_bytes=VMEM_LIMIT),
        name="finish",
    )(*out)
    outputs, grad_inputs, d_fk, d_fv, d_r, d_k, d_v, d_g, d_c, d_o = done[:10]
    small = [vector.reshape(block) for vector in done[10:]]
    return (
        outputs, grad_inputs, small[6], small[0], small[1], small[2], small[3], d_r, d_k, d_v, d_g,
        small[8], small[9], small[10], d_o, small[7], small[4], small[5], d_fk, d_fv, d_c,
    )


def body(*args):
    data_parts, parts = lax.axis_size("dp"), lax.axis_size("mp")
    width, shard, hidden = args[0].shape[2], args[7].shape[0], args[18].shape[1]
    fitted = (
        data_parts == 4
        and parts == 8
        and shard == LANE_WIDTH
        and width == 4 * parts * shard
        and hidden % 128 == 0
        and args[0].shape[:2] == (2, 128)
    )
    return fast_body(*args) if fitted else general_body(*args)


def solution(mesh):
    return jax.shard_map(
        body,
        mesh=mesh,
        in_specs=(
            P(None, "dp", None),
            P(None, "dp", None),
            P(),
            P(),
            P(),
            P(),
            P(),
            P(("dp", "mp"), None),
            P(("dp", "mp"), None),
            P(("dp", "mp"), None),
            P(("dp", "mp"), None),
            P(),
            P(),
            P(),
            P(("dp", "mp"), None),
            P(),
            P(),
            P(),
            P("dp", "mp"),
            P("dp", "mp"),
            P(("dp", "mp"), None),
            P(None, "dp", None),
        ),
        out_specs=(
            P(None, "dp", None),
            P(None, "dp", None),
            P("dp"),
            P("dp"),
            P("dp"),
            P("dp"),
            P("dp"),
            P(("dp", "mp"), None),
            P(("dp", "mp"), None),
            P(("dp", "mp"), None),
            P(("dp", "mp"), None),
            P("dp"),
            P("dp"),
            P("dp"),
            P(("dp", "mp"), None),
            P("dp"),
            P("dp"),
            P("dp"),
            P("dp", "mp"),
            P("dp", "mp"),
            P(("dp", "mp"), None),
        ),
        check_vma=False,
    )
```

```python
import functools
from functools import reduce

import jax
import jax.numpy as jnp
from jax import lax
from jax.experimental import pallas as pl
from jax.experimental.pallas import tpu as pltpu
from jax.sharding import PartitionSpec as P

LANE_WIDTH = 64
SPAN = 64


EPSILON = 1e-05
GROUP_EPSILON = 0.25
MIXED_MODE = lax.Precision.HIGH


def shortened(x):
    return jax.tree.map(lambda a: a.astype(jnp.bfloat16) if a.dtype == jnp.float32 else a, x)


def product(first_operand, second_operand):
    return jnp.dot(first_operand, second_operand, preferred_element_type=jnp.float32)


def product_rows(first_operand, second_operand):
    return lax.dot_general(
        first_operand, second_operand, (((0,), (0,)), ((), ())), preferred_element_type=jnp.float32
    )


def product_back(first_operand, second_operand):
    return lax.dot_general(
        first_operand, second_operand, (((1,), (1,)), ((), ())), preferred_element_type=jnp.float32
    )


def layer_norm(values, gain_entries):
    average = jnp.mean(values, axis=-1, keepdims=True)
    centered = values - average
    spread = jnp.mean(centered * centered, axis=-1, keepdims=True)
    return centered * lax.rsqrt(spread + EPSILON) * gain_entries


def group_norm(values, head_count):
    grouped = values.reshape(values.shape[0], head_count, -1)
    average = jnp.mean(grouped, axis=-1, keepdims=True)
    centered = grouped - average
    spread = jnp.mean(centered * centered, axis=-1, keepdims=True)
    return (centered * lax.rsqrt(spread + GROUP_EPSILON)).reshape(values.shape)


def segment_info(lengths, row_count):
    segment_ends = jnp.cumsum(lengths)
    places = jnp.arange(row_count, dtype=jnp.int32)
    sequence_label = jnp.sum((places[:, None] >= segment_ends[None, :]).astype(jnp.int32), axis=1)
    earlier = jnp.concatenate([jnp.full((1,), -1, jnp.int32), sequence_label[:-1]])
    common_series_filter = (sequence_label == earlier).astype(jnp.float32)
    valid_rows = (places < segment_ends[-1]).astype(jnp.float32)
    return (sequence_label, common_series_filter, valid_rows)


def shift_rows(values, common_series_filter):
    before = jnp.concatenate([jnp.zeros_like(values[:1]), values[:-1]], axis=0)
    return before * common_series_filter[:, None]


def iterative_renewal(
    accept_lines,
    lookup_weight_lines,
    payload_weight_lines,
    decay_logarithm,
    reward_scaler,
    sequence_label,
    layer_rows,
):
    row_count, head_count, head_width = accept_lines.shape
    block_count = row_count // layer_rows
    blocked = (block_count, layer_rows, head_count, head_width)
    accept_blocks = accept_lines.reshape(blocked)
    lookup_blocks = lookup_weight_lines.reshape(blocked)
    payload_blocks = payload_weight_lines.reshape(blocked)
    segment_blocks = sequence_label.reshape(block_count, layer_rows)
    positions = jnp.arange(layer_rows, dtype=jnp.float32)
    middle_step = float(layer_rows // 2)
    query_scale = jnp.exp(decay_logarithm[None] * (positions - middle_step)[:, None, None])
    key_scale = jnp.exp(decay_logarithm[None] * (middle_step - 1.0 - positions)[:, None, None])
    scores = jnp.einsum(
        "cthi,cshi->chts",
        accept_blocks * query_scale,
        lookup_blocks * key_scale,
        precision=MIXED_MODE,
    )
    causal = positions[:, None] > positions[None, :]
    within = segment_blocks[:, :, None] == segment_blocks[:, None, :]
    allowed = jnp.logical_and(causal[None], within).astype(jnp.float32)
    scores = scores * allowed[:, None]
    nested_routine = jnp.einsum("chts,cshj->cthj", scores, payload_blocks, precision=MIXED_MODE)
    reward_term = jnp.sum(accept_blocks * reward_scaler * lookup_blocks, axis=-1)
    nested_routine = nested_routine + reward_term[..., None] * payload_blocks
    last_segment = segment_blocks[:, -1]
    prior_segment = jnp.concatenate([jnp.full((1,), -1, jnp.int32), last_segment[:-1]])
    tail_scale = jnp.exp(decay_logarithm[None] * (layer_rows - 1.0 - positions)[:, None, None])
    tail_keep = (segment_blocks == last_segment[:, None]).astype(jnp.float32)
    added_state = jnp.einsum(
        "cshi,cshj->chij",
        lookup_blocks * tail_scale * tail_keep[:, :, None, None],
        payload_blocks,
        precision=MIXED_MODE,
    )
    carry_keep = (last_segment == prior_segment).astype(jnp.float32)
    whole_decay = jnp.exp(decay_logarithm * layer_rows)

    def advance(carry_state, piece_pair):
        addition, keep_flag = piece_pair
        return (whole_decay[:, :, None] * carry_state * keep_flag + addition, carry_state)

    initial = jnp.zeros((head_count, head_width, head_width), jnp.float32)
    unused, starts = lax.scan(advance, initial, (added_state, carry_keep))
    entry_keep = (segment_blocks == prior_segment[:, None]).astype(jnp.float32)
    entry_scale = jnp.exp(decay_logarithm[None] * positions[:, None, None])
    outside = jnp.einsum(
        "cthi,chij->cthj",
        accept_blocks * entry_scale * entry_keep[:, :, None, None],
        starts,
        precision=MIXED_MODE,
    )
    return (nested_routine + outside).reshape(row_count, head_count, head_width)


def add_terms(first_terms, second_terms):
    return jax.tree.map(jnp.add, first_terms, second_terms)


def general_body(
    block_arguments,
    bundled_spans,
    opening_normalize_scale,
    accept_lagmix,
    lookup_lagmix,
    payload_lagmix,
    valve_lagmix,
    accept_weights,
    lookup_weights,
    payload_weights,
    valve_weights,
    fading_speed_logs,
    present_reward,
    lane_normalize_scale,
    emission_weights,
    closing_normalize_scale,
    feedforward_lookup_lagmix,
    feedforward_accept_lagmix,
    feedforward_lookup_weights,
    feedforward_payload_weights,
    feedforward_accept_weights,
    upstream_sensitivity,
):
    micro_count, row_count, model_width = block_arguments.shape
    layer_rows = SPAN
    data_parts = lax.axis_size("dp")
    model_parts = lax.axis_size("mp")
    shard_rows = accept_weights.shape[0]
    model_place = lax.axis_index("mp")
    partition_lanes = model_width // LANE_WIDTH

    def own_columns(values):
        split_values = values.reshape(row_count, data_parts, model_parts, shard_rows)
        picked = lax.dynamic_index_in_dim(split_values, model_place, axis=2, keepdims=False)
        return picked.reshape(row_count, data_parts * shard_rows)

    outputs_list = []
    input_grads = []
    gradient_terms = []
    for micro_index in range(micro_count):
        projections = (
            lax.all_gather(accept_weights, ("dp", "mp"), axis=0, tiled=True),
            lax.all_gather(lookup_weights, ("dp", "mp"), axis=0, tiled=True),
            lax.all_gather(payload_weights, ("dp", "mp"), axis=0, tiled=True),
            lax.all_gather(valve_weights, ("dp", "mp"), axis=0, tiled=True),
            lax.all_gather(emission_weights, ("dp", "mp"), axis=0, tiled=True),
            lax.all_gather(feedforward_accept_weights, ("dp", "mp"), axis=0, tiled=True),
        )
        hidden_pair = (
            lax.all_gather(feedforward_lookup_weights, "dp", axis=0, tiled=True),
            lax.all_gather(feedforward_payload_weights, "dp", axis=0, tiled=True),
        )
        full_recept, full_key, full_value, full_gate, full_output, full_channel = projections
        hidden_key, hidden_value = hidden_pair
        sequence_label, common_series_filter, valid_rows = segment_info(
            bundled_spans[micro_index, 0], row_count
        )
        rows_float = block_arguments[micro_index].astype(jnp.float32)

        def front_part(rows_value, gain_entries, recept_mix, key_mix, value_mix, gate_mix):
            normed = layer_norm(rows_value, gain_entries)
            before = shift_rows(normed, common_series_filter)
            return tuple(
                (
                    normed * weight_mix + before * (1.0 - weight_mix)
                    for weight_mix in (recept_mix, key_mix, value_mix, gate_mix)
                )
            )

        front_values, front_pull = jax.vjp(
            front_part,
            rows_float,
            opening_normalize_scale,
            accept_lagmix,
            lookup_lagmix,
            payload_lagmix,
            valve_lagmix,
        )
        recept_in, key_in, value_in, gate_in = [
            front_piece.astype(jnp.bfloat16) for front_piece in front_values
        ]
        accept_lines = product(recept_in, full_recept).astype(jnp.bfloat16)
        lookup_weight_lines = product(key_in, full_key).astype(jnp.bfloat16)
        payload_weight_lines = product(value_in, full_value).astype(jnp.bfloat16)
        gate_raw = product(gate_in, full_gate)

        def middle_part(
            receptance_activation,
            key_value_product,
            value_activation,
            gate_activation,
            decay_parameter,
            reward_weight,
            gain_entries,
        ):
            decay_logarithm = -jnp.exp(decay_parameter).reshape(partition_lanes, -1)
            reward_scaler = reward_weight.reshape(partition_lanes, -1)
            reformed_array = (row_count, partition_lanes, model_width // partition_lanes)
            lane_answers = iterative_renewal(
                receptance_activation.reshape(reformed_array),
                key_value_product.reshape(reformed_array),
                value_activation.reshape(reformed_array),
                decay_logarithm,
                reward_scaler,
                sequence_label,
                layer_rows,
            )
            grouped = (
                group_norm(lane_answers.reshape(row_count, model_width), partition_lanes)
                * gain_entries
            )
            return grouped * jax.nn.silu(gate_activation)

        mixed_float, middle_pull = jax.vjp(
            middle_part,
            accept_lines.astype(jnp.float32),
            lookup_weight_lines.astype(jnp.float32),
            payload_weight_lines.astype(jnp.float32),
            gate_raw,
            fading_speed_logs,
            present_reward,
            lane_normalize_scale,
        )
        merged_lanes = mixed_float.astype(jnp.bfloat16)
        middle = rows_float + product(merged_lanes, full_output)

        def back_part(middle_value, gain_entries, key_mix, recept_mix):
            normed = layer_norm(middle_value, gain_entries)
            before = shift_rows(normed, common_series_filter)
            return (
                normed * key_mix + before * (1.0 - key_mix),
                normed * recept_mix + before * (1.0 - recept_mix),
            )

        channel_values, back_pull = jax.vjp(
            back_part,
            middle,
            closing_normalize_scale,
            feedforward_lookup_lagmix,
            feedforward_accept_lagmix,
        )
        channel_key_in = channel_values[0].astype(jnp.bfloat16)
        channel_recept_in = channel_values[1].astype(jnp.bfloat16)
        hidden_input = product(channel_key_in, hidden_key)
        hidden = jnp.square(jnp.maximum(hidden_input, 0.0)).astype(jnp.bfloat16)
        carried = lax.psum(product_back(hidden, hidden_value).astype(jnp.bfloat16), "mp").astype(
            jnp.float32
        )
        channel_gate = jax.nn.sigmoid(product(channel_recept_in, full_channel))
        outputs_list.append(
            ((middle + channel_gate * carried) * valid_rows[:, None]).astype(jnp.bfloat16)
        )
        top_grad = upstream_sensitivity[micro_index].astype(jnp.float32) * valid_rows[:, None]
        carried_grad = (top_grad * channel_gate).astype(jnp.bfloat16)
        gate_input_grad = (top_grad * carried * channel_gate * (1.0 - channel_gate)).astype(
            jnp.bfloat16
        )
        pre_grad = (
            product(carried_grad, hidden_value) * 2.0 * jnp.maximum(hidden_input, 0.0)
        ).astype(jnp.bfloat16)
        channel_key_grad = lax.psum(
            product_back(pre_grad, hidden_key).astype(jnp.bfloat16), "mp"
        ).astype(jnp.float32)
        channel_recept_grad = product_back(gate_input_grad, full_channel)
        middle_back, grad_second, feedforward_lookup_lagmix_sens, feedforward_accept_lagmix_sens = (
            back_pull((channel_key_grad, channel_recept_grad))
        )
        middle_grad = top_grad + middle_back
        branch_grad = middle_grad.astype(jnp.bfloat16)
        mixed_grad = product_back(branch_grad, full_output)
        output_term = product_rows(own_columns(merged_lanes), branch_grad)
        (
            receptance_single_precision,
            key_single_precision,
            value_single_precision,
            gate_single_precision,
            decay_gradient,
            reward_derivative,
            lane_normalize_derivative,
        ) = middle_pull(mixed_grad)
        recept_grad = receptance_single_precision.astype(jnp.bfloat16)
        key_grad = key_single_precision.astype(jnp.bfloat16)
        value_grad = value_single_precision.astype(jnp.bfloat16)
        gate_grad = gate_single_precision.astype(jnp.bfloat16)
        (
            line_derivatives,
            grad_first,
            grad_recept_mix,
            grad_key_mix,
            grad_value_mix,
            grad_gate_mix,
        ) = front_pull(
            (
                product_back(recept_grad, full_recept),
                product_back(key_grad, full_key),
                product_back(value_grad, full_value),
                product_back(gate_grad, full_gate),
            )
        )
        projection_terms = (
            product_rows(own_columns(recept_in), recept_grad),
            product_rows(own_columns(key_in), key_grad),
            product_rows(own_columns(value_in), value_grad),
            product_rows(own_columns(gate_in), gate_grad),
            output_term,
        )
        input_grads.append((middle_grad + line_derivatives).astype(jnp.bfloat16))
        local_terms = (
            grad_first,
            grad_recept_mix,
            grad_key_mix,
            grad_value_mix,
            grad_gate_mix,
            decay_gradient,
            reward_derivative,
            lane_normalize_derivative,
            grad_second,
            feedforward_lookup_lagmix_sens,
            feedforward_accept_lagmix_sens,
            product_rows(channel_key_in, pre_grad),
            product_rows(carried_grad, hidden),
            product_rows(own_columns(channel_recept_in), gate_input_grad),
        ) + projection_terms
        gradient_terms.append(local_terms)
    summed = reduce(add_terms, gradient_terms)
    summed = jax.tree.map(
        lambda part: part.astype(jnp.float32),
        lax.psum_scatter(shortened(summed), "dp", scatter_dimension=0, tiled=True),
    )
    (
        grad_first,
        grad_recept_mix,
        grad_key_mix,
        grad_value_mix,
        grad_gate_mix,
        decay_gradient,
        reward_derivative,
        lane_normalize_derivative,
        grad_second,
        feedforward_lookup_lagmix_sens,
        feedforward_accept_lagmix_sens,
        feedforward_lookup_derivative,
        feedforward_payload_derivative,
        feedforward_accept_derivative,
        grad_recept,
        grad_key,
        grad_value,
        grad_gate,
        grad_output,
    ) = summed
    return (
        jnp.stack(outputs_list),
        jnp.stack(input_grads),
        grad_first,
        grad_recept_mix,
        grad_key_mix,
        grad_value_mix,
        grad_gate_mix,
        grad_recept,
        grad_key,
        grad_value,
        grad_gate,
        decay_gradient,
        reward_derivative,
        lane_normalize_derivative,
        grad_output,
        grad_second,
        feedforward_lookup_lagmix_sens,
        feedforward_accept_lagmix_sens,
        feedforward_lookup_derivative,
        feedforward_payload_derivative,
        feedforward_accept_derivative,
    )


MESH = pl.DeviceIdType.MESH
BF = jnp.bfloat16
F32 = jnp.float32
VMEM_LIMIT = 63 << 20
OPENING, CLOSING, FADING, REWARD, LANE = 0, 5, 8, 9, 10


def struct(shape, dtype):
    return jax.ShapeDtypeStruct(shape, dtype)


def flip(place, other):
    low = lax.rem(lax.rem(place, 2) + lax.rem(other, 2), 2)
    high = lax.rem(lax.div(place, 2) + lax.div(other, 2), 2)
    return 2 * high + low


def nt(a, b):
    return lax.dot_general(a, b, (((1,), (1,)), ((), ())), preferred_element_type=F32)


def tn(a, b):
    return lax.dot_general(a, b, (((0,), (0,)), ((), ())), preferred_element_type=F32)


def nn(a, b):
    return lax.dot_general(a, b, (((1,), (0,)), ((), ())), preferred_element_type=F32)


def roll_rows(values, shift):
    return pltpu.roll(values, shift % values.shape[0], 0)


def swap_halves(tile):
    return pltpu.roll(tile, LANE_WIDTH, 1)


def head_sums(values, low):
    first = jnp.sum(jnp.where(low, values, 0.0), axis=1, keepdims=True)
    second = jnp.sum(jnp.where(low, 0.0, values), axis=1, keepdims=True)
    return jnp.where(low, first, second)


class Links:
    def __init__(self, send, recv):
        self.send, self.recv = send, recv
        self.used = 0
        self.open = []

    def push(self, source, target, peer):
        i = self.used
        self.used += 1
        copy = pltpu.make_async_remote_copy(
            source, target, self.send.at[i], self.recv.at[i], device_id=peer, device_id_type=MESH
        )
        copy.start()
        self.open.append(copy)
        return copy

    def group(self, sources, targets, peers, whole):
        i = self.used
        self.used += 1
        for source, target, peer in zip(sources, targets, peers):
            pltpu.make_async_remote_copy(
                source, target, self.send.at[i], self.recv.at[i], device_id=peer, device_id_type=MESH
            ).start()
        copy = pltpu.make_async_remote_copy(
            whole, whole, self.send.at[i], self.recv.at[i], device_id=peers[0], device_id_type=MESH
        )
        self.open.append(copy)
        return copy

    def sent(self, copy):
        if any(other is copy for other in self.open):
            copy.wait_send()
            self.open = [other for other in self.open if other is not copy]

    def finish(self):
        for copy in self.open:
            copy.wait_send()


COPIES = 204


def block_kernel(
    spans, x_ref, up_ref, v0, v1, v2, v3, v4, v5, v6, v7, v8, v9, v10, w_recept, w_key, w_value, w_gate, w_out, w_channel, fk, fv,
    out_full, gin_full, ffk_out, ffv_out, back_out, wo_out, vec_out,
    vec, blocks, g, fkb, fvb, wob, acts, mean1, rstd1, mean2, rstd2, order_vec, head_vec, seen,
    rkv, gate_raw, n_ref, n_scale, mixed, part, half, pair, far, small,
    mid_own, mid_own_b, mid, kin, cri, hid, pos, pre, channel_gate, cg_own, cg,
    out_own, gig, middle_grad, branch_own, branch, mixed_grad, time_grads, sens, head_small,
    ff_send, ff_got, ff_got2, tm_send, tm_got, tm_got2, channel_sum,
    wo_part, wo_got, wo_send, wo_got2, gin_own, u_got, u2_own, u2_got, u3_own, u3_got,
    send, recv, local,
):
    d, m = lax.axis_index("dp"), lax.axis_index("mp")
    z, c = lax.div(m, 2), lax.rem(m, 2)
    chips, parts = 4, 8
    buckets, rows = 2, x_ref.shape[0] // 2
    width = x_ref.shape[1]
    own = width // parts
    block = width // 4
    shard = w_out.shape[0]
    pairs = own // 128
    links = Links(send, recv)
    mate = (d, 2 * z + 1 - c)
    chips_away = [lax.rem(z + i, chips) for i in range(1, chips)]
    others = [lax.rem(m + i, parts) for i in range(1, parts)]
    x_peer = (d + 1 - 2 * lax.rem(d, 2), m)
    y_peer = (d + 2 - 4 * lax.div(d, 2), m)
    diagonal = (3 - d, m)
    order = [d, x_peer[0], y_peer[0], diagonal[0]]

    def own_lanes(owner):
        return pl.ds(pl.multiple_of(owner * own, own), own)

    def moved_lanes(owner):
        place = 2 * flip(lax.div(owner, 2), d) + lax.rem(owner, 2)
        return pl.ds(pl.multiple_of(place * own, own), own)

    def bucket_rows(b):
        return slice(b * rows, (b + 1) * rows)

    barrier = pltpu.get_barrier_semaphore()
    greeted = [(d, other) for other in others] + [x_peer, y_peer, diagonal]
    for peer in greeted:
        pl.semaphore_signal(barrier, inc=1, device_id=peer, device_id_type=MESH)
    top_copy = pltpu.make_async_copy(up_ref.at[:, own_lanes(m)], seen, local.at[0])
    top_copy.start()
    low16 = lax.broadcasted_iota(jnp.int32, (shard, 128), 1) < LANE_WIDTH
    vec[...] = jnp.zeros_like(vec)
    for i, ref in enumerate((v0, v1, v2, v3, v4, v5, v6, v7, v8, v9, v10)):
        vec[i : i + 1] = ref[...]

    def head_blocks(w, weight):
        for to in range(parts):
            for q in range(pairs):
                tiles = []
                for j in (2 * q, 2 * q + 1):
                    start = j * block + (to // 2) * 128
                    tiles.append(weight[:, start : start + 128].astype(F32))
                if to % 2 == 0:
                    tile = jnp.where(low16, tiles[0], swap_halves(tiles[1]))
                else:
                    tile = jnp.where(low16, swap_halves(tiles[0]), tiles[1])
                blocks[w, to, :, q * 128 : (q + 1) * 128] = tile.astype(BF)

    pl.semaphore_wait(barrier, len(greeted))
    top_copy.wait()

    my_rows = pl.ds(pl.multiple_of(m * shard, shard), shard)

    def exchange(w):
        if w < 4:
            sources = [blocks.at[w, other] for other in others]
        else:
            sources = [w_channel.at[:, own_lanes(other)] for other in others]
        return links.group(
            sources,
            [g.at[0, w, my_rows]] * (parts - 1),
            [(d, other) for other in others],
            g.at[0, w, pl.ds(0, (parts - 1) * shard)],
        )

    half_block = block // 2
    upper_half, lower_half = pl.ds(0, half_block), pl.ds(half_block, half_block)

    def relay_out(source, slot1, slot2, which):
        return (
            links.push(source.at[which], slot1.at[which], x_peer),
            links.push(source.at[which], slot2.at[which], y_peer),
        )

    def forward(upper_copies, lower_copies, slot1, slot2, slot3):
        upper_copies[0].wait_recv()
        one = links.push(slot1.at[upper_half], slot3.at[upper_half], y_peer)
        lower_copies[1].wait_recv()
        two = links.push(slot2.at[lower_half], slot3.at[lower_half], x_peer)
        return (one, two) + (() if upper_copies is lower_copies else (upper_copies[1], lower_copies[0]))

    fk_upper = relay_out(fk, fkb.at[0], fkb.at[1], upper_half)

    def out_rows(dp_place, start, size):
        return pl.ds(pl.multiple_of(dp_place * shard + start, 32), size)

    wo_first = [links.push(w_out, wob.at[out_rows(d, 0, shard)], peer) for peer in (x_peer, y_peer)]
    arrivals = []
    for w, weight in enumerate((w_recept, w_key, w_value, w_gate)):
        head_blocks(w, weight)
        arrivals.append(exchange(w))
    arrivals.append(exchange(4))
    for w in range(4):
        g[0, w, my_rows] = blocks[w, m]
    g[0, 4, my_rows] = w_channel[:, own_lanes(m)]
    wob[out_rows(d, 0, shard)] = w_out[...]

    for j in range(4):
        order_vec[:, j * block : (j + 1) * block] = vec[
            :, pl.ds(pl.multiple_of(order[j] * block, block), block)
        ]
    low_row = lax.broadcasted_iota(jnp.int32, (16, 128), 1) < LANE_WIDTH
    upper = lax.rem(m, 2) == 1

    def head_tile(j):
        start = pl.multiple_of(j * block + lax.div(m, 2) * 128, 128)
        return vec[:, pl.ds(start, 128)]

    for q in range(pairs):
        first, second = head_tile(2 * q), head_tile(2 * q + 1)
        first = jnp.where(upper, swap_halves(first), first)
        second = jnp.where(upper, second, swap_halves(second))
        head_vec[:, q * 128 : (q + 1) * 128] = jnp.where(low_row, first, second)

    def row_masks(b):
        t = lax.broadcasted_iota(jnp.int32, (rows, 1), 0)
        lane = lax.broadcasted_iota(jnp.int32, (1, rows), 1)
        label, past, ahead = (jnp.zeros((rows, 1), jnp.int32) for unused in range(3))
        label_row = jnp.zeros((1, rows), jnp.int32)
        end = jnp.int32(0)
        for j in range(spans.shape[1]):
            end = end + spans[b, j]
            label = label + jnp.where(t >= end, 1, 0)
            past = past + jnp.where(t - 1 >= end, 1, 0)
            ahead = ahead + jnp.where(t + 1 >= end, 1, 0)
            label_row = label_row + jnp.where(lane >= end, 1, 0)
        same = jnp.where(jnp.logical_and(label == past, t > 0), 1.0, 0.0)
        following = jnp.where(jnp.logical_and(label == ahead, t < rows - 1), 1.0, 0.0)
        valid = jnp.where(t < end, 1.0, 0.0)
        return label, label_row, same, following, valid

    masks = [row_masks(b) for b in range(buckets)]

    def mix(b, take, mean, rstd, gain_row, mix_row, outs):
        rs = bucket_rows(b)
        same = masks[b][2]
        total = jnp.zeros((rows, 1), F32)
        for j in range(4):
            total = total + jnp.sum(take(rs, j).astype(F32), axis=1, keepdims=True)
        average = total / width
        spread = jnp.zeros((rows, 1), F32)
        for j in range(4):
            centered = take(rs, j).astype(F32) - average
            spread = spread + jnp.sum(centered * centered, axis=1, keepdims=True)
        scale = lax.rsqrt(spread / width + EPSILON)
        mean[rs, :] = average
        rstd[rs, :] = scale
        for j in range(4):
            cols = slice(j * block, (j + 1) * block)
            normed = (take(rs, j).astype(F32) - average) * scale * order_vec[gain_row : gain_row + 1, cols]
            before = roll_rows(normed, 1) * same
            change = normed - before
            for i, out in enumerate(outs):
                weight = order_vec[mix_row + i : mix_row + i + 1, cols]
                out[rs, cols] = (before + change * weight).astype(BF)

    def take_x(rs, j):
        return x_ref[rs, pl.ds(pl.multiple_of(order[j] * block, block), block)]

    def take_mid(rs, j):
        return mid[rs, j * block : (j + 1) * block]

    for b in range(buckets):
        mix(b, take_x, mean1, rstd1, OPENING, OPENING + 1, [acts.at[w] for w in range(4)])

    g_first = []
    everything = pl.ds(0, block)
    for w in range(4):
        arrivals[w].wait_recv()
        g_first.append(relay_out(g.at[0, w], g.at[1, w], g.at[2, w], everything))
    g_second = [forward(g_first[w], g_first[w], g.at[1, w], g.at[2, w], g.at[3, w]) for w in range(4)]
    wo_first[0].wait_recv()
    wo_rows = out_rows(x_peer[0], 0, shard // 2)
    wo_second = [links.push(wob.at[wo_rows], wob.at[wo_rows], y_peer)]
    wo_first[1].wait_recv()
    wo_rows = out_rows(y_peer[0], shard // 2, shard // 2)
    wo_second.append(links.push(wob.at[wo_rows], wob.at[wo_rows], x_peer))
    fk_lower = relay_out(fk, fkb.at[0], fkb.at[1], lower_half)
    arrivals[4].wait_recv()
    g_first.append(relay_out(g.at[0, 4], g.at[1, 4], g.at[2, 4], everything))

    for w in range(4):
        for copy in g_second[w]:
            copy.wait_recv()
        for b in range(buckets):
            rs = bucket_rows(b)
            total = nn(acts[w, rs, 0:block], g[0, w])
            for j in range(1, 4):
                total = total + nn(acts[w, rs, j * block : (j + 1) * block], g[j, w])
            if w < 3:
                rkv[w, rs] = total.astype(BF)
            else:
                gate_raw[rs] = total
    fv_upper = relay_out(fv, fvb.at[0], fvb.at[1], upper_half)

    low = lax.broadcasted_iota(jnp.int32, (rows, 128), 1) < LANE_WIDTH
    t_square = lax.broadcasted_iota(jnp.int32, (rows, rows), 0)
    s_square = lax.broadcasted_iota(jnp.int32, (rows, rows), 1)
    places = lax.broadcasted_iota(jnp.int32, (rows, 1), 0).astype(F32) - float(rows // 2)

    def decay_scales(cols):
        log_decay = -jnp.exp(head_vec[FADING : FADING + 1, cols])
        return jnp.exp(log_decay * places), jnp.exp(log_decay * (-1.0 - places))

    def allowed_pairs(b):
        return jnp.logical_and(s_square < t_square, masks[b][0] == masks[b][1])

    def scores_of(rt, kt, now, mine, allowed):
        scores = nt(jnp.where(mine, rt, 0.0).astype(BF), kt)
        here = jnp.sum(jnp.where(mine, now, 0.0), axis=1, keepdims=True)
        return jnp.where(allowed, scores, jnp.where(s_square == t_square, here, 0.0)).astype(BF)

    def time_forward(b):
        rs = bucket_rows(b)
        allowed = allowed_pairs(b)
        for p in range(pairs):
            cols = slice(p * 128, (p + 1) * 128)
            out_scale, in_scale = decay_scales(cols)
            r, k = rkv[0, rs, cols].astype(F32), rkv[1, rs, cols].astype(F32)
            v = rkv[2, rs, cols]
            rt, kt = r * out_scale, (k * in_scale).astype(BF)
            now = r * head_vec[REWARD : REWARD + 1, cols] * k
            first = nn(scores_of(rt, kt, now, low, allowed), v)
            second = nn(scores_of(rt, kt, now, jnp.logical_not(low), allowed), v)
            wkv = jnp.where(low, first, second)
            centered = wkv - head_sums(wkv, low) / LANE_WIDTH
            scale = lax.rsqrt(head_sums(centered * centered, low) / LANE_WIDTH + GROUP_EPSILON)
            n = centered * scale
            n_ref[rs, cols] = n
            n_scale[rs, cols] = scale
            gate = gate_raw[rs, cols]
            gained = n * head_vec[LANE : LANE + 1, cols] * gate * jax.nn.sigmoid(gate)
            mixed[rs, cols] = gained.astype(BF)

    pair_copies = {}
    own_copies = []

    def scatter_start(k, b, source, lanes):
        rs = pl.ds(b * rows, rows)
        return [
            links.push(source.at[rs, lanes(2 * other + 1 - c)], half.at[k, b, i], mate)
            for i, other in enumerate(chips_away + [z])
        ]

    def scatter_middle(k, b, source, lanes, first):
        rs = pl.ds(b * rows, rows)
        copies = []
        for i, other in enumerate(chips_away):
            if (b, i) in pair_copies:
                links.sent(pair_copies[b, i])
            first[i].wait_recv()
            value = source[rs, lanes(2 * other + c)].astype(F32) + half[k, b, i].astype(F32)
            pair[b, i] = value.astype(BF)
            copy = links.push(pair.at[b, i], far.at[k, b, i], (d, 2 * other + c))
            pair_copies[b, i] = copy
            copies.append(copy)
        return copies

    def scatter_end(k, b, source, lanes, first, second):
        rs = pl.ds(b * rows, rows)
        first[chips - 1].wait_recv()
        total = source[rs, lanes(m)].astype(F32) + half[k, b, chips - 1].astype(F32)
        for i, copy in enumerate(second):
            copy.wait_recv()
            total = total + far[k, b, i].astype(F32)
        return total

    def stats_start(k, b):
        return links.push(small.at[k, b, 0], small.at[k, b, 1], mate)

    def stats_middle(k, b, first):
        first.wait_recv()
        small[k, b, 2] = small[k, b, 0] + small[k, b, 1]
        return [
            links.push(small.at[k, b, 2], small.at[k, b, 3 + i], (d, 2 * other + c))
            for i, other in enumerate(chips_away)
        ]

    eye8 = jnp.where(lax.broadcasted_iota(jnp.int32, (16, 128), 0) == 0, 1.0, 0.0)
    eye16 = jnp.where(lax.broadcasted_iota(jnp.int32, (16, 128), 0) == 8, 1.0, 0.0)

    def stats_end(k, b, second):
        total = small[k, b, 2]
        for i, copy in enumerate(second):
            copy.wait_recv()
            total = total + small[k, b, 3 + i]
        total = total / width
        turn = lambda e: lax.dot_general(
            total, e, (((0,), (0,)), ((), ())), precision=lax.Precision.HIGHEST, preferred_element_type=F32
        )[:, 0:1]
        return turn(eye8), turn(eye16)

    def gather_start(source, target, lanes, rs, keep=None):
        mine = target.at[rs, lanes(m)]
        copies = [links.push(source.at[rs], mine, (d, 2 * other + c)) for other in chips_away]
        copies.append(links.push(source.at[rs], mine, mate))
        if keep is None:
            target[rs, lanes(m)] = source[rs]
        else:
            own_copies.append(pltpu.make_async_copy(source.at[rs], mine, local.at[keep]))
            own_copies[-1].start()
        return copies

    def gather_middle(target, lanes, rs, first):
        copies = []
        for i in range(chips - 1):
            source = 2 * lax.rem(z - (i + 1) + chips, chips) + c
            first[i].wait_recv()
            copies.append(links.push(target.at[rs, lanes(source)], target.at[rs, lanes(source)], mate))
        return copies

    def gather_end(first, second):
        first[-1].wait_recv()
        for copy in second:
            copy.wait_recv()

    both = (0, 1)
    slices = [pl.ds(b * rows, rows) for b in both]
    all_rows = pl.ds(0, buckets * rows)

    for copy in wo_second:
        copy.wait_recv()
    first1 = []
    for b in both:
        time_forward(b)
        rs = bucket_rows(b)
        for j in range(4):
            cols = slice(j * block, (j + 1) * block)
            part[0, rs, cols] = nn(mixed[rs], wob[:, cols]).astype(BF)
        first1.append(scatter_start(0, b, part.at[0], own_lanes))
    g_second.append(forward(g_first[4], g_first[4], g.at[1, 4], g.at[2, 4], g.at[3, 4]))
    fk_second = forward(fk_upper, fk_lower, fkb.at[0], fkb.at[1], fkb.at[2])
    fv_lower = relay_out(fv, fvb.at[0], fvb.at[1], lower_half)
    second1 = [scatter_middle(0, b, part.at[0], own_lanes, first1[b]) for b in both]
    gathers = []
    for b in both:
        rs = bucket_rows(b)
        total = scatter_end(0, b, part.at[0], own_lanes, first1[b], second1[b])
        middle = x_ref[rs, own_lanes(m)].astype(F32) + total
        mid_own[rs] = middle
        mid_own_b[rs] = middle.astype(BF)
        gathers.append(gather_start(mid_own_b, mid, moved_lanes, slices[b]))
    onward = [gather_middle(mid, moved_lanes, slices[b], gathers[b]) for b in both]
    for b in both:
        gather_end(gathers[b], onward[b])
        mix(b, take_mid, mean2, rstd2, CLOSING, CLOSING + 1, [kin, cri])
    for copy in g_second[4]:
        copy.wait_recv()

    def top(b):
        return seen[bucket_rows(b)].astype(F32) * masks[b][4]

    for b in both:
        rs = bucket_rows(b)
        total = nn(cri[rs, 0:block], g[0, 4])
        for j in range(1, 4):
            total = total + nn(cri[rs, j * block : (j + 1) * block], g[j, 4])
        gate = jax.nn.sigmoid(total)
        channel_gate[rs] = gate
        cg_own[rs] = (top(b) * gate).astype(BF)
    gathers = gather_start(cg_own, cg, moved_lanes, all_rows)
    for copy in fk_second:
        copy.wait_recv()

    def fk_piece(j):
        return fk if j == 0 else fkb.at[j - 1]

    def fv_piece(j):
        return fv if j == 0 else fvb.at[j - 1]

    for b in both:
        rs = bucket_rows(b)
        total = nn(kin[rs, 0:block], fk[...])
        for j in range(1, 4):
            total = total + nn(kin[rs, j * block : (j + 1) * block], fkb[j - 1])
        positive = jnp.maximum(total, 0.0)
        hid[rs] = (positive * positive).astype(BF)
        pos[rs] = positive.astype(BF)
    fv_second = forward(fv_upper, fv_lower, fvb.at[0], fvb.at[1], fvb.at[2])
    onward = gather_middle(cg, moved_lanes, all_rows, gathers)
    gather_end(gathers, onward)

    piece = own

    def product_piece(lhs, rhs, i):
        return tn(lhs[:, i * piece : (i + 1) * piece], rhs[...])

    def ff_grad_start(k, lhs, rhs):
        for i, (way, slot) in ((2, (0, 0)), (6, (0, 1)), (5, (1, 0)), (7, (1, 1))):
            ff_send[k, way, slot] = product_piece(lhs, rhs, i).astype(BF)
        return (
            links.push(ff_send.at[k, 0], ff_got.at[k, 0], x_peer),
            links.push(ff_send.at[k, 1], ff_got.at[k, 1], y_peer),
        )

    def ff_grad_middle(k, lhs, rhs, first):
        for way, i in ((0, 4), (1, 3)):
            value = product_piece(lhs, rhs, i)
            first[way].wait_recv()
            links.sent(first[way])
            ff_send[k, way, 0] = (value + ff_got[k, way, 1].astype(F32)).astype(BF)

    def ff_grad_relay(k):
        return (
            links.push(ff_send.at[k, 0, 0], ff_got2.at[k, 0], y_peer),
            links.push(ff_send.at[k, 1, 0], ff_got2.at[k, 1], x_peer),
        )

    def ff_grad_end(k, lhs, rhs, second, out):
        for way in range(2):
            second[way].wait_recv()
            total = product_piece(lhs, rhs, way) + ff_got[k, way, 0].astype(F32) + ff_got2[k, way].astype(F32)
            ff_send[k, way, 1] = total.astype(BF)
            own_copies.append(
                pltpu.make_async_copy(
                    ff_send.at[k, way, 1], out.at[pl.ds(way * piece, piece)], local.at[1 + 2 * k + way]
                )
            )
            own_copies[-1].start()

    tm_first, tm_second, back_copies = {}, {}, []

    def tm_lhs(w):
        return acts.at[w] if w < 4 else cri

    def tm_rhs(w):
        return time_grads.at[w] if w < 4 else gig

    def tm_grad_start(w):
        for i, (way, slot) in ((2, (0, 0)), (6, (0, 1)), (5, (1, 0)), (7, (1, 1))):
            tm_send[w, way, slot] = product_piece(tm_lhs(w), tm_rhs(w), i).astype(BF)
        tm_first[w] = (
            links.push(tm_send.at[w, 0], tm_got.at[w, 0], x_peer),
            links.push(tm_send.at[w, 1], tm_got.at[w, 1], y_peer),
        )

    def tm_grad_middle(w):
        copies = []
        for way, (i, peer) in enumerate(((4, y_peer), (3, x_peer))):
            value = product_piece(tm_lhs(w), tm_rhs(w), i)
            tm_first[w][way].wait_recv()
            links.sent(tm_first[w][way])
            tm_send[w, way, 0] = (value + tm_got[w, way, 1].astype(F32)).astype(BF)
            copies.append(links.push(tm_send.at[w, way, 0], tm_got2.at[w, way], peer))
        tm_second[w] = copies

    def tm_grad_end(w):
        links.sent(arrivals[w])
        sums = blocks.at[w] if w < 4 else channel_sum
        for way in range(2):
            value = product_piece(tm_lhs(w), tm_rhs(w), way)
            tm_second[w][way].wait_recv()
            value = value + tm_got[w, way, 0].astype(F32) + tm_got2[w, way].astype(F32)
            sums[4 * way : 4 * way + 4] = value.astype(BF).reshape(4, shard, own)
        back_copies.append(
            links.group(
                [sums.at[other] for other in others],
                [back_out.at[w, m]] * (parts - 1),
                [(d, other) for other in others],
                back_out.at[w, pl.ds(0, parts - 1)],
            )
        )
        own_copies.append(pltpu.make_async_copy(sums.at[m], back_out.at[w, m], local.at[5 + w]))
        own_copies[-1].start()

    fv_grad1 = ff_grad_start(0, cg, hid)

    for copy in fv_second:
        copy.wait_recv()
    first3 = []
    for b in both:
        rs = bucket_rows(b)
        for j in range(4):
            cols = slice(j * block, (j + 1) * block)
            part[1, rs, cols] = nt(hid[rs], fv_piece(j)[...]).astype(BF)
        first3.append(scatter_start(1, b, part.at[1], moved_lanes))
    second3 = []
    for b in both:
        rs = bucket_rows(b)
        total = nn(cg[rs, 0:block], fv[...])
        for j in range(1, 4):
            total = total + nn(cg[rs, j * block : (j + 1) * block], fvb[j - 1])
        pre[rs] = (total * 2.0 * pos[rs].astype(F32)).astype(BF)
        second3.append(scatter_middle(1, b, part.at[1], moved_lanes, first3[b]))
    fk_grad1 = ff_grad_start(1, kin, pre)
    sens[...] = jnp.zeros_like(sens)
    head_small[...] = jnp.zeros_like(head_small)
    gate_first = []
    for b in both:
        rs = bucket_rows(b)
        gate = channel_gate[rs]
        total = scatter_end(1, b, part.at[1], moved_lanes, first3[b], second3[b])
        out_own[rs] = ((mid_own[rs] + gate * total) * masks[b][4]).astype(BF)
        gig[rs] = (top(b) * total * gate * (1.0 - gate)).astype(BF)
    tm_grad_start(4)

    ones = jnp.ones((8, own), BF)

    def back_mix(k, b, target, take, mean, rstd, gain_row, mix_row, sens_row, grads):
        rs = bucket_rows(b)
        same, following = masks[b][2], masks[b][3]
        average, scale = mean[rs, :], rstd[rs, :]
        one, two = jnp.zeros((8, rows), F32), jnp.zeros((8, rows), F32)
        for e in range(parts):
            cols = slice(e * own, (e + 1) * own)
            hat = (take(rs, e).astype(F32) - average) * scale
            gain = order_vec[gain_row : gain_row + 1, cols]
            normed = hat * gain
            change = normed - roll_rows(normed, 1) * same
            now = jnp.zeros((rows, own), F32)
            whole = jnp.zeros((rows, own), F32)
            for i, (grad, weight_of) in enumerate(grads):
                value = nt(grad(rs), weight_of(e))
                at = slice(sens_row + i, sens_row + i + 1)
                sens[at, cols] += jnp.sum(value * change, axis=0, keepdims=True)
                weight = order_vec[mix_row + i : mix_row + i + 1, cols]
                now = now + value * weight
                whole = whole + value
            back = now + following * roll_rows(whole - now, -1)
            target[rs, cols] = back.astype(BF)
            scaled = back * gain
            one = one + nt(ones, scaled.astype(BF))
            two = two + nt(ones, (scaled * hat).astype(BF))
        small[k, b, 0, 0:8] = one
        small[k, b, 0, 8:16] = two

    def piece_rows(e):
        return slice((e % 2) * own, (e % 2 + 1) * own)

    def take_mid_own(rs, e):
        return mid[rs, e * own : (e + 1) * own]

    def take_x_own(rs, e):
        start = pl.multiple_of(order[e // 2] * block + (e % 2) * own, own)
        return x_ref[rs, pl.ds(start, own)]

    def fk_rows(e):
        return fk_piece(e // 2)[piece_rows(e)]

    def g_rows(w):
        return lambda e: g[e // 2, w, piece_rows(e)]

    for copies in first1 + second1:
        for copy in copies:
            links.sent(copy)
    first4, stats4 = [], []
    for b in both:
        back_mix(
            0, b, part.at[0], take_mid_own, mean2, rstd2, CLOSING, CLOSING + 1, 4,
            [(lambda rs: pre[rs], fk_rows), (lambda rs: gig[rs], g_rows(4))],
        )
        first4.append(scatter_start(2, b, part.at[0], moved_lanes))
        stats4.append(stats_start(0, b))
    second4, stats4b = [], []
    for b in both:
        second4.append(scatter_middle(2, b, part.at[0], moved_lanes, first4[b]))
        stats4b.append(stats_middle(0, b, stats4[b]))
    ff_grad_middle(0, cg, hid, fv_grad1)
    fv_grad2 = ff_grad_relay(0)

    def norm_back(b, back, hat, gain_row, rstd, means):
        gain = vec[gain_row : gain_row + 1, own_lanes(m)]
        return (back * gain - means[0] - hat * means[1]) * rstd[bucket_rows(b), :]

    closing = jnp.zeros((1, own), F32)
    gathers = []
    for b in both:
        rs = bucket_rows(b)
        back = scatter_end(2, b, part.at[0], moved_lanes, first4[b], second4[b])
        means = stats_end(0, b, stats4b[b])
        hat = (mid_own_b[rs].astype(F32) - mean2[rs, :]) * rstd2[rs, :]
        closing = closing + jnp.sum(back * hat, axis=0, keepdims=True)
        value = top(b) + norm_back(b, back, hat, CLOSING, rstd2, means)
        middle_grad[rs] = value
        branch_own[rs] = value.astype(BF)
        gathers.append(gather_start(branch_own, branch, own_lanes, slices[b]))
    onward = [gather_middle(branch, own_lanes, slices[b], gathers[b]) for b in both]
    out_first = gather_start(out_own, out_full, own_lanes, all_rows, keep=11)

    def time_backward(b):
        rs = bucket_rows(b)
        allowed = allowed_pairs(b)
        for p in range(pairs):
            cols = slice(p * 128, (p + 1) * 128)
            out_scale, in_scale = decay_scales(cols)
            u, gn = head_vec[REWARD : REWARD + 1, cols], head_vec[LANE : LANE + 1, cols]
            g_in, gate, n = mixed_grad[rs, cols], gate_raw[rs, cols], n_ref[rs, cols]
            sg = jax.nn.sigmoid(gate)
            silu = gate * sg
            time_grads[3, rs, cols] = (g_in * n * gn * sg * (1.0 + gate * (1.0 - sg))).astype(BF)
            q = g_in * gn * silu
            dout = q - head_sums(q, low) / LANE_WIDTH - n * (head_sums(q * n, low) / LANE_WIDTH)
            dout = dout * n_scale[rs, cols]
            r, k = rkv[0, rs, cols].astype(F32), rkv[1, rs, cols].astype(F32)
            v = rkv[2, rs, cols]
            rt, kt = r * out_scale, (k * in_scale).astype(BF)
            rtb = rt.astype(BF)
            now = r * u * k
            diag = head_sums(dout * v.astype(F32), low)
            found = []
            for mine in (low, jnp.logical_not(low)):
                dmine = jnp.where(mine, dout, 0.0).astype(BF)
                scores = scores_of(rt, kt, now, mine, allowed)
                a = jnp.where(allowed, nt(dmine, v), 0.0).astype(BF)
                found.append((tn(scores, dmine), nn(a, kt), tn(a, rtb)))
            dv, drt, dkt = (jnp.where(low, one, two) for one, two in zip(*found))
            time_grads[0, rs, cols] = (drt * out_scale + u * k * diag).astype(BF)
            time_grads[1, rs, cols] = (dkt * in_scale + u * r * diag).astype(BF)
            time_grads[2, rs, cols] = dv.astype(BF)
            lags = places * rtb.astype(F32) * drt - (places + 1.0) * kt.astype(F32) * dkt
            log_decay = -jnp.exp(head_vec[FADING : FADING + 1, cols])
            head_small[0:1, cols] += jnp.sum(lags, axis=0, keepdims=True) * log_decay
            head_small[1:2, cols] += jnp.sum(r * k * diag, axis=0, keepdims=True)
            head_small[2:3, cols] += jnp.sum(g_in * n * silu, axis=0, keepdims=True)

    for copies in first3 + second3:
        for copy in copies:
            links.sent(copy)
    wo_second = []
    left, right = pl.ds(0, width // 2), pl.ds(width // 2, width // 2)
    first6, stats6 = [], []
    for b in both:
        gather_end(gathers[b], onward[b])
        rs = bucket_rows(b)
        if b == 1:
            for j in range(4):
                wo_part[j] = tn(mixed[:, j * LANE_WIDTH : (j + 1) * LANE_WIDTH], branch[...]).astype(BF)
            wo_first = [
                links.push(wo_part.at[peer[0], :, lanes], wo_got.at[way, i], way_peer)
                for way, lanes, way_peer, near in ((0, left, x_peer, x_peer), (1, right, y_peer, y_peer))
                for i, peer in enumerate((near, diagonal))
            ]
        mixed_grad[rs] = nt(branch[rs], wob[...])
        time_backward(b)
        back_mix(
            1, b, part.at[1], take_x_own, mean1, rstd1, OPENING, OPENING + 1, 0,
            [((lambda rs, w=w: time_grads[w, rs]), g_rows(w)) for w in range(4)],
        )
        first6.append(scatter_start(3, b, part.at[1], moved_lanes))
        stats6.append(stats_start(1, b))

    for w in (0, 1):
        tm_grad_start(w)
    vec_copies = links.group(
        [sens.at[:, moved_lanes(other)] for other in others],
        [u_got.at[i] for i in range(parts - 1)],
        [(d, other) for other in others],
        u_got,
    )
    second6, stats6b = [], []
    for b in both:
        second6.append(scatter_middle(3, b, part.at[1], moved_lanes, first6[b]))
        stats6b.append(stats_middle(1, b, stats6[b]))
    out_second = gather_middle(out_full, own_lanes, all_rows, out_first)
    tm_grad_middle(4)
    ff_grad_middle(1, kin, pre, fk_grad1)
    for way, (lanes, near, peer) in enumerate(((left, y_peer, y_peer), (right, x_peer, x_peer))):
        for copy in wo_first[2 * way : 2 * way + 2]:
            copy.wait_recv()
        value = wo_part[near[0], :, lanes].astype(F32) + wo_got[way, 1].astype(F32)
        wo_send[way] = value.astype(BF)
        wo_second.append(links.push(wo_send.at[way], wo_got2.at[way], peer))
    opening = jnp.zeros((1, own), F32)
    for b in both:
        rs = bucket_rows(b)
        back = scatter_end(3, b, part.at[1], moved_lanes, first6[b], second6[b])
        means = stats_end(1, b, stats6b[b])
        hat = (x_ref[rs, own_lanes(m)].astype(F32) - mean1[rs, :]) * rstd1[rs, :]
        opening = opening + jnp.sum(back * hat, axis=0, keepdims=True)
        value = middle_grad[rs] + norm_back(b, back, hat, OPENING, rstd1, means)
        gin_own[rs] = value.astype(BF)
    gin_first = gather_start(gin_own, gin_full, own_lanes, all_rows, keep=10)
    tm_grad_middle(0)
    tm_grad_start(2)
    tm_grad_middle(1)
    tm_grad_start(3)
    tm_grad_end(4)
    gin_second = gather_middle(gin_full, own_lanes, all_rows, gin_first)

    vec_copies.wait_recv()
    total = sens[:, moved_lanes(m)]
    for i in range(parts - 1):
        total = total + u_got[i]
    u2_own[0:8] = total
    u2_own[6:7] = opening
    u2_own[7:8] = closing
    u2_own[8:16] = head_small[...]
    dp_copies = links.group(
        [u2_own] * 3, [u2_got.at[i] for i in range(3)], [x_peer, y_peer, diagonal], u2_got
    )
    tm_grad_end(0)
    tm_grad_middle(2)
    tm_grad_middle(3)
    tm_grad_end(1)
    fk_grad2 = ff_grad_relay(1)
    tm_grad_end(2)
    dp_copies.wait_recv()
    u3_own[...] = (u2_own[...] + u2_got[0]) + (u2_got[1] + u2_got[2])
    all_copies = links.group(
        [u3_own] * (parts - 1),
        [u3_got.at[m]] * (parts - 1),
        [(d, other) for other in others],
        u3_got.at[pl.ds(0, parts - 1)],
    )
    u3_got[m] = u3_own[...]

    tm_grad_end(3)
    ff_grad_end(0, cg, hid, fv_grad2, ffv_out)
    for way, lanes in enumerate((left, right)):
        wo_second[way].wait_recv()
        total = wo_part[d, :, lanes].astype(F32) + wo_got[way, 0].astype(F32) + wo_got2[way].astype(F32)
        wo_out[:, lanes] = total.astype(BF)
    ff_grad_end(1, kin, pre, fk_grad2, ffk_out)
    all_copies.wait_recv()
    upper_d = lax.rem(d, 2) == 1
    low_vec = lax.broadcasted_iota(jnp.int32, (8, 128), 1) < LANE_WIDTH
    for e in range(2):
        vec_out[0:8, e * own : (e + 1) * own] = u3_got[2 * d + e, 0:8]
    for u in range(4):
        lanes = pl.ds(pl.multiple_of(lax.div(d, 2) * 128, 128), 128)
        first, second = u3_got[2 * u, 8:16, lanes], u3_got[2 * u + 1, 8:16, lanes]
        first = jnp.where(upper_d, swap_halves(first), first)
        second = jnp.where(upper_d, second, swap_halves(second))
        vec_out[8:16, u * 128 : (u + 1) * 128] = jnp.where(low_vec, first, second)
    gather_end(gin_first, gin_second)
    gather_end(out_first, out_second)
    for copy in back_copies:
        copy.wait_recv()
    for copy in own_copies:
        copy.wait()
    links.finish()
    assert links.used == COPIES, links.used


def finish_kernel(
    out, gin, ffk, ffv, back, wo, vec,
    out_o, gin_o, ffk_o, ffv_o, r_o, k_o, v_o, g_o, c_o, wo_o,
    y0, y1, y2, y3, y4, y5, y6, y7, y8, y9, y10,
    out_v, gin_v, ffk_v, ffv_v, back_v, wo_v, ffk_f, ffv_f, square, read, write,
):
    buckets, rows = out_o.shape[:2]
    reads = [
        pltpu.make_async_copy(a, b, read.at[i])
        for i, (a, b) in enumerate(
            ((ffv, ffv_v), (ffk, ffk_v), (wo, wo_v), (back, back_v), (out, out_v), (gin, gin_v))
        )
    ]
    for copy in reads:
        copy.start()
    writes = []

    def store(source, target):
        copy = pltpu.make_async_copy(source, target, write.at[len(writes)])
        copy.start()
        writes.append(copy)

    for i, ref in enumerate((y0, y1, y2, y3, y4, y5, y6, y7, y8, y9, y10)):
        ref[...] = vec[i : i + 1]
    for copy, source, middle, target in zip(reads, (ffv_v, ffk_v, wo_v), (ffv_f, ffk_f, square.at[5]), (ffv_o, ffk_o, wo_o)):
        copy.wait()
        middle[...] = source[...].astype(F32)
        store(middle, target)
    reads[3].wait()
    parts, shard, own = back_v.shape[1:]
    low = lax.broadcasted_iota(jnp.int32, (shard, 128), 1) < LANE_WIDTH
    for to in range(parts):
        square[4, :, to * own : (to + 1) * own] = back_v[4, to].astype(F32)
    store(square.at[4], c_o)
    for w, target in enumerate((r_o, k_o, v_o, g_o)):
        for j in range(4):
            for u in range(4):
                lanes = slice((j // 2) * 128, (j // 2 + 1) * 128)
                first = back_v[w, 2 * u, :, lanes].astype(F32)
                second = back_v[w, 2 * u + 1, :, lanes].astype(F32)
                if j % 2 == 0:
                    tile = jnp.where(low, first, swap_halves(second))
                else:
                    tile = jnp.where(low, swap_halves(first), second)
                start = j * 4 * 128 + u * 128
                square[w, :, start : start + 128] = tile
        store(square.at[w], target)
    for copy, source, target in ((reads[4], out_v, out_o), (reads[5], gin_v, gin_o)):
        copy.wait()
        for b in range(buckets):
            store(source.at[pl.ds(b * rows, rows)], target.at[b])
    for copy in writes:
        copy.wait()


def fast_body(*args):
    (
        block_arguments, bundled_spans, opening_gain, mix_r, mix_k, mix_v, mix_g, w_recept, w_key, w_value, w_gate,
        fading, reward, lane_gain, w_out, closing_gain, mix_fk, mix_fr, fk, fv, w_channel, upstream,
    ) = args
    buckets, bucket_rows, width = block_arguments.shape
    rows = buckets * bucket_rows
    parts, chips = 8, 4
    own, block = width // parts, width // 4
    hidden = fk.shape[1]
    shard = w_out.shape[0]
    vectors = [
        opening_gain, mix_r, mix_k, mix_v, mix_g, closing_gain, mix_fk, mix_fr, fading, reward, lane_gain,
    ]
    vectors = [vector.reshape(1, width) for vector in vectors]
    v, sm = pltpu.VMEM, pltpu.SMEM
    vm = pl.BlockSpec(memory_space=pltpu.VMEM)
    half_block = block // 2
    scratch = [
        v((16, width), F32), v((4, parts, shard, own), BF), v((4, 5, block, own), BF), v((3, block, hidden), BF), v((3, block, hidden), BF),
        v((4 * shard, width), BF), v((4, rows, width), BF), v((rows, 1), F32), v((rows, 1), F32), v((rows, 1), F32),
        v((rows, 1), F32), v((16, width), F32), v((16, own), F32), v((rows, own), BF),
        v((3, rows, own), BF), v((rows, own), F32), v((rows, own), F32), v((rows, own), F32), v((rows, own), BF),
        v((2, rows, width), BF), v((4, buckets, chips, bucket_rows, own), BF),
        v((buckets, chips - 1, bucket_rows, own), BF), v((4, buckets, chips - 1, bucket_rows, own), BF),
        v((2, buckets, chips + 2, 16, bucket_rows), F32),
        v((rows, own), F32), v((rows, own), BF), v((rows, width), BF), v((rows, width), BF), v((rows, width), BF),
        v((rows, hidden), BF), v((rows, hidden), BF), v((rows, hidden), BF), v((rows, own), F32), v((rows, own), BF),
        v((rows, width), BF),
        v((rows, own), BF), v((rows, own), BF), v((rows, own), F32), v((rows, own), BF),
        v((rows, width), BF), v((rows, own), F32), v((4, rows, own), BF), v((8, width), F32), v((8, own), F32),
        v((2, 2, 2, own, hidden), BF), v((2, 2, 2, own, hidden), BF), v((2, 2, own, hidden), BF),
        v((5, 2, 2, own, own), BF), v((5, 2, 2, own, own), BF), v((5, 2, own, own), BF),
        v((parts, shard, own), BF),
        v((4, shard, width), BF), v((2, 2, shard, width // 2), BF), v((2, shard, width // 2), BF),
        v((2, shard, width // 2), BF), v((rows, own), BF),
        v((parts - 1, 8, own), F32), v((16, own), F32), v((3, 16, own), F32), v((16, own), F32),
        v((parts, 16, own), F32),
        pltpu.SemaphoreType.DMA((COPIES,)), pltpu.SemaphoreType.DMA((COPIES,)), pltpu.SemaphoreType.DMA((12,)),
    ]
    out = pl.pallas_call(
        block_kernel,
        out_shape=[
            struct((rows, width), BF), struct((rows, width), BF), struct((block, hidden), BF),
            struct((block, hidden), BF), struct((5, parts, shard, own), BF), struct((shard, width), BF),
            struct((16, block), F32),
        ],
        in_specs=[pl.BlockSpec(memory_space=sm), vm, pl.BlockSpec(memory_space=pl.ANY)] + [vm] * 19,
        out_specs=[pl.BlockSpec(memory_space=pl.ANY)] * 5 + [vm] * 2,
        scratch_shapes=scratch,
        compiler_params=pltpu.CompilerParams(
            collective_id=0, has_side_effects=True, vmem_limit_bytes=VMEM_LIMIT
        ),
        name="whole_block",
    )(
        bundled_spans.reshape(buckets, -1), block_arguments.reshape(rows, width), upstream.reshape(rows, width), *vectors,
        w_recept, w_key, w_value, w_gate, w_out, w_channel, fk, fv,
    )
    square = struct((shard, width), F32)
    hbm = pl.BlockSpec(memory_space=pl.ANY)
    done = pl.pallas_call(
        finish_kernel,
        out_shape=[
            struct(block_arguments.shape, BF), struct(block_arguments.shape, BF), struct(fk.shape, F32),
            struct(fv.shape, F32), square, square, square, square, square, square,
        ]
        + [struct((1, block), F32)] * 11,
        in_specs=[hbm] * 6 + [vm],
        out_specs=[hbm] * 10 + [vm] * 11,
        scratch_shapes=[
            v((rows, width), BF), v((rows, width), BF), v(fk.shape, BF), v(fv.shape, BF), v((5, parts, shard, own), BF), v((shard, width), BF),
            v(fk.shape, F32), v(fv.shape, F32), v((6, shard, width), F32),
            pltpu.SemaphoreType.DMA((6,)), pltpu.SemaphoreType.DMA((2 * buckets + 8,)),
        ],
        compiler_params=pltpu.CompilerParams(vmem_limit_bytes=VMEM_LIMIT),
        name="finish",
    )(*out)
    outputs, grad_inputs, d_fk, d_fv, d_r, d_k, d_v, d_g, d_c, d_o = done[:10]
    small = [vector.reshape(block) for vector in done[10:]]
    return (
        outputs, grad_inputs, small[6], small[0], small[1], small[2], small[3], d_r, d_k, d_v, d_g,
        small[8], small[9], small[10], d_o, small[7], small[4], small[5], d_fk, d_fv, d_c,
    )


def body(*args):
    data_parts, parts = lax.axis_size("dp"), lax.axis_size("mp")
    width, shard, hidden = args[0].shape[2], args[7].shape[0], args[18].shape[1]
    fitted = (
        data_parts == 4
        and parts == 8
        and shard == LANE_WIDTH
        and width == 4 * parts * shard
        and hidden % 128 == 0
        and args[0].shape[:2] == (2, 128)
    )
    return fast_body(*args) if fitted else general_body(*args)


def solution(mesh):
    return jax.shard_map(
        body,
        mesh=mesh,
        in_specs=(
            P(None, "dp", None),
            P(None, "dp", None),
            P(),
            P(),
            P(),
            P(),
            P(),
            P(("dp", "mp"), None),
            P(("dp", "mp"), None),
            P(("dp", "mp"), None),
            P(("dp", "mp"), None),
            P(),
            P(),
            P(),
            P(("dp", "mp"), None),
            P(),
            P(),
            P(),
            P("dp", "mp"),
            P("dp", "mp"),
            P(("dp", "mp"), None),
            P(None, "dp", None),
        ),
        out_specs=(
            P(None, "dp", None),
            P(None, "dp", None),
            P("dp"),
            P("dp"),
            P("dp"),
            P("dp"),
            P("dp"),
            P(("dp", "mp"), None),
            P(("dp", "mp"), None),
            P(("dp", "mp"), None),
            P(("dp", "mp"), None),
            P("dp"),
            P("dp"),
            P("dp"),
            P(("dp", "mp"), None),
            P("dp"),
            P("dp"),
            P("dp"),
            P("dp", "mp"),
            P("dp", "mp"),
            P(("dp", "mp"), None),
        ),
        check_vma=False,
    )
```
